128 devices in a mesh: pair: 2 (over x_hi), gx: 8 (over y, x_lo), gy: 8 (over z, core).
Axes of the slice: x: 4 (x_hi: 2, x_lo: 2; x = x_hi * 2 + x_lo), y: 4, z: 4, core: 2. Of those that a mesh axis runs over, the one named last changes fastest.
Arguments:
- sound_speed_sq: float32 [64, 64, 1024], P('gx', 'gy'), may hold values from 0.5 to 2
- wind_profile: float32 [3, 1024], replicated, may hold values from -0.6 to 0.6
- forward_field: bfloat16 [4, 4, 64, 64, 1024], P(None, None, 'gx', 'gy'), may hold values from -6 to 6
- adjoint_state: float32 [2, 4, 64, 64, 1024], P('pair', None, 'gx', 'gy'), may hold values from -0.3125 to 0.3125
- pair_counts: int32 [2], P('pair'), may hold values from 64 to 256, as said below
- source_cells: int32 [512, 3], P('pair'), may hold values from 0 to 1023, as said below
- receiver_cells: int32 [512, 3], P('pair'), may hold values from 0 to 1023, as said below
- residuals: float32 [512, 4], P('pair'), may hold values from -16 to 16
Outputs:
- kernels: float32 [4, 64, 64, 1024], P(None, 'gx', 'gy', 'pair')
- final_state: float32 [2, 4, 64, 64, 1024], P('pair', None, 'gx', 'gy')
The draws below stay inside these ranges and needn't reach their ends.
Inputs may be any that keep to these rules, and one draw needn't show every extreme that they name: `pair_counts`: one group in every draw has exactly 256 live pairs. `source_cells`: columns are the cell along the first, second and third dimension, each within the grid. `receiver_cells`: columns are the cell along the first, second and third dimension, each within the grid; several pairs may share a cell.
All inputs are finite; a program needn't handle non-finite values.
Results may differ from the reference program's by a relative error of at most 0.00115.
Values may be sent and summed in bfloat16 or wider, within the bound.
A program may use at most 128 MiB of HBM per device.

```python
import math
import jax
import jax.numpy as jnp

NZ = 1024
PMAX = 256
STEPS = 4
GROUPS = 2
PAIRS = 512
NX = 64
NY = 64


def draw_pair_counts(key, part):
    counts = jax.random.randint(key, (GROUPS,), PMAX // 4, PMAX + 1)
    chosen = jax.random.randint(jax.random.fold_in(key, 7), (), 0, GROUPS)
    return jnp.where(jnp.arange(GROUPS) == chosen, PMAX, counts).astype(jnp.int32)


def station_cells(key):
    first = jax.random.randint(jax.random.fold_in(key, 1), (PAIRS,), 0, NX)
    second = jax.random.randint(jax.random.fold_in(key, 2), (PAIRS,), 0, NY)
    third = jax.random.randint(jax.random.fold_in(key, 3), (PAIRS,), 0, NZ)
    slot = jnp.arange(PAIRS, dtype=jnp.int32)
    first = jnp.where(slot == 0, NX - 1, jnp.where(slot == 1, 0, first))
    second = jnp.where(slot == 0, NY - 1, jnp.where(slot == 1, 0, second))
    third = jnp.where(slot == 0, NZ - 1, jnp.where(slot == 1, 0, third))
    return jnp.stack([first, second, third], axis=1).astype(jnp.int32)


def draw_source_cells(key, part):
    return station_cells(jax.random.fold_in(key, 11))


def draw_receiver_cells(key, part):
    return station_cells(jax.random.fold_in(key, 13))


def level_of(stream_key, extent, cuts, least, largest):
    gain = 1.0
    for dim, parts in cuts:
        heights = jax.random.uniform(jax.random.fold_in(jax.random.fold_in(stream_key, 6), dim), (parts,), jnp.float32, least / len(cuts), largest / len(cuts))
        gain = gain * jnp.repeat(jnp.exp(heights), extent[dim] // parts).reshape((-1,) + (1,) * (len(extent) - 1 - dim))
    return gain


def noise(rng, shape, spread, reach, cuts=(), held_as=jnp.bfloat16):
    entries = spread * jax.random.normal(rng, shape, jnp.float32)
    if cuts:
        entries = entries * level_of(rng, shape, cuts, -0.22, 0.18)
    return jnp.clip(entries, -reach, reach).astype(held_as)


def setup_inputs(seed: int = 0) -> dict:
    splits = jax.random.split(jax.random.key(seed), 9)
    sound_speed_sq = jnp.clip(jnp.exp(math.log(2.0) - 1.3862944 * jax.random.uniform(splits[0], (NX, NY, NZ), jnp.float32) ** level_of(splits[0], (NX, NY, NZ), ((0, 8), (1, 8)), -0.2, 0.2)), 0.5, 2.0)
    wind_profile = jnp.clip(jax.random.uniform(splits[1], (3, NZ), jnp.float32, -0.6, 0.6), -0.6, 0.6)
    forward_field = noise(splits[2], (STEPS, 4, NX, NY, NZ), 1.0, 6.0, ((2, 8), (3, 8)))
    adjoint_state = noise(splits[3], (GROUPS, 4, NX, NY, NZ), 0.05, 0.3125, ((0, 2), (2, 8), (3, 8)), jnp.float32)
    pair_counts = draw_pair_counts(jax.random.fold_in(splits[8], 71), 0)
    source_cells = draw_source_cells(jax.random.fold_in(splits[8], 71), 0)
    receiver_cells = draw_receiver_cells(jax.random.fold_in(splits[8], 71), 0)
    residuals = noise(splits[7], (PAIRS, STEPS), 3.0, 16.0, ((0, 2),), jnp.float32)
    return {"sound_speed_sq": sound_speed_sq, "wind_profile": wind_profile, "forward_field": forward_field, "adjoint_state": adjoint_state, "pair_counts": pair_counts, "source_cells": source_cells, "receiver_cells": receiver_cells, "residuals": residuals}


step_length = 0.25


def central(field):
    dims = field.ndim
    wide = [(0, 0)] * (dims - 3) + [(1, 1), (1, 1), (0, 0)]
    padded = jnp.pad(field, wide)
    east_diff = (padded[..., 2:, 1:-1, :] - padded[..., :-2, 1:-1, :]) * 0.5
    north_diff = (padded[..., 1:-1, 2:, :] - padded[..., 1:-1, :-2, :]) * 0.5
    center = padded[..., 1:-1, 1:-1, :]
    vertical = jnp.pad(center, [(0, 0)] * (dims - 1) + [(1, 1)])
    up_diff = (vertical[..., 2:] - vertical[..., :-2]) * 0.5
    return east_diff, north_diff, up_diff


def reference(sound_speed_sq, wind_profile, forward_field, adjoint_state, pair_counts, source_cells, receiver_cells, residuals):
    east_wind = wind_profile[0]
    north_wind = wind_profile[1]
    vertical_wind = wind_profile[2]
    kernel_total = jnp.zeros((4, NX, NY, NZ), jnp.float32)
    states = []
    for group in range(GROUPS):
        lower = group * PMAX
        src = source_cells[lower:lower + PMAX]
        rcv = receiver_cells[lower:lower + PMAX]
        misfit = residuals[lower:lower + PMAX]
        live = (jnp.arange(PMAX, dtype=jnp.int32) < pair_counts[group]).astype(jnp.float32)
        src_flat = (src[:, 0] * NY + src[:, 1]) * NZ + src[:, 2]
        rcv_flat = (rcv[:, 0] * NY + rcv[:, 1]) * NZ + rcv[:, 2]
        state = adjoint_state[group]
        for step in range(STEPS):
            snap = STEPS - 1 - step
            forward = forward_field[snap].astype(jnp.float32)
            sample = forward[0].reshape(-1)[src_flat]
            amplitude = misfit[:, snap] * sample * live
            injected = jnp.zeros((NX * NY * NZ,), jnp.float32).at[rcv_flat].add(amplitude).reshape(NX, NY, NZ)
            east_diff, north_diff, up_diff = central(state)
            pressure = state[0]
            velocity = state[1:]
            divergence = east_diff[1] + north_diff[2] + up_diff[3]
            p_new = pressure + step_length * (sound_speed_sq * divergence + east_wind * east_diff[0] + north_wind * north_diff[0] + vertical_wind * up_diff[0]) + injected
            p_east, p_north, p_up = central(p_new)
            gradient = jnp.stack([p_east, p_north, p_up])
            a_new = velocity + step_length * (gradient + east_wind * east_diff[1:] + north_wind * north_diff[1:] + vertical_wind * up_diff[1:])
            f_east, f_north, f_up = central(forward)
            pieces = [p_new * (f_east[1] + f_north[2] + f_up[3])]
            for along in (f_east, f_north, f_up):
                pieces.append(p_new * along[0] + a_new[0] * along[1] + a_new[1] * along[2] + a_new[2] * along[3])
            kernel_total = kernel_total + jnp.stack(pieces)
            state = jnp.concatenate([p_new[None], a_new], axis=0)
        states.append(state)
    return kernel_total, jnp.stack(states)
```

```python
import jax
import jax.numpy as jnp
from jax import lax
from jax.sharding import PartitionSpec as P

step_length = 0.25


def neighbours(shard, axis, dim):
    size, length = (lax.axis_size(axis), shard.shape[dim])
    up = [(i, i + 1) for i in range(size - 1)]
    down = [(i + 1, i) for i in range(size - 1)]
    last = lax.slice_in_dim(shard, length - 1, length, axis=dim)
    first = lax.slice_in_dim(shard, 0, 1, axis=dim)
    before = lax.ppermute(last, axis, up)
    after = lax.ppermute(first, axis, down)
    return (before, after)


def halos(shard, dim_x, dim_y):
    return (neighbours(shard, "gx", dim_x), neighbours(shard, "gy", dim_y))


def central(field, rims):
    (west, east), (south, north) = rims
    dims = field.ndim
    x_hi = jnp.concatenate([lax.slice_in_dim(field, 1, field.shape[-3], axis=dims - 3), east], axis=dims - 3)
    x_lo = jnp.concatenate([west, lax.slice_in_dim(field, 0, field.shape[-3] - 1, axis=dims - 3)], axis=dims - 3)
    y_hi = jnp.concatenate([lax.slice_in_dim(field, 1, field.shape[-2], axis=dims - 2), north], axis=dims - 2)
    y_lo = jnp.concatenate([south, lax.slice_in_dim(field, 0, field.shape[-2] - 1, axis=dims - 2)], axis=dims - 2)
    east_diff = (x_hi - x_lo) * 0.5
    north_diff = (y_hi - y_lo) * 0.5
    vertical = jnp.pad(field, [(0, 0)] * (dims - 1) + [(1, 1)])
    up_diff = (vertical[..., 2:] - vertical[..., :-2]) * 0.5
    return (east_diff, north_diff, up_diff)


def local_cells(cells, width_x, width_y):
    local_x = cells[:, 0] - lax.axis_index("gx") * width_x
    local_y = cells[:, 1] - lax.axis_index("gy") * width_y
    inside = (local_x >= 0) & (local_x < width_x) & (local_y >= 0) & (local_y < width_y)
    return (
        jnp.clip(local_x, 0, width_x - 1),
        jnp.clip(local_y, 0, width_y - 1),
        cells[:, 2],
        inside.astype(jnp.float32),
    )


def shards(
    sound_speed_sq,
    wind_profile,
    forward_field,
    adjoint_state,
    pair_counts,
    source_cells,
    receiver_cells,
    residuals,
):
    steps_total = forward_field.shape[0]
    width_x, width_y, depth = sound_speed_sq.shape
    slots = residuals.shape[0]
    east_wind = wind_profile[0]
    north_wind = wind_profile[1]
    vertical_wind = wind_profile[2]
    live = (jnp.arange(slots, dtype=jnp.int32) < pair_counts[0]).astype(jnp.float32)
    sx, sy, sz, src_inside = local_cells(source_cells, width_x, width_y)
    rx, ry, rz, rcv_inside = local_cells(receiver_cells, width_x, width_y)
    local_samples = jnp.stack(
        [forward_field[t, 0][sx, sy, sz] for t in range(steps_total)]
    ).astype(jnp.float32) * src_inside[None, :]
    me = lax.axis_index("pair")
    slot = jnp.zeros((lax.axis_size("pair"),) + local_samples.shape, jnp.float32)
    samples = lax.psum(slot.at[me].set(local_samples), ("pair", "gx", "gy"))[me]
    forward_rims = halos(forward_field, 2, 3)
    rcv_flat = (rx * width_y + ry) * depth + rz
    state = adjoint_state[0]
    kernel_local = jnp.zeros((4, width_x, width_y, depth), jnp.float32)
    for step in range(steps_total):
        snap = steps_total - 1 - step
        amplitude = residuals[:, snap] * samples[snap] * live * rcv_inside
        injected = (
            jnp.zeros((width_x * width_y * depth,), jnp.float32)
            .at[rcv_flat]
            .add(amplitude)
            .reshape(width_x, width_y, depth)
        )
        east_diff, north_diff, up_diff = central(state, halos(state, 1, 2))
        pressure = state[0]
        velocity = state[1:]
        divergence = east_diff[1] + north_diff[2] + up_diff[3]
        p_new = (
            pressure
            + step_length
            * (
                sound_speed_sq * divergence
                + east_wind * east_diff[0]
                + north_wind * north_diff[0]
                + vertical_wind * up_diff[0]
            )
            + injected
        )
        p_east, p_north, p_up = central(p_new, halos(p_new, 0, 1))
        gradient = jnp.stack([p_east, p_north, p_up])
        a_new = velocity + step_length * (
            gradient
            + east_wind * east_diff[1:]
            + north_wind * north_diff[1:]
            + vertical_wind * up_diff[1:]
        )
        forward = forward_field[snap].astype(jnp.float32)
        rims = tuple(
            tuple(side[snap].astype(jnp.float32) for side in pair) for pair in forward_rims
        )
        f_east, f_north, f_up = central(forward, rims)
        pieces = [p_new * (f_east[1] + f_north[2] + f_up[3])]
        for along in (f_east, f_north, f_up):
            pieces.append(
                p_new * along[0] + a_new[0] * along[1] + a_new[1] * along[2] + a_new[2] * along[3]
            )
        increment = jnp.stack(pieces)
        kernel_local = kernel_local + increment
        state = jnp.concatenate([p_new[None], a_new], axis=0)
    kernels = lax.psum_scatter(kernel_local, "pair", scatter_dimension=3, tiled=True)
    return (kernels, state[None])


def solution(mesh):
    in_specs = (
        P("gx", "gy", None),
        P(),
        P(None, None, "gx", "gy", None),
        P("pair", None, "gx", "gy", None),
        P("pair"),
        P("pair", None),
        P("pair", None),
        P("pair", None),
    )
    out_specs = (P(None, "gx", "gy", "pair"), P("pair", None, "gx", "gy", None))
    return jax.shard_map(shards, mesh=mesh, in_specs=in_specs, out_specs=out_specs, check_vma=False)
```

```python
import functools

import jax
import jax.numpy as jnp
from jax import lax
from jax.experimental import pallas as pl
from jax.experimental.pallas import tpu as pltpu
from jax.sharding import PartitionSpec as P

step_length = 0.25
MESH = pl.DeviceIdType.MESH


def neighbours(shard, axis, dim):
    size, length = (lax.axis_size(axis), shard.shape[dim])
    up = [(i, i + 1) for i in range(size - 1)]
    down = [(i + 1, i) for i in range(size - 1)]
    last = lax.slice_in_dim(shard, length - 1, length, axis=dim)
    first = lax.slice_in_dim(shard, 0, 1, axis=dim)
    before = lax.ppermute(last, axis, up)
    after = lax.ppermute(first, axis, down)
    return (before, after)


def local_cells(cells, width_x, width_y):
    local_x = cells[:, 0] - lax.axis_index("gx") * width_x
    local_y = cells[:, 1] - lax.axis_index("gy") * width_y
    inside = (local_x >= 0) & (local_x < width_x) & (local_y >= 0) & (local_y < width_y)
    return (
        jnp.clip(local_x, 0, width_x - 1),
        jnp.clip(local_y, 0, width_y - 1),
        cells[:, 2],
        inside.astype(jnp.float32),
    )


def stencil_kernel(
    nx, ny, steps,
    state_in, sound, wind, fpad, fyr, inj,
    state_out, acc_out,
    pads, pbuf, ysend, yrecv, ypsend, yprecv, ss, rs, ps, pr,
):
    _, width_x, width_y, depth = state_in.shape
    me_p = lax.axis_index("pair")
    gx = lax.axis_index("gx")
    gy = lax.axis_index("gy")
    has_lo_x = gx > 0
    has_hi_x = gx < nx - 1
    has_lo_y = gy > 0
    has_hi_y = gy < ny - 1
    dev_lo_x = (me_p, gx - 1, gy)
    dev_hi_x = (me_p, gx + 1, gy)
    dev_lo_y = (me_p, gx, gy - 1)
    dev_hi_y = (me_p, gx, gy + 1)

    zero_slab = jnp.zeros((width_y, depth), jnp.float32)
    for par in range(2):
        for c in range(4):
            pads[par, c, 0] = zero_slab
            pads[par, c, width_x + 1] = zero_slab
            for side in range(2):
                yrecv[par, side, c] = jnp.zeros((width_x, 1, depth), jnp.float32)
    pbuf[0] = zero_slab
    pbuf[width_x + 1] = zero_slab
    for side in range(2):
        yprecv[side] = jnp.zeros((width_x, 1, depth), jnp.float32)

    barrier = pltpu.get_barrier_semaphore()
    for cond, dev in ((has_lo_x, dev_lo_x), (has_hi_x, dev_hi_x), (has_lo_y, dev_lo_y), (has_hi_y, dev_hi_y)):
        @pl.when(cond)
        def _():
            pl.semaphore_signal(barrier, 1, device_id=dev, device_id_type=MESH)
    peers = (
        (gx + nx - 1) // nx + (2 * nx - 2 - gx) // nx
        + (gy + ny - 1) // ny + (2 * ny - 2 - gy) // ny
    )
    pl.semaphore_wait(barrier, peers)

    iy = lax.broadcasted_iota(jnp.int32, (width_y, depth), 0)
    iz = lax.broadcasted_iota(jnp.int32, (width_y, depth), 1)
    we = wind[0:1, :]
    wn = wind[1:2, :]
    wv = wind[2:3, :]

    def dy(v, lo, hi):
        up = jnp.where(iy == width_y - 1, hi, pltpu.roll(v, width_y - 1, 0))
        down = jnp.where(iy == 0, lo, pltpu.roll(v, 1, 0))
        return (up - down) * 0.5

    def dz(v):
        up = jnp.where(iz == depth - 1, 0.0, pltpu.roll(v, depth - 1, 1))
        down = jnp.where(iz == 0, 0.0, pltpu.roll(v, 1, 1))
        return (up - down) * 0.5

    def exchange(src_lo_x, src_hi_x, dst_lo_x, dst_hi_x, src_y_hi, src_y_lo, dst_y_lo, dst_y_hi, send, recv):
        outs = (
            (has_hi_x, src_hi_x, dst_lo_x, 0, dev_hi_x),
            (has_lo_x, src_lo_x, dst_hi_x, 1, dev_lo_x),
            (has_hi_y, src_y_hi, dst_y_lo, 2, dev_hi_y),
            (has_lo_y, src_y_lo, dst_y_hi, 3, dev_lo_y),
        )
        copies = []
        for cond, src, dst, slot, dev in outs:
            copy = pltpu.make_async_remote_copy(
                src_ref=src, dst_ref=dst, send_sem=send.at[slot], recv_sem=recv.at[slot],
                device_id=dev, device_id_type=MESH,
            )
            copies.append((cond, copy))

            @pl.when(cond)
            def _():
                copy.start()
        incoming = (has_lo_x, has_hi_x, has_lo_y, has_hi_y)
        for (cond, copy), arrives in zip(copies, incoming):
            @pl.when(cond)
            def _():
                copy.wait_send()

            @pl.when(arrives)
            def _():
                copy.wait_recv()

    def fill_state(par, x, c, v):
        pads[par, c, x + 1] = v
        ysend[par, 0, c, x] = v[width_y - 1:width_y, :]
        ysend[par, 1, c, x] = v[0:1, :]

    def copy_in(x, carry):
        for c in range(4):
            fill_state(0, x, c, state_in[c, x])
        return carry

    lax.fori_loop(0, width_x, copy_in, 0)

    for step in range(steps):
        par = step % 2
        nxt = 1 - par
        snap = steps - 1 - step
        last = step == steps - 1
        exchange(
            pads.at[par, :, pl.ds(1, 1)], pads.at[par, :, pl.ds(width_x, 1)],
            pads.at[par, :, pl.ds(0, 1)], pads.at[par, :, pl.ds(width_x + 1, 1)],
            ysend.at[par, 0], ysend.at[par, 1], yrecv.at[par, 0], yrecv.at[par, 1],
            ss.at[par], rs.at[par],
        )

        def pressure_slab(x, carry, par=par, snap=snap):
            xp = x + 1
            old = pads.at[par]
            p = old[0, xp]
            dxp = (old[0, xp + 1] - old[0, x]) * 0.5
            dxa = (old[1, xp + 1] - old[1, x]) * 0.5
            dyp = dy(p, yrecv[par, 0, 0, x], yrecv[par, 1, 0, x])
            dya = dy(old[2, xp], yrecv[par, 0, 2, x], yrecv[par, 1, 2, x])
            dzp = dz(p)
            dza = dz(old[3, xp])
            divergence = dxa + dya + dza
            p_new = (
                p
                + step_length * (sound[x] * divergence + we * dxp + wn * dyp + wv * dzp)
                + inj[snap, x]
            )
            pbuf[xp] = p_new
            ypsend[0, x] = p_new[width_y - 1:width_y, :]
            ypsend[1, x] = p_new[0:1, :]
            return carry

        lax.fori_loop(0, width_x, pressure_slab, 0)
        exchange(
            pbuf.at[pl.ds(1, 1)], pbuf.at[pl.ds(width_x, 1)],
            pbuf.at[pl.ds(0, 1)], pbuf.at[pl.ds(width_x + 1, 1)],
            ypsend.at[0], ypsend.at[1], yprecv.at[0], yprecv.at[1],
            ps, pr,
        )

        def velocity_slab(x, carry, par=par, nxt=nxt, snap=snap, last=last, step=step):
            xp = x + 1
            old = pads.at[par]
            p_new = pbuf[xp]
            grad = (
                (pbuf[xp + 1] - pbuf[x]) * 0.5,
                dy(p_new, yprecv[0, x], yprecv[1, x]),
                dz(p_new),
            )
            a_new = []
            for i in range(3):
                a = old[1 + i, xp]
                dxa = (old[1 + i, xp + 1] - old[1 + i, x]) * 0.5
                dya = dy(a, yrecv[par, 0, 1 + i, x], yrecv[par, 1, 1 + i, x])
                dza = dz(a)
                a_new.append(a + step_length * (grad[i] + we * dxa + wn * dya + wv * dza))
            fe, fn, fu = [], [], []
            for c in range(4):
                f = fpad[snap, c, xp].astype(jnp.float32)
                fe.append((fpad[snap, c, xp + 1].astype(jnp.float32) - fpad[snap, c, x].astype(jnp.float32)) * 0.5)
                fn.append(dy(f, fyr[snap, 0, c, x].astype(jnp.float32), fyr[snap, 1, c, x].astype(jnp.float32)))
                fu.append(dz(f))
            pieces = [p_new * (fe[1] + fn[2] + fu[3])]
            for along in (fe, fn, fu):
                pieces.append(p_new * along[0] + a_new[0] * along[1] + a_new[1] * along[2] + a_new[2] * along[3])
            for c in range(4):
                if step == 0:
                    acc_out[c, x] = pieces[c]
                else:
                    acc_out[c, x] = acc_out[c, x] + pieces[c]
            new_state = [p_new] + a_new
            for c in range(4):
                if last:
                    state_out[c, x] = new_state[c]
                else:
                    fill_state(nxt, x, c, new_state[c])
            return carry

        lax.fori_loop(0, width_x, velocity_slab, 0)


def shards(
    sound_speed_sq,
    wind_profile,
    forward_field,
    adjoint_state,
    pair_counts,
    source_cells,
    receiver_cells,
    residuals,
):
    steps_total = forward_field.shape[0]
    width_x, width_y, depth = sound_speed_sq.shape
    slots = residuals.shape[0]
    live = (jnp.arange(slots, dtype=jnp.int32) < pair_counts[0]).astype(jnp.float32)
    sx, sy, sz, src_inside = local_cells(source_cells, width_x, width_y)
    rx, ry, rz, rcv_inside = local_cells(receiver_cells, width_x, width_y)
    local_samples = jnp.stack(
        [forward_field[t, 0][sx, sy, sz] for t in range(steps_total)]
    ).astype(jnp.float32) * src_inside[None, :]
    me = lax.axis_index("pair")
    slot = jnp.zeros((lax.axis_size("pair"),) + local_samples.shape, jnp.float32)
    samples = lax.psum(slot.at[me].set(local_samples), ("pair", "gx", "gy"))[me]
    amplitude = jnp.transpose(residuals) * samples * (live * rcv_inside)[None, :]
    rcv_flat = (rx * width_y + ry) * depth + rz
    step_index = jnp.broadcast_to(jnp.arange(steps_total)[:, None], amplitude.shape)
    injected = (
        jnp.zeros((steps_total, width_x * width_y * depth), jnp.float32)
        .at[step_index, jnp.broadcast_to(rcv_flat[None, :], amplitude.shape)]
        .add(amplitude)
        .reshape(steps_total, width_x, width_y, depth)
    )
    lo_x, hi_x = neighbours(forward_field, "gx", 2)
    fpad = jnp.concatenate([lo_x, forward_field, hi_x], axis=2)
    up = [(i, i + 1) for i in range(lax.axis_size("gy") - 1)]
    down = [(i + 1, i) for i in range(lax.axis_size("gy") - 1)]
    lo_y = lax.ppermute(forward_field[:, :, :, width_y - 1:width_y, :], "gy", up)
    hi_y = lax.ppermute(forward_field[:, :, :, 0:1, :], "gy", down)
    fyr = jnp.stack([lo_y, hi_y], axis=1)

    vmem = pl.BlockSpec(memory_space=pltpu.VMEM)
    kernel = functools.partial(
        stencil_kernel, lax.axis_size("gx"), lax.axis_size("gy"), steps_total
    )
    state_new, kernel_local = pl.pallas_call(
        kernel,
        out_shape=(
            jax.ShapeDtypeStruct((4, width_x, width_y, depth), jnp.float32),
            jax.ShapeDtypeStruct((4, width_x, width_y, depth), jnp.float32),
        ),
        in_specs=[vmem] * 6,
        out_specs=(vmem, vmem),
        scratch_shapes=[
            pltpu.VMEM((2, 4, width_x + 2, width_y, depth), jnp.float32),
            pltpu.VMEM((width_x + 2, width_y, depth), jnp.float32),
            pltpu.VMEM((2, 2, 4, width_x, 1, depth), jnp.float32),
            pltpu.VMEM((2, 2, 4, width_x, 1, depth), jnp.float32),
            pltpu.VMEM((2, width_x, 1, depth), jnp.float32),
            pltpu.VMEM((2, width_x, 1, depth), jnp.float32),
            pltpu.SemaphoreType.DMA((2, 4)),
            pltpu.SemaphoreType.DMA((2, 4)),
            pltpu.SemaphoreType.DMA((4,)),
            pltpu.SemaphoreType.DMA((4,)),
        ],
        compiler_params=pltpu.CompilerParams(
            collective_id=0, has_side_effects=True, vmem_limit_bytes=48 * 1024 * 1024
        ),
    )(adjoint_state[0], sound_speed_sq, wind_profile, fpad, fyr, injected)
    kernels = lax.psum_scatter(kernel_local, "pair", scatter_dimension=3, tiled=True)
    return (kernels, state_new[None])


def solution(mesh):
    in_specs = (
        P("gx", "gy", None),
        P(),
        P(None, None, "gx", "gy", None),
        P("pair", None, "gx", "gy", None),
        P("pair"),
        P("pair", None),
        P("pair", None),
        P("pair", None),
    )
    out_specs = (P(None, "gx", "gy", "pair"), P("pair", None, "gx", "gy", None))
    return jax.shard_map(shards, mesh=mesh, in_specs=in_specs, out_specs=out_specs, check_vma=False)
```

```python
import functools

import jax
import jax.numpy as jnp
from jax import lax
from jax.experimental import pallas as pl
from jax.experimental.pallas import tpu as pltpu
from jax.sharding import PartitionSpec as P

step_length = 0.25
MESH = pl.DeviceIdType.MESH


def neighbours(shard, axis, dim):
    size, length = (lax.axis_size(axis), shard.shape[dim])
    up = [(i, i + 1) for i in range(size - 1)]
    down = [(i + 1, i) for i in range(size - 1)]
    last = lax.slice_in_dim(shard, length - 1, length, axis=dim)
    first = lax.slice_in_dim(shard, 0, 1, axis=dim)
    before = lax.ppermute(last, axis, up)
    after = lax.ppermute(first, axis, down)
    return (before, after)


def local_cells(cells, width_x, width_y):
    local_x = cells[:, 0] - lax.axis_index("gx") * width_x
    local_y = cells[:, 1] - lax.axis_index("gy") * width_y
    inside = (local_x >= 0) & (local_x < width_x) & (local_y >= 0) & (local_y < width_y)
    return (
        jnp.clip(local_x, 0, width_x - 1),
        jnp.clip(local_y, 0, width_y - 1),
        cells[:, 2],
        inside.astype(jnp.float32),
    )


def stencil_kernel(
    nx, ny, steps,
    state_in, sound, wind, fpad, fyr, inj,
    state_out, acc_out,
    pads, pbuf, ysend, yrecv, ypsend, yprecv, ss, rs, ps, pr,
):
    _, width_x, width_y, depth = state_in.shape
    me_p = lax.axis_index("pair")
    gx = lax.axis_index("gx")
    gy = lax.axis_index("gy")
    has_lo_x = gx > 0
    has_hi_x = gx < nx - 1
    has_lo_y = gy > 0
    has_hi_y = gy < ny - 1
    dev_lo_x = (me_p, gx - 1, gy)
    dev_hi_x = (me_p, gx + 1, gy)
    dev_lo_y = (me_p, gx, gy - 1)
    dev_hi_y = (me_p, gx, gy + 1)

    zero_slab = jnp.zeros((width_y, depth), jnp.float32)
    for par in range(2):
        for c in range(4):
            pads[par, c, 0] = zero_slab
            pads[par, c, width_x + 1] = zero_slab
            for side in range(2):
                yrecv[par, side, c] = jnp.zeros((width_x, 1, depth), jnp.float32)
    pbuf[0] = zero_slab
    pbuf[width_x + 1] = zero_slab
    for side in range(2):
        yprecv[side] = jnp.zeros((width_x, 1, depth), jnp.float32)

    barrier = pltpu.get_barrier_semaphore()
    for cond, dev in ((has_lo_x, dev_lo_x), (has_hi_x, dev_hi_x), (has_lo_y, dev_lo_y), (has_hi_y, dev_hi_y)):
        @pl.when(cond)
        def _():
            pl.semaphore_signal(barrier, 1, device_id=dev, device_id_type=MESH)
    peers = (
        (gx + nx - 1) // nx + (2 * nx - 2 - gx) // nx
        + (gy + ny - 1) // ny + (2 * ny - 2 - gy) // ny
    )
    pl.semaphore_wait(barrier, peers)

    iy = lax.broadcasted_iota(jnp.int32, (width_y, depth), 0)
    iz = lax.broadcasted_iota(jnp.int32, (width_y, depth), 1)
    we = wind[0:1, :]
    wn = wind[1:2, :]
    wv = wind[2:3, :]

    def dy(v, lo, hi):
        up = jnp.where(iy == width_y - 1, hi, pltpu.roll(v, width_y - 1, 0))
        down = jnp.where(iy == 0, lo, pltpu.roll(v, 1, 0))
        return (up - down) * 0.5

    def dz(v):
        up = jnp.where(iz == depth - 1, 0.0, pltpu.roll(v, depth - 1, 1))
        down = jnp.where(iz == 0, 0.0, pltpu.roll(v, 1, 1))
        return (up - down) * 0.5

    def exchange(src_lo_x, src_hi_x, dst_lo_x, dst_hi_x, src_y_hi, src_y_lo, dst_y_lo, dst_y_hi, send, recv):
        outs = (
            (has_hi_x, src_hi_x, dst_lo_x, 0, dev_hi_x),
            (has_lo_x, src_lo_x, dst_hi_x, 1, dev_lo_x),
            (has_hi_y, src_y_hi, dst_y_lo, 2, dev_hi_y),
            (has_lo_y, src_y_lo, dst_y_hi, 3, dev_lo_y),
        )
        copies = []
        for cond, src, dst, slot, dev in outs:
            copy = pltpu.make_async_remote_copy(
                src_ref=src, dst_ref=dst, send_sem=send.at[slot], recv_sem=recv.at[slot],
                device_id=dev, device_id_type=MESH,
            )
            copies.append((cond, copy))

            @pl.when(cond)
            def _():
                copy.start()
        incoming = (has_lo_x, has_hi_x, has_lo_y, has_hi_y)
        for (cond, copy), arrives in zip(copies, incoming):
            @pl.when(cond)
            def _():
                copy.wait_send()

            @pl.when(arrives)
            def _():
                copy.wait_recv()

    def fill_state(par, x, c, v):
        pads[par, c, x + 1] = v
        ysend[par, 0, c, x] = v[width_y - 1:width_y, :]
        ysend[par, 1, c, x] = v[0:1, :]

    def copy_in(x, carry):
        for c in range(4):
            fill_state(0, x, c, state_in[c, x])
        return carry

    lax.fori_loop(0, width_x, copy_in, 0)

    for step in range(steps):
        par = step % 2
        nxt = 1 - par
        snap = steps - 1 - step
        last = step == steps - 1
        exchange(
            pads.at[par, :, pl.ds(1, 1)], pads.at[par, :, pl.ds(width_x, 1)],
            pads.at[par, :, pl.ds(0, 1)], pads.at[par, :, pl.ds(width_x + 1, 1)],
            ysend.at[par, 0], ysend.at[par, 1], yrecv.at[par, 0], yrecv.at[par, 1],
            ss.at[par], rs.at[par],
        )

        def pressure_slab(x, carry, par=par, snap=snap):
            xp = x + 1
            old = pads.at[par]
            p = old[0, xp]
            dxp = (old[0, xp + 1] - old[0, x]) * 0.5
            dxa = (old[1, xp + 1] - old[1, x]) * 0.5
            dyp = dy(p, yrecv[par, 0, 0, x], yrecv[par, 1, 0, x])
            dya = dy(old[2, xp], yrecv[par, 0, 2, x], yrecv[par, 1, 2, x])
            dzp = dz(p)
            dza = dz(old[3, xp])
            divergence = dxa + dya + dza
            p_new = (
                p
                + step_length * (sound[x] * divergence + we * dxp + wn * dyp + wv * dzp)
                + inj[snap, x]
            )
            pbuf[xp] = p_new
            ypsend[0, x] = p_new[width_y - 1:width_y, :]
            ypsend[1, x] = p_new[0:1, :]
            return carry

        lax.fori_loop(0, width_x, pressure_slab, 0)
        exchange(
            pbuf.at[pl.ds(1, 1)], pbuf.at[pl.ds(width_x, 1)],
            pbuf.at[pl.ds(0, 1)], pbuf.at[pl.ds(width_x + 1, 1)],
            ypsend.at[0], ypsend.at[1], yprecv.at[0], yprecv.at[1],
            ps, pr,
        )

        def velocity_slab(x, carry, par=par, nxt=nxt, snap=snap, last=last, step=step):
            xp = x + 1
            old = pads.at[par]
            p_new = pbuf[xp]
            grad = (
                (pbuf[xp + 1] - pbuf[x]) * 0.5,
                dy(p_new, yprecv[0, x], yprecv[1, x]),
                dz(p_new),
            )
            a_new = []
            for i in range(3):
                a = old[1 + i, xp]
                dxa = (old[1 + i, xp + 1] - old[1 + i, x]) * 0.5
                dya = dy(a, yrecv[par, 0, 1 + i, x], yrecv[par, 1, 1 + i, x])
                dza = dz(a)
                a_new.append(a + step_length * (grad[i] + we * dxa + wn * dya + wv * dza))
            fe, fn, fu = [], [], []
            for c in range(4):
                f = fpad[snap, c, xp].astype(jnp.float32)
                fe.append((fpad[snap, c, xp + 1].astype(jnp.float32) - fpad[snap, c, x].astype(jnp.float32)) * 0.5)
                fn.append(dy(f, fyr[snap, 0, c, x].astype(jnp.float32), fyr[snap, 1, c, x].astype(jnp.float32)))
                fu.append(dz(f))
            pieces = [p_new * (fe[1] + fn[2] + fu[3])]
            for along in (fe, fn, fu):
                pieces.append(p_new * along[0] + a_new[0] * along[1] + a_new[1] * along[2] + a_new[2] * along[3])
            for c in range(4):
                if step == 0:
                    acc_out[c, x] = pieces[c]
                else:
                    acc_out[c, x] = acc_out[c, x] + pieces[c]
            new_state = [p_new] + a_new
            for c in range(4):
                if last:
                    state_out[c, x] = new_state[c]
                else:
                    fill_state(nxt, x, c, new_state[c])
            return carry

        lax.fori_loop(0, width_x, velocity_slab, 0)


def samples_kernel(nx, ny, local_ref, out_ref, sent, got, send_sem, recv_sem):
    me_p = lax.axis_index("pair")
    gx = lax.axis_index("gx")
    gy = lax.axis_index("gy")
    rounds = []
    k = 1
    while k < nx:
        rounds.append((me_p, gx + k - 2 * k * ((gx // k) % 2), gy))
        k *= 2
    k = 1
    while k < ny:
        rounds.append((me_p, gx, gy + k - 2 * k * ((gy // k) % 2)))
        k *= 2
    barrier = pltpu.get_barrier_semaphore()
    for dev in rounds:
        pl.semaphore_signal(barrier, 1, device_id=dev, device_id_type=MESH)
    pl.semaphore_wait(barrier, len(rounds))
    total = local_ref[...]
    for r, dev in enumerate(rounds):
        src = local_ref
        if r > 0:
            sent[r] = total
            src = sent.at[r]
        copy = pltpu.make_async_remote_copy(
            src_ref=src, dst_ref=got.at[r], send_sem=send_sem.at[r], recv_sem=recv_sem.at[r],
            device_id=dev, device_id_type=MESH,
        )
        copy.start()
        copy.wait_send()
        copy.wait_recv()
        total = total + got[r]
    out_ref[...] = total


def gathered_samples(local_samples):
    nx, ny = lax.axis_size("gx"), lax.axis_size("gy")
    rounds = (nx.bit_length() - 1) + (ny.bit_length() - 1)
    if (nx & (nx - 1)) or (ny & (ny - 1)) or rounds == 0:
        return lax.psum(local_samples, ("gx", "gy"))
    vmem = pl.BlockSpec(memory_space=pltpu.VMEM)
    return pl.pallas_call(
        functools.partial(samples_kernel, nx, ny),
        out_shape=jax.ShapeDtypeStruct(local_samples.shape, jnp.float32),
        in_specs=[vmem],
        out_specs=vmem,
        scratch_shapes=[
            pltpu.VMEM((rounds,) + local_samples.shape, jnp.float32),
            pltpu.VMEM((rounds,) + local_samples.shape, jnp.float32),
            pltpu.SemaphoreType.DMA((rounds,)),
            pltpu.SemaphoreType.DMA((rounds,)),
        ],
        compiler_params=pltpu.CompilerParams(collective_id=1, has_side_effects=True),
    )(local_samples)


def shards(
    sound_speed_sq,
    wind_profile,
    forward_field,
    adjoint_state,
    pair_counts,
    source_cells,
    receiver_cells,
    residuals,
):
    steps_total = forward_field.shape[0]
    width_x, width_y, depth = sound_speed_sq.shape
    slots = residuals.shape[0]
    live = (jnp.arange(slots, dtype=jnp.int32) < pair_counts[0]).astype(jnp.float32)
    sx, sy, sz, src_inside = local_cells(source_cells, width_x, width_y)
    rx, ry, rz, rcv_inside = local_cells(receiver_cells, width_x, width_y)
    local_samples = jnp.stack(
        [forward_field[t, 0][sx, sy, sz] for t in range(steps_total)]
    ).astype(jnp.float32) * src_inside[None, :]
    samples = gathered_samples(local_samples)
    amplitude = jnp.transpose(residuals) * samples * (live * rcv_inside)[None, :]
    rcv_flat = (rx * width_y + ry) * depth + rz
    step_index = jnp.broadcast_to(jnp.arange(steps_total)[:, None], amplitude.shape)
    injected = (
        jnp.zeros((steps_total, width_x * width_y * depth), jnp.float32)
        .at[step_index, jnp.broadcast_to(rcv_flat[None, :], amplitude.shape)]
        .add(amplitude)
        .reshape(steps_total, width_x, width_y, depth)
    )
    lo_x, hi_x = neighbours(forward_field, "gx", 2)
    fpad = jnp.concatenate([lo_x, forward_field, hi_x], axis=2)
    up = [(i, i + 1) for i in range(lax.axis_size("gy") - 1)]
    down = [(i + 1, i) for i in range(lax.axis_size("gy") - 1)]
    lo_y = lax.ppermute(forward_field[:, :, :, width_y - 1:width_y, :], "gy", up)
    hi_y = lax.ppermute(forward_field[:, :, :, 0:1, :], "gy", down)
    fyr = jnp.stack([lo_y, hi_y], axis=1)

    vmem = pl.BlockSpec(memory_space=pltpu.VMEM)
    kernel = functools.partial(
        stencil_kernel, lax.axis_size("gx"), lax.axis_size("gy"), steps_total
    )
    state_new, kernel_local = pl.pallas_call(
        kernel,
        out_shape=(
            jax.ShapeDtypeStruct((4, width_x, width_y, depth), jnp.float32),
            jax.ShapeDtypeStruct((4, width_x, width_y, depth), jnp.float32),
        ),
        in_specs=[vmem] * 6,
        out_specs=(vmem, vmem),
        scratch_shapes=[
            pltpu.VMEM((2, 4, width_x + 2, width_y, depth), jnp.float32),
            pltpu.VMEM((width_x + 2, width_y, depth), jnp.float32),
            pltpu.VMEM((2, 2, 4, width_x, 1, depth), jnp.float32),
            pltpu.VMEM((2, 2, 4, width_x, 1, depth), jnp.float32),
            pltpu.VMEM((2, width_x, 1, depth), jnp.float32),
            pltpu.VMEM((2, width_x, 1, depth), jnp.float32),
            pltpu.SemaphoreType.DMA((2, 4)),
            pltpu.SemaphoreType.DMA((2, 4)),
            pltpu.SemaphoreType.DMA((4,)),
            pltpu.SemaphoreType.DMA((4,)),
        ],
        compiler_params=pltpu.CompilerParams(
            collective_id=0, has_side_effects=True, vmem_limit_bytes=48 * 1024 * 1024
        ),
    )(adjoint_state[0], sound_speed_sq, wind_profile, fpad, fyr, injected)
    kernels = lax.psum_scatter(kernel_local, "pair", scatter_dimension=3, tiled=True)
    return (kernels, state_new[None])


def solution(mesh):
    in_specs = (
        P("gx", "gy", None),
        P(),
        P(None, None, "gx", "gy", None),
        P("pair", None, "gx", "gy", None),
        P("pair"),
        P("pair", None),
        P("pair", None),
        P("pair", None),
    )
    out_specs = (P(None, "gx", "gy", "pair"), P("pair", None, "gx", "gy", None))
    return jax.shard_map(shards, mesh=mesh, in_specs=in_specs, out_specs=out_specs, check_vma=False)
```

```python
import functools

import jax
import jax.numpy as jnp
from jax import lax
from jax.experimental import pallas as pl
from jax.experimental.pallas import tpu as pltpu
from jax.sharding import PartitionSpec as P

step_length = 0.25
MESH = pl.DeviceIdType.MESH


def neighbours(shard, axis, dim):
    size, length = (lax.axis_size(axis), shard.shape[dim])
    up = [(i, i + 1) for i in range(size - 1)]
    down = [(i + 1, i) for i in range(size - 1)]
    last = lax.slice_in_dim(shard, length - 1, length, axis=dim)
    first = lax.slice_in_dim(shard, 0, 1, axis=dim)
    before = lax.ppermute(last, axis, up)
    after = lax.ppermute(first, axis, down)
    return (before, after)


def local_cells(cells, width_x, width_y):
    local_x = cells[:, 0] - lax.axis_index("gx") * width_x
    local_y = cells[:, 1] - lax.axis_index("gy") * width_y
    inside = (local_x >= 0) & (local_x < width_x) & (local_y >= 0) & (local_y < width_y)
    return (
        jnp.clip(local_x, 0, width_x - 1),
        jnp.clip(local_y, 0, width_y - 1),
        cells[:, 2],
        inside.astype(jnp.float32),
    )


def stencil_kernel(
    nx, ny, steps,
    state_in, sound, wind, fpad, fyr, inj,
    state_out, kernel_out,
    pads, pbuf, ysend, yrecv, ypsend, yprecv, acc_out, ksend, krecv, ss, rs, ps, pr, ks, kr,
):
    _, width_x, width_y, depth = state_in.shape
    me_p = lax.axis_index("pair")
    gx = lax.axis_index("gx")
    gy = lax.axis_index("gy")
    has_lo_x = gx > 0
    has_hi_x = gx < nx - 1
    has_lo_y = gy > 0
    has_hi_y = gy < ny - 1
    dev_lo_x = (me_p, gx - 1, gy)
    dev_hi_x = (me_p, gx + 1, gy)
    dev_lo_y = (me_p, gx, gy - 1)
    dev_hi_y = (me_p, gx, gy + 1)
    dev_pair = (1 - me_p, gx, gy)
    half = depth // 2

    zero_slab = jnp.zeros((width_y, depth), jnp.float32)
    for par in range(2):
        for c in range(4):
            pads[par, c, 0] = zero_slab
            pads[par, c, width_x + 1] = zero_slab
            for side in range(2):
                yrecv[par, side, c] = jnp.zeros((width_x, 1, depth), jnp.float32)
    pbuf[0] = zero_slab
    pbuf[width_x + 1] = zero_slab
    for side in range(2):
        yprecv[side] = jnp.zeros((width_x, 1, depth), jnp.float32)

    barrier = pltpu.get_barrier_semaphore()
    pl.semaphore_signal(barrier, 1, device_id=dev_pair, device_id_type=MESH)
    for cond, dev in ((has_lo_x, dev_lo_x), (has_hi_x, dev_hi_x), (has_lo_y, dev_lo_y), (has_hi_y, dev_hi_y)):
        @pl.when(cond)
        def _():
            pl.semaphore_signal(barrier, 1, device_id=dev, device_id_type=MESH)
    peers = 1 + (
        (gx + nx - 1) // nx + (2 * nx - 2 - gx) // nx
        + (gy + ny - 1) // ny + (2 * ny - 2 - gy) // ny
    )
    pl.semaphore_wait(barrier, peers)

    iy = lax.broadcasted_iota(jnp.int32, (width_y, depth), 0)
    iz = lax.broadcasted_iota(jnp.int32, (width_y, depth), 1)
    we = wind[0:1, :]
    wn = wind[1:2, :]
    wv = wind[2:3, :]

    def dy(v, lo, hi):
        up = jnp.where(iy == width_y - 1, hi, pltpu.roll(v, width_y - 1, 0))
        down = jnp.where(iy == 0, lo, pltpu.roll(v, 1, 0))
        return (up - down) * 0.5

    def dz(v):
        up = jnp.where(iz == depth - 1, 0.0, pltpu.roll(v, depth - 1, 1))
        down = jnp.where(iz == 0, 0.0, pltpu.roll(v, 1, 1))
        return (up - down) * 0.5

    def exchange(src_lo_x, src_hi_x, dst_lo_x, dst_hi_x, src_y_hi, src_y_lo, dst_y_lo, dst_y_hi, send, recv):
        outs = (
            (has_hi_x, src_hi_x, dst_lo_x, 0, dev_hi_x),
            (has_lo_x, src_lo_x, dst_hi_x, 1, dev_lo_x),
            (has_hi_y, src_y_hi, dst_y_lo, 2, dev_hi_y),
            (has_lo_y, src_y_lo, dst_y_hi, 3, dev_lo_y),
        )
        copies = []
        for cond, src, dst, slot, dev in outs:
            copy = pltpu.make_async_remote_copy(
                src_ref=src, dst_ref=dst, send_sem=send.at[slot], recv_sem=recv.at[slot],
                device_id=dev, device_id_type=MESH,
            )
            copies.append((cond, copy))

            @pl.when(cond)
            def _():
                copy.start()
        incoming = (has_lo_x, has_hi_x, has_lo_y, has_hi_y)
        for (cond, copy), arrives in zip(copies, incoming):
            @pl.when(cond)
            def _():
                copy.wait_send()

            @pl.when(arrives)
            def _():
                copy.wait_recv()

    def fill_state(par, x, c, v):
        pads[par, c, x + 1] = v
        ysend[par, 0, c, x] = v[width_y - 1:width_y, :]
        ysend[par, 1, c, x] = v[0:1, :]

    def copy_in(x, carry):
        for c in range(4):
            fill_state(0, x, c, state_in[c, x])
        return carry

    lax.fori_loop(0, width_x, copy_in, 0)

    for step in range(steps):
        par = step % 2
        nxt = 1 - par
        snap = steps - 1 - step
        last = step == steps - 1
        exchange(
            pads.at[par, :, pl.ds(1, 1)], pads.at[par, :, pl.ds(width_x, 1)],
            pads.at[par, :, pl.ds(0, 1)], pads.at[par, :, pl.ds(width_x + 1, 1)],
            ysend.at[par, 0], ysend.at[par, 1], yrecv.at[par, 0], yrecv.at[par, 1],
            ss.at[par], rs.at[par],
        )

        def pressure_slab(x, carry, par=par, snap=snap):
            xp = x + 1
            old = pads.at[par]
            p = old[0, xp]
            dxp = (old[0, xp + 1] - old[0, x]) * 0.5
            dxa = (old[1, xp + 1] - old[1, x]) * 0.5
            dyp = dy(p, yrecv[par, 0, 0, x], yrecv[par, 1, 0, x])
            dya = dy(old[2, xp], yrecv[par, 0, 2, x], yrecv[par, 1, 2, x])
            dzp = dz(p)
            dza = dz(old[3, xp])
            divergence = dxa + dya + dza
            p_new = (
                p
                + step_length * (sound[x] * divergence + we * dxp + wn * dyp + wv * dzp)
                + inj[snap, x]
            )
            pbuf[xp] = p_new
            ypsend[0, x] = p_new[width_y - 1:width_y, :]
            ypsend[1, x] = p_new[0:1, :]
            return carry

        lax.fori_loop(0, width_x, pressure_slab, 0)
        exchange(
            pbuf.at[pl.ds(1, 1)], pbuf.at[pl.ds(width_x, 1)],
            pbuf.at[pl.ds(0, 1)], pbuf.at[pl.ds(width_x + 1, 1)],
            ypsend.at[0], ypsend.at[1], yprecv.at[0], yprecv.at[1],
            ps, pr,
        )

        def velocity_slab(x, carry, par=par, nxt=nxt, snap=snap, last=last, step=step):
            xp = x + 1
            old = pads.at[par]
            p_new = pbuf[xp]
            grad = (
                (pbuf[xp + 1] - pbuf[x]) * 0.5,
                dy(p_new, yprecv[0, x], yprecv[1, x]),
                dz(p_new),
            )
            a_new = []
            for i in range(3):
                a = old[1 + i, xp]
                dxa = (old[1 + i, xp + 1] - old[1 + i, x]) * 0.5
                dya = dy(a, yrecv[par, 0, 1 + i, x], yrecv[par, 1, 1 + i, x])
                dza = dz(a)
                a_new.append(a + step_length * (grad[i] + we * dxa + wn * dya + wv * dza))
            fe, fn, fu = [], [], []
            for c in range(4):
                f = fpad[snap, c, xp].astype(jnp.float32)
                fe.append((fpad[snap, c, xp + 1].astype(jnp.float32) - fpad[snap, c, x].astype(jnp.float32)) * 0.5)
                fn.append(dy(f, fyr[snap, 0, c, x].astype(jnp.float32), fyr[snap, 1, c, x].astype(jnp.float32)))
                fu.append(dz(f))
            pieces = [p_new * (fe[1] + fn[2] + fu[3])]
            for along in (fe, fn, fu):
                pieces.append(p_new * along[0] + a_new[0] * along[1] + a_new[1] * along[2] + a_new[2] * along[3])
            for c in range(4):
                total = pieces[c] if step == 0 else acc_out[c, x] + pieces[c]
                if not last:
                    acc_out[c, x] = total
                    continue
                low, high = total[:, :half], total[:, half:]
                kernel_out[c, x] = jnp.where(me_p == 0, low, high)
                ksend[x, c] = jnp.where(me_p == 0, high, low)
            if last:
                pltpu.make_async_remote_copy(
                    src_ref=ksend.at[x], dst_ref=krecv.at[x], send_sem=ks.at[x], recv_sem=kr.at[x],
                    device_id=dev_pair, device_id_type=MESH,
                ).start()
            new_state = [p_new] + a_new
            for c in range(4):
                if last:
                    state_out[c, x] = new_state[c]
                else:
                    fill_state(nxt, x, c, new_state[c])
            return carry

        lax.fori_loop(0, width_x, velocity_slab, 0)

    for x in range(width_x):
        copy = pltpu.make_async_remote_copy(
            src_ref=ksend.at[x], dst_ref=krecv.at[x], send_sem=ks.at[x], recv_sem=kr.at[x],
            device_id=dev_pair, device_id_type=MESH,
        )
        copy.wait_send()
        copy.wait_recv()

    def add_partner(x, carry):
        for c in range(4):
            kernel_out[c, x] = kernel_out[c, x] + krecv[x, c]
        return carry

    lax.fori_loop(0, width_x, add_partner, 0)


def samples_kernel(nx, ny, local_ref, out_ref, sent, got, send_sem, recv_sem):
    me_p = lax.axis_index("pair")
    gx = lax.axis_index("gx")
    gy = lax.axis_index("gy")
    rounds = []
    k = 1
    while k < nx:
        rounds.append((me_p, gx + k - 2 * k * ((gx // k) % 2), gy))
        k *= 2
    k = 1
    while k < ny:
        rounds.append((me_p, gx, gy + k - 2 * k * ((gy // k) % 2)))
        k *= 2
    barrier = pltpu.get_barrier_semaphore()
    for dev in rounds:
        pl.semaphore_signal(barrier, 1, device_id=dev, device_id_type=MESH)
    pl.semaphore_wait(barrier, len(rounds))
    total = local_ref[...]
    for r, dev in enumerate(rounds):
        src = local_ref
        if r > 0:
            sent[r] = total
            src = sent.at[r]
        copy = pltpu.make_async_remote_copy(
            src_ref=src, dst_ref=got.at[r], send_sem=send_sem.at[r], recv_sem=recv_sem.at[r],
            device_id=dev, device_id_type=MESH,
        )
        copy.start()
        copy.wait_send()
        copy.wait_recv()
        total = total + got[r]
    out_ref[...] = total


def gathered_samples(local_samples):
    nx, ny = lax.axis_size("gx"), lax.axis_size("gy")
    rounds = (nx.bit_length() - 1) + (ny.bit_length() - 1)
    if (nx & (nx - 1)) or (ny & (ny - 1)) or rounds == 0:
        return lax.psum(local_samples, ("gx", "gy"))
    vmem = pl.BlockSpec(memory_space=pltpu.VMEM)
    return pl.pallas_call(
        functools.partial(samples_kernel, nx, ny),
        out_shape=jax.ShapeDtypeStruct(local_samples.shape, jnp.float32),
        in_specs=[vmem],
        out_specs=vmem,
        scratch_shapes=[
            pltpu.VMEM((rounds,) + local_samples.shape, jnp.float32),
            pltpu.VMEM((rounds,) + local_samples.shape, jnp.float32),
            pltpu.SemaphoreType.DMA((rounds,)),
            pltpu.SemaphoreType.DMA((rounds,)),
        ],
        compiler_params=pltpu.CompilerParams(collective_id=1, has_side_effects=True),
    )(local_samples)


def shards(
    sound_speed_sq,
    wind_profile,
    forward_field,
    adjoint_state,
    pair_counts,
    source_cells,
    receiver_cells,
    residuals,
):
    steps_total = forward_field.shape[0]
    width_x, width_y, depth = sound_speed_sq.shape
    slots = residuals.shape[0]
    live = (jnp.arange(slots, dtype=jnp.int32) < pair_counts[0]).astype(jnp.float32)
    sx, sy, sz, src_inside = local_cells(source_cells, width_x, width_y)
    rx, ry, rz, rcv_inside = local_cells(receiver_cells, width_x, width_y)
    local_samples = jnp.stack(
        [forward_field[t, 0][sx, sy, sz] for t in range(steps_total)]
    ).astype(jnp.float32) * src_inside[None, :]
    samples = gathered_samples(local_samples)
    amplitude = jnp.transpose(residuals) * samples * (live * rcv_inside)[None, :]
    rcv_flat = (rx * width_y + ry) * depth + rz
    step_index = jnp.broadcast_to(jnp.arange(steps_total)[:, None], amplitude.shape)
    injected = (
        jnp.zeros((steps_total, width_x * width_y * depth), jnp.float32)
        .at[step_index, jnp.broadcast_to(rcv_flat[None, :], amplitude.shape)]
        .add(amplitude)
        .reshape(steps_total, width_x, width_y, depth)
    )
    lo_x, hi_x = neighbours(forward_field, "gx", 2)
    fpad = jnp.concatenate([lo_x, forward_field, hi_x], axis=2)
    up = [(i, i + 1) for i in range(lax.axis_size("gy") - 1)]
    down = [(i + 1, i) for i in range(lax.axis_size("gy") - 1)]
    lo_y = lax.ppermute(forward_field[:, :, :, width_y - 1:width_y, :], "gy", up)
    hi_y = lax.ppermute(forward_field[:, :, :, 0:1, :], "gy", down)
    fyr = jnp.stack([lo_y, hi_y], axis=1)

    vmem = pl.BlockSpec(memory_space=pltpu.VMEM)
    kernel = functools.partial(
        stencil_kernel, lax.axis_size("gx"), lax.axis_size("gy"), steps_total
    )
    state_new, kernels = pl.pallas_call(
        kernel,
        out_shape=(
            jax.ShapeDtypeStruct((4, width_x, width_y, depth), jnp.float32),
            jax.ShapeDtypeStruct((4, width_x, width_y, depth // 2), jnp.float32),
        ),
        in_specs=[vmem] * 6,
        out_specs=(vmem, vmem),
        scratch_shapes=[
            pltpu.VMEM((2, 4, width_x + 2, width_y, depth), jnp.float32),
            pltpu.VMEM((width_x + 2, width_y, depth), jnp.float32),
            pltpu.VMEM((2, 2, 4, width_x, 1, depth), jnp.float32),
            pltpu.VMEM((2, 2, 4, width_x, 1, depth), jnp.float32),
            pltpu.VMEM((2, width_x, 1, depth), jnp.float32),
            pltpu.VMEM((2, width_x, 1, depth), jnp.float32),
            pltpu.VMEM((4, width_x, width_y, depth), jnp.float32),
            pltpu.VMEM((width_x, 4, width_y, depth // 2), jnp.float32),
            pltpu.VMEM((width_x, 4, width_y, depth // 2), jnp.float32),
            pltpu.SemaphoreType.DMA((2, 4)),
            pltpu.SemaphoreType.DMA((2, 4)),
            pltpu.SemaphoreType.DMA((4,)),
            pltpu.SemaphoreType.DMA((4,)),
            pltpu.SemaphoreType.DMA((width_x,)),
            pltpu.SemaphoreType.DMA((width_x,)),
        ],
        compiler_params=pltpu.CompilerParams(
            collective_id=0, has_side_effects=True, vmem_limit_bytes=48 * 1024 * 1024
        ),
    )(adjoint_state[0], sound_speed_sq, wind_profile, fpad, fyr, injected)
    return (kernels, state_new[None])


def solution(mesh):
    in_specs = (
        P("gx", "gy", None),
        P(),
        P(None, None, "gx", "gy", None),
        P("pair", None, "gx", "gy", None),
        P("pair"),
        P("pair", None),
        P("pair", None),
        P("pair", None),
    )
    out_specs = (P(None, "gx", "gy", "pair"), P("pair", None, "gx", "gy", None))
    return jax.shard_map(shards, mesh=mesh, in_specs=in_specs, out_specs=out_specs, check_vma=False)
```

```python
import functools

import jax
import jax.numpy as jnp
from jax import lax
from jax.experimental import pallas as pl
from jax.experimental.pallas import tpu as pltpu
from jax.sharding import PartitionSpec as P

step_length = 0.25
MESH = pl.DeviceIdType.MESH


def neighbours(shard, axis, dim):
    size, length = (lax.axis_size(axis), shard.shape[dim])
    up = [(i, i + 1) for i in range(size - 1)]
    down = [(i + 1, i) for i in range(size - 1)]
    last = lax.slice_in_dim(shard, length - 1, length, axis=dim)
    first = lax.slice_in_dim(shard, 0, 1, axis=dim)
    before = lax.ppermute(last, axis, up)
    after = lax.ppermute(first, axis, down)
    return (before, after)


def local_cells(cells, width_x, width_y):
    local_x = cells[:, 0] - lax.axis_index("gx") * width_x
    local_y = cells[:, 1] - lax.axis_index("gy") * width_y
    inside = (local_x >= 0) & (local_x < width_x) & (local_y >= 0) & (local_y < width_y)
    return (
        jnp.clip(local_x, 0, width_x - 1),
        jnp.clip(local_y, 0, width_y - 1),
        cells[:, 2],
        inside.astype(jnp.float32),
    )


def stencil_kernel(
    nx, ny, steps,
    state_in, sound, wind, fpad, fyr, inj,
    state_out, kernel_out,
    pads, pbuf, ysend, yrecv, ypsend, yprecv, acc_out, ksend, krecv, ss, rs, ps, pr, ks, kr,
):
    _, width_x, width_y, depth = state_in.shape
    me_p = lax.axis_index("pair")
    gx = lax.axis_index("gx")
    gy = lax.axis_index("gy")
    has_lo_x = gx > 0
    has_hi_x = gx < nx - 1
    has_lo_y = gy > 0
    has_hi_y = gy < ny - 1
    dev_lo_x = (me_p, gx - 1, gy)
    dev_hi_x = (me_p, gx + 1, gy)
    dev_lo_y = (me_p, gx, gy - 1)
    dev_hi_y = (me_p, gx, gy + 1)
    dev_pair = (1 - me_p, gx, gy)
    half = depth // 2

    zero_slab = jnp.zeros((width_y, depth), jnp.float32)
    for par in range(2):
        for c in range(4):
            pads[par, c, 0] = zero_slab
            pads[par, c, width_x + 1] = zero_slab
            for side in range(2):
                yrecv[par, side, c] = jnp.zeros((width_x, 1, depth), jnp.float32)
    pbuf[0] = zero_slab
    pbuf[width_x + 1] = zero_slab
    for side in range(2):
        yprecv[side] = jnp.zeros((width_x, 1, depth), jnp.float32)

    barrier = pltpu.get_barrier_semaphore()
    pl.semaphore_signal(barrier, 1, device_id=dev_pair, device_id_type=MESH)
    for cond, dev in ((has_lo_x, dev_lo_x), (has_hi_x, dev_hi_x), (has_lo_y, dev_lo_y), (has_hi_y, dev_hi_y)):
        @pl.when(cond)
        def _():
            pl.semaphore_signal(barrier, 1, device_id=dev, device_id_type=MESH)
    peers = 1 + (
        (gx + nx - 1) // nx + (2 * nx - 2 - gx) // nx
        + (gy + ny - 1) // ny + (2 * ny - 2 - gy) // ny
    )
    pl.semaphore_wait(barrier, peers)

    iy = lax.broadcasted_iota(jnp.int32, (width_y, depth), 0)
    iz = lax.broadcasted_iota(jnp.int32, (width_y, depth), 1)
    we = wind[0:1, :]
    wn = wind[1:2, :]
    wv = wind[2:3, :]

    def dy(v, lo, hi):
        up = jnp.where(iy == width_y - 1, hi, pltpu.roll(v, width_y - 1, 0))
        down = jnp.where(iy == 0, lo, pltpu.roll(v, 1, 0))
        return (up - down) * 0.5

    def dz(v):
        up = jnp.where(iz == depth - 1, 0.0, pltpu.roll(v, depth - 1, 1))
        down = jnp.where(iz == 0, 0.0, pltpu.roll(v, 1, 1))
        return (up - down) * 0.5

    def exchange(src_lo_x, src_hi_x, dst_lo_x, dst_hi_x, src_y_hi, src_y_lo, dst_y_lo, dst_y_hi, send, recv):
        outs = (
            (has_hi_x, src_hi_x, dst_lo_x, 0, dev_hi_x),
            (has_lo_x, src_lo_x, dst_hi_x, 1, dev_lo_x),
            (has_hi_y, src_y_hi, dst_y_lo, 2, dev_hi_y),
            (has_lo_y, src_y_lo, dst_y_hi, 3, dev_lo_y),
        )
        copies = []
        for cond, src, dst, slot, dev in outs:
            copy = pltpu.make_async_remote_copy(
                src_ref=src, dst_ref=dst, send_sem=send.at[slot], recv_sem=recv.at[slot],
                device_id=dev, device_id_type=MESH,
            )
            copies.append((cond, copy))

            @pl.when(cond)
            def _():
                copy.start()
        incoming = (has_lo_x, has_hi_x, has_lo_y, has_hi_y)
        for (cond, copy), arrives in zip(copies, incoming):
            @pl.when(cond)
            def _():
                copy.wait_send()

            @pl.when(arrives)
            def _():
                copy.wait_recv()

    def fill_state(par, x, c, v):
        pads[par, c, x + 1] = v
        ysend[par, 0, c, x] = v[width_y - 1:width_y, :]
        ysend[par, 1, c, x] = v[0:1, :]

    def copy_in(x, carry):
        for c in range(4):
            fill_state(0, x, c, state_in[c, x])
        return carry

    lax.fori_loop(0, width_x, copy_in, 0)

    for step in range(steps):
        par = step % 2
        nxt = 1 - par
        snap = steps - 1 - step
        last = step == steps - 1
        exchange(
            pads.at[par, :, pl.ds(1, 1)], pads.at[par, :, pl.ds(width_x, 1)],
            pads.at[par, :, pl.ds(0, 1)], pads.at[par, :, pl.ds(width_x + 1, 1)],
            ysend.at[par, 0], ysend.at[par, 1], yrecv.at[par, 0], yrecv.at[par, 1],
            ss.at[par], rs.at[par],
        )

        def pressure_slab(x, carry, par=par, snap=snap):
            xp = x + 1
            old = pads.at[par]
            p = old[0, xp]
            dxp = (old[0, xp + 1] - old[0, x]) * 0.5
            dxa = (old[1, xp + 1] - old[1, x]) * 0.5
            dyp = dy(p, yrecv[par, 0, 0, x], yrecv[par, 1, 0, x])
            dya = dy(old[2, xp], yrecv[par, 0, 2, x], yrecv[par, 1, 2, x])
            dzp = dz(p)
            dza = dz(old[3, xp])
            divergence = dxa + dya + dza
            p_new = (
                p
                + step_length * (sound[x] * divergence + we * dxp + wn * dyp + wv * dzp)
                + inj[snap, x]
            )
            pbuf[xp] = p_new
            ypsend[0, x] = p_new[width_y - 1:width_y, :]
            ypsend[1, x] = p_new[0:1, :]
            return carry

        lax.fori_loop(0, width_x, pressure_slab, 0)
        exchange(
            pbuf.at[pl.ds(1, 1)], pbuf.at[pl.ds(width_x, 1)],
            pbuf.at[pl.ds(0, 1)], pbuf.at[pl.ds(width_x + 1, 1)],
            ypsend.at[0], ypsend.at[1], yprecv.at[0], yprecv.at[1],
            ps, pr,
        )

        def velocity_slab(x, carry, par=par, nxt=nxt, snap=snap, last=last, step=step):
            xp = x + 1
            old = pads.at[par]
            p_new = pbuf[xp]
            grad = (
                (pbuf[xp + 1] - pbuf[x]) * 0.5,
                dy(p_new, yprecv[0, x], yprecv[1, x]),
                dz(p_new),
            )
            a_new = []
            for i in range(3):
                a = old[1 + i, xp]
                dxa = (old[1 + i, xp + 1] - old[1 + i, x]) * 0.5
                dya = dy(a, yrecv[par, 0, 1 + i, x], yrecv[par, 1, 1 + i, x])
                dza = dz(a)
                a_new.append(a + step_length * (grad[i] + we * dxa + wn * dya + wv * dza))
            fe, fn, fu = [], [], []
            for c in range(4):
                f = fpad[snap, c, xp].astype(jnp.float32)
                fe.append((fpad[snap, c, xp + 1].astype(jnp.float32) - fpad[snap, c, x].astype(jnp.float32)) * 0.5)
                fn.append(dy(f, fyr[snap, 0, c, x].astype(jnp.float32), fyr[snap, 1, c, x].astype(jnp.float32)))
                fu.append(dz(f))
            pieces = [p_new * (fe[1] + fn[2] + fu[3])]
            for along in (fe, fn, fu):
                pieces.append(p_new * along[0] + a_new[0] * along[1] + a_new[1] * along[2] + a_new[2] * along[3])
            for c in range(4):
                total = pieces[c] if step == 0 else acc_out[c, x] + pieces[c]
                if not last:
                    acc_out[c, x] = total
                    continue
                low, high = total[:, :half], total[:, half:]
                kernel_out[c, x] = jnp.where(me_p == 0, low, high)
                ksend[x, c] = jnp.where(me_p == 0, high, low)
            if last:
                pltpu.make_async_remote_copy(
                    src_ref=ksend.at[x], dst_ref=krecv.at[x], send_sem=ks.at[x], recv_sem=kr.at[x],
                    device_id=dev_pair, device_id_type=MESH,
                ).start()
            new_state = [p_new] + a_new
            for c in range(4):
                if last:
                    state_out[c, x] = new_state[c]
                else:
                    fill_state(nxt, x, c, new_state[c])
            return carry

        lax.fori_loop(0, width_x, velocity_slab, 0)

    for x in range(width_x):
        copy = pltpu.make_async_remote_copy(
            src_ref=ksend.at[x], dst_ref=krecv.at[x], send_sem=ks.at[x], recv_sem=kr.at[x],
            device_id=dev_pair, device_id_type=MESH,
        )
        copy.wait_send()
        copy.wait_recv()

    def add_partner(x, carry):
        for c in range(4):
            kernel_out[c, x] = kernel_out[c, x] + krecv[x, c]
        return carry

    lax.fori_loop(0, width_x, add_partner, 0)


def samples_kernel(nx, ny, local_ref, out_ref, sent, got, send_sem, recv_sem):
    me_p = lax.axis_index("pair")
    gx = lax.axis_index("gx")
    gy = lax.axis_index("gy")
    rounds = []
    k = 1
    while k < nx:
        rounds.append((me_p, gx + k - 2 * k * ((gx // k) % 2), gy))
        k *= 2
    k = 1
    while k < ny:
        rounds.append((me_p, gx, gy + k - 2 * k * ((gy // k) % 2)))
        k *= 2
    barrier = pltpu.get_barrier_semaphore()
    for dev in rounds:
        pl.semaphore_signal(barrier, 1, device_id=dev, device_id_type=MESH)
    pl.semaphore_wait(barrier, len(rounds))
    total = local_ref[...]
    for r, dev in enumerate(rounds):
        src = local_ref
        if r > 0:
            sent[r] = total
            src = sent.at[r]
        copy = pltpu.make_async_remote_copy(
            src_ref=src, dst_ref=got.at[r], send_sem=send_sem.at[r], recv_sem=recv_sem.at[r],
            device_id=dev, device_id_type=MESH,
        )
        copy.start()
        copy.wait_send()
        copy.wait_recv()
        total = total + got[r]
    out_ref[...] = total


def gathered_samples(local_samples):
    nx, ny = lax.axis_size("gx"), lax.axis_size("gy")
    rounds = (nx.bit_length() - 1) + (ny.bit_length() - 1)
    if (nx & (nx - 1)) or (ny & (ny - 1)) or rounds == 0:
        return lax.psum(local_samples, ("gx", "gy"))
    vmem = pl.BlockSpec(memory_space=pltpu.VMEM)
    return pl.pallas_call(
        functools.partial(samples_kernel, nx, ny),
        out_shape=jax.ShapeDtypeStruct(local_samples.shape, jnp.float32),
        in_specs=[vmem],
        out_specs=vmem,
        scratch_shapes=[
            pltpu.VMEM((rounds,) + local_samples.shape, jnp.float32),
            pltpu.VMEM((rounds,) + local_samples.shape, jnp.float32),
            pltpu.SemaphoreType.DMA((rounds,)),
            pltpu.SemaphoreType.DMA((rounds,)),
        ],
        compiler_params=pltpu.CompilerParams(collective_id=1, has_side_effects=True),
    )(local_samples)


def shards(
    sound_speed_sq,
    wind_profile,
    forward_field,
    adjoint_state,
    pair_counts,
    source_cells,
    receiver_cells,
    residuals,
):
    steps_total = forward_field.shape[0]
    width_x, width_y, depth = sound_speed_sq.shape
    slots = residuals.shape[0]
    live = (jnp.arange(slots, dtype=jnp.int32) < pair_counts[0]).astype(jnp.float32)
    gx_first = lax.axis_index("gx") * width_x
    gy_first = lax.axis_index("gy") * width_y
    x_range = jnp.arange(width_x, dtype=jnp.int32)
    y_range = jnp.arange(width_y, dtype=jnp.int32)
    z_range = jnp.arange(depth, dtype=jnp.int32)

    def tile_mask(cells):
        on_x = (cells[:, 0][None, :] - gx_first) == x_range[:, None]
        on_y = (cells[:, 1][None, :] - gy_first) == y_range[:, None]
        return (on_x[:, None, :] & on_y[None, :, :]).astype(jnp.float32)

    source_z = (source_cells[:, 2][None, :] == z_range[:, None]).astype(jnp.bfloat16)
    along_z = jnp.einsum(
        "txyz,zn->txyn", forward_field[:, 0], source_z, preferred_element_type=jnp.float32
    )
    local_samples = jnp.sum(along_z * tile_mask(source_cells)[None], axis=(1, 2))
    samples = gathered_samples(local_samples)
    amplitude = jnp.transpose(residuals) * samples * live[None, :]
    spread = amplitude[:, None, None, :] * tile_mask(receiver_cells)[None]
    receiver_z = (receiver_cells[:, 2][:, None] == z_range[None, :]).astype(jnp.float32)
    injected = jnp.einsum(
        "txyn,nz->txyz", spread, receiver_z, precision=lax.Precision.HIGHEST,
        preferred_element_type=jnp.float32,
    )
    lo_x, hi_x = neighbours(forward_field, "gx", 2)
    fpad = jnp.concatenate([lo_x, forward_field, hi_x], axis=2)
    up = [(i, i + 1) for i in range(lax.axis_size("gy") - 1)]
    down = [(i + 1, i) for i in range(lax.axis_size("gy") - 1)]
    lo_y = lax.ppermute(forward_field[:, :, :, width_y - 1:width_y, :], "gy", up)
    hi_y = lax.ppermute(forward_field[:, :, :, 0:1, :], "gy", down)
    fyr = jnp.stack([lo_y, hi_y], axis=1)

    vmem = pl.BlockSpec(memory_space=pltpu.VMEM)
    kernel = functools.partial(
        stencil_kernel, lax.axis_size("gx"), lax.axis_size("gy"), steps_total
    )
    state_new, kernels = pl.pallas_call(
        kernel,
        out_shape=(
            jax.ShapeDtypeStruct((4, width_x, width_y, depth), jnp.float32),
            jax.ShapeDtypeStruct((4, width_x, width_y, depth // 2), jnp.float32),
        ),
        in_specs=[vmem] * 6,
        out_specs=(vmem, vmem),
        scratch_shapes=[
            pltpu.VMEM((2, 4, width_x + 2, width_y, depth), jnp.float32),
            pltpu.VMEM((width_x + 2, width_y, depth), jnp.float32),
            pltpu.VMEM((2, 2, 4, width_x, 1, depth), jnp.float32),
            pltpu.VMEM((2, 2, 4, width_x, 1, depth), jnp.float32),
            pltpu.VMEM((2, width_x, 1, depth), jnp.float32),
            pltpu.VMEM((2, width_x, 1, depth), jnp.float32),
            pltpu.VMEM((4, width_x, width_y, depth), jnp.float32),
            pltpu.VMEM((width_x, 4, width_y, depth // 2), jnp.float32),
            pltpu.VMEM((width_x, 4, width_y, depth // 2), jnp.float32),
            pltpu.SemaphoreType.DMA((2, 4)),
            pltpu.SemaphoreType.DMA((2, 4)),
            pltpu.SemaphoreType.DMA((4,)),
            pltpu.SemaphoreType.DMA((4,)),
            pltpu.SemaphoreType.DMA((width_x,)),
            pltpu.SemaphoreType.DMA((width_x,)),
        ],
        compiler_params=pltpu.CompilerParams(
            collective_id=0, has_side_effects=True, vmem_limit_bytes=48 * 1024 * 1024
        ),
    )(adjoint_state[0], sound_speed_sq, wind_profile, fpad, fyr, injected)
    return (kernels, state_new[None])


def solution(mesh):
    in_specs = (
        P("gx", "gy", None),
        P(),
        P(None, None, "gx", "gy", None),
        P("pair", None, "gx", "gy", None),
        P("pair"),
        P("pair", None),
        P("pair", None),
        P("pair", None),
    )
    out_specs = (P(None, "gx", "gy", "pair"), P("pair", None, "gx", "gy", None))
    return jax.shard_map(shards, mesh=mesh, in_specs=in_specs, out_specs=out_specs, check_vma=False)
```

```python
import functools

import jax
import jax.numpy as jnp
from jax import lax
from jax.experimental import pallas as pl
from jax.experimental.pallas import tpu as pltpu
from jax.sharding import PartitionSpec as P

step_length = 0.25
MESH = pl.DeviceIdType.MESH


def neighbours(shard, axis, dim):
    size, length = (lax.axis_size(axis), shard.shape[dim])
    up = [(i, i + 1) for i in range(size - 1)]
    down = [(i + 1, i) for i in range(size - 1)]
    last = lax.slice_in_dim(shard, length - 1, length, axis=dim)
    first = lax.slice_in_dim(shard, 0, 1, axis=dim)
    before = lax.ppermute(last, axis, up)
    after = lax.ppermute(first, axis, down)
    return (before, after)


def local_cells(cells, width_x, width_y):
    local_x = cells[:, 0] - lax.axis_index("gx") * width_x
    local_y = cells[:, 1] - lax.axis_index("gy") * width_y
    inside = (local_x >= 0) & (local_x < width_x) & (local_y >= 0) & (local_y < width_y)
    return (
        jnp.clip(local_x, 0, width_x - 1),
        jnp.clip(local_y, 0, width_y - 1),
        cells[:, 2],
        inside.astype(jnp.float32),
    )


def stencil_kernel(
    nx, ny, steps,
    state_in, sound, wind, fpad, fyr, inj,
    state_out, kernel_out,
    pads, pbuf, ysend, yrecv, ypsend, yprecv, acc_out, ksend, krecv, ss, rs, ps, pr, ks, kr,
):
    _, width_x, width_y, depth = state_in.shape
    me_p = lax.axis_index("pair")
    gx = lax.axis_index("gx")
    gy = lax.axis_index("gy")
    has_lo_x = gx > 0
    has_hi_x = gx < nx - 1
    has_lo_y = gy > 0
    has_hi_y = gy < ny - 1
    dev_lo_x = (me_p, gx - 1, gy)
    dev_hi_x = (me_p, gx + 1, gy)
    dev_lo_y = (me_p, gx, gy - 1)
    dev_hi_y = (me_p, gx, gy + 1)
    dev_pair = (1 - me_p, gx, gy)
    half = depth // 2

    zero_slab = jnp.zeros((width_y, depth), jnp.float32)
    for par in range(2):
        for c in range(4):
            pads[par, c, 0] = zero_slab
            pads[par, c, width_x + 1] = zero_slab
            for side in range(2):
                yrecv[par, side, c] = jnp.zeros((width_x, 1, depth), jnp.float32)
    pbuf[0] = zero_slab
    pbuf[width_x + 1] = zero_slab
    for side in range(2):
        yprecv[side] = jnp.zeros((width_x, 1, depth), jnp.float32)

    barrier = pltpu.get_barrier_semaphore()
    pl.semaphore_signal(barrier, 1, device_id=dev_pair, device_id_type=MESH)
    for cond, dev in ((has_lo_x, dev_lo_x), (has_hi_x, dev_hi_x), (has_lo_y, dev_lo_y), (has_hi_y, dev_hi_y)):
        @pl.when(cond)
        def _():
            pl.semaphore_signal(barrier, 1, device_id=dev, device_id_type=MESH)
    peers = 1 + (
        (gx + nx - 1) // nx + (2 * nx - 2 - gx) // nx
        + (gy + ny - 1) // ny + (2 * ny - 2 - gy) // ny
    )
    pl.semaphore_wait(barrier, peers)

    iy = lax.broadcasted_iota(jnp.int32, (width_y, depth), 0)
    iz = lax.broadcasted_iota(jnp.int32, (width_y, depth), 1)
    we = wind[0:1, :]
    wn = wind[1:2, :]
    wv = wind[2:3, :]

    def dy(v, lo, hi):
        up = jnp.where(iy == width_y - 1, hi, pltpu.roll(v, width_y - 1, 0))
        down = jnp.where(iy == 0, lo, pltpu.roll(v, 1, 0))
        return (up - down) * 0.5

    def dz(v):
        up = jnp.where(iz == depth - 1, 0.0, pltpu.roll(v, depth - 1, 1))
        down = jnp.where(iz == 0, 0.0, pltpu.roll(v, 1, 1))
        return (up - down) * 0.5

    def exchange(src_lo_x, src_hi_x, dst_lo_x, dst_hi_x, src_y_hi, src_y_lo, dst_y_lo, dst_y_hi, send, recv):
        outs = (
            (has_hi_x, src_hi_x, dst_lo_x, 0, dev_hi_x),
            (has_lo_x, src_lo_x, dst_hi_x, 1, dev_lo_x),
            (has_hi_y, src_y_hi, dst_y_lo, 2, dev_hi_y),
            (has_lo_y, src_y_lo, dst_y_hi, 3, dev_lo_y),
        )
        copies = []
        for cond, src, dst, slot, dev in outs:
            copy = pltpu.make_async_remote_copy(
                src_ref=src, dst_ref=dst, send_sem=send.at[slot], recv_sem=recv.at[slot],
                device_id=dev, device_id_type=MESH,
            )
            copies.append((cond, copy))

            @pl.when(cond)
            def _():
                copy.start()
        incoming = (has_lo_x, has_hi_x, has_lo_y, has_hi_y)
        for (cond, copy), arrives in zip(copies, incoming):
            @pl.when(cond)
            def _():
                copy.wait_send()

            @pl.when(arrives)
            def _():
                copy.wait_recv()

    def fill_state(par, x, c, v):
        pads[par, c, x + 1] = v
        ysend[par, 0, c, x] = v[width_y - 1:width_y, :]
        ysend[par, 1, c, x] = v[0:1, :]

    def copy_in(x, carry):
        for c in range(4):
            fill_state(0, x, c, state_in[c, x])
        return carry

    lax.fori_loop(0, width_x, copy_in, 0)

    for step in range(steps):
        par = step % 2
        nxt = 1 - par
        snap = steps - 1 - step
        last = step == steps - 1
        exchange(
            pads.at[par, :, pl.ds(1, 1)], pads.at[par, :, pl.ds(width_x, 1)],
            pads.at[par, :, pl.ds(0, 1)], pads.at[par, :, pl.ds(width_x + 1, 1)],
            ysend.at[par, 0], ysend.at[par, 1], yrecv.at[par, 0], yrecv.at[par, 1],
            ss.at[par], rs.at[par],
        )

        def pressure_slab(x, carry, par=par, snap=snap):
            xp = x + 1
            old = pads.at[par]
            p = old[0, xp]
            dxp = (old[0, xp + 1] - old[0, x]) * 0.5
            dxa = (old[1, xp + 1] - old[1, x]) * 0.5
            dyp = dy(p, yrecv[par, 0, 0, x], yrecv[par, 1, 0, x])
            dya = dy(old[2, xp], yrecv[par, 0, 2, x], yrecv[par, 1, 2, x])
            dzp = dz(p)
            dza = dz(old[3, xp])
            divergence = dxa + dya + dza
            p_new = (
                p
                + step_length * (sound[x] * divergence + we * dxp + wn * dyp + wv * dzp)
                + inj[snap, x]
            )
            pbuf[xp] = p_new
            ypsend[0, x] = p_new[width_y - 1:width_y, :]
            ypsend[1, x] = p_new[0:1, :]
            return carry

        lax.fori_loop(0, width_x, pressure_slab, 0)
        exchange(
            pbuf.at[pl.ds(1, 1)], pbuf.at[pl.ds(width_x, 1)],
            pbuf.at[pl.ds(0, 1)], pbuf.at[pl.ds(width_x + 1, 1)],
            ypsend.at[0], ypsend.at[1], yprecv.at[0], yprecv.at[1],
            ps, pr,
        )

        def velocity_slab(x, carry, par=par, nxt=nxt, snap=snap, last=last, step=step):
            xp = x + 1
            old = pads.at[par]
            p_new = pbuf[xp]
            grad = (
                (pbuf[xp + 1] - pbuf[x]) * 0.5,
                dy(p_new, yprecv[0, x], yprecv[1, x]),
                dz(p_new),
            )
            a_new = []
            for i in range(3):
                a = old[1 + i, xp]
                dxa = (old[1 + i, xp + 1] - old[1 + i, x]) * 0.5
                dya = dy(a, yrecv[par, 0, 1 + i, x], yrecv[par, 1, 1 + i, x])
                dza = dz(a)
                a_new.append(a + step_length * (grad[i] + we * dxa + wn * dya + wv * dza))
            fe, fn, fu = [], [], []
            for c in range(4):
                f = fpad[snap, c, xp].astype(jnp.float32)
                fe.append((fpad[snap, c, xp + 1].astype(jnp.float32) - fpad[snap, c, x].astype(jnp.float32)) * 0.5)
                fn.append(dy(f, fyr[snap, 0, c, x].astype(jnp.float32), fyr[snap, 1, c, x].astype(jnp.float32)))
                fu.append(dz(f))
            pieces = [p_new * (fe[1] + fn[2] + fu[3])]
            for along in (fe, fn, fu):
                pieces.append(p_new * along[0] + a_new[0] * along[1] + a_new[1] * along[2] + a_new[2] * along[3])
            for c in range(4):
                total = pieces[c] if step == 0 else acc_out[c, x] + pieces[c]
                if not last:
                    acc_out[c, x] = total
                    continue
                low, high = total[:, :half], total[:, half:]
                kernel_out[c, x] = jnp.where(me_p == 0, low, high)
                ksend[x, c] = jnp.where(me_p == 0, high, low)
            if last:
                pltpu.make_async_remote_copy(
                    src_ref=ksend.at[x], dst_ref=krecv.at[x], send_sem=ks.at[x], recv_sem=kr.at[x],
                    device_id=dev_pair, device_id_type=MESH,
                ).start()
            new_state = [p_new] + a_new
            for c in range(4):
                if last:
                    state_out[c, x] = new_state[c]
                else:
                    fill_state(nxt, x, c, new_state[c])
            return carry

        lax.fori_loop(0, width_x, velocity_slab, 0)

    for x in range(width_x):
        copy = pltpu.make_async_remote_copy(
            src_ref=ksend.at[x], dst_ref=krecv.at[x], send_sem=ks.at[x], recv_sem=kr.at[x],
            device_id=dev_pair, device_id_type=MESH,
        )
        copy.wait_send()
        copy.wait_recv()

    def add_partner(x, carry):
        for c in range(4):
            kernel_out[c, x] = kernel_out[c, x] + krecv[x, c]
        return carry

    lax.fori_loop(0, width_x, add_partner, 0)


def samples_kernel(nx, ny, local_ref, out_ref, sent, got_x, got_y, send_sem, recv_sem):
    me_p = lax.axis_index("pair")
    gx = lax.axis_index("gx")
    gy = lax.axis_index("gy")
    peers_x = [(me_p, (gx + d) % nx, gy) for d in range(1, nx)]
    peers_y = [(me_p, gx, (gy + d) % ny) for d in range(1, ny)]
    barrier = pltpu.get_barrier_semaphore()
    for dev in peers_x + peers_y:
        pl.semaphore_signal(barrier, 1, device_id=dev, device_id_type=MESH)
    pl.semaphore_wait(barrier, len(peers_x) + len(peers_y))
    rounds = ((local_ref, got_x, peers_x, 0), (sent, got_y, peers_y, nx - 1))
    total = local_ref[...]
    for src, got, peers, base in rounds:
        copies = []
        for i, dev in enumerate(peers):
            copy = pltpu.make_async_remote_copy(
                src_ref=src, dst_ref=got.at[i], send_sem=send_sem.at[base + i],
                recv_sem=recv_sem.at[base + i], device_id=dev, device_id_type=MESH,
            )
            copy.start()
            copies.append(copy)
        for copy in copies:
            copy.wait_send()
            copy.wait_recv()
        for i in range(len(peers)):
            total = total + got[i]
        if base == 0:
            sent[...] = total
    out_ref[...] = total


def gathered_samples(local_samples):
    nx, ny = lax.axis_size("gx"), lax.axis_size("gy")
    if nx < 2 or ny < 2:
        return lax.psum(local_samples, ("gx", "gy"))
    vmem = pl.BlockSpec(memory_space=pltpu.VMEM)
    return pl.pallas_call(
        functools.partial(samples_kernel, nx, ny),
        out_shape=jax.ShapeDtypeStruct(local_samples.shape, jnp.float32),
        in_specs=[vmem],
        out_specs=vmem,
        scratch_shapes=[
            pltpu.VMEM(local_samples.shape, jnp.float32),
            pltpu.VMEM((nx - 1,) + local_samples.shape, jnp.float32),
            pltpu.VMEM((ny - 1,) + local_samples.shape, jnp.float32),
            pltpu.SemaphoreType.DMA((nx + ny - 2,)),
            pltpu.SemaphoreType.DMA((nx + ny - 2,)),
        ],
        compiler_params=pltpu.CompilerParams(collective_id=1, has_side_effects=True),
    )(local_samples)


def shards(
    sound_speed_sq,
    wind_profile,
    forward_field,
    adjoint_state,
    pair_counts,
    source_cells,
    receiver_cells,
    residuals,
):
    steps_total = forward_field.shape[0]
    width_x, width_y, depth = sound_speed_sq.shape
    slots = residuals.shape[0]
    live = (jnp.arange(slots, dtype=jnp.int32) < pair_counts[0]).astype(jnp.float32)
    gx_first = lax.axis_index("gx") * width_x
    gy_first = lax.axis_index("gy") * width_y
    x_range = jnp.arange(width_x, dtype=jnp.int32)
    y_range = jnp.arange(width_y, dtype=jnp.int32)
    z_range = jnp.arange(depth, dtype=jnp.int32)

    def tile_mask(cells):
        on_x = (cells[:, 0][None, :] - gx_first) == x_range[:, None]
        on_y = (cells[:, 1][None, :] - gy_first) == y_range[:, None]
        return (on_x[:, None, :] & on_y[None, :, :]).astype(jnp.float32)

    source_z = (source_cells[:, 2][None, :] == z_range[:, None]).astype(jnp.bfloat16)
    along_z = jnp.einsum(
        "txyz,zn->txyn", forward_field[:, 0], source_z, preferred_element_type=jnp.float32
    )
    local_samples = jnp.sum(along_z * tile_mask(source_cells)[None], axis=(1, 2))
    samples = gathered_samples(local_samples)
    amplitude = jnp.transpose(residuals) * samples * live[None, :]
    spread = amplitude[:, None, None, :] * tile_mask(receiver_cells)[None]
    receiver_z = (receiver_cells[:, 2][:, None] == z_range[None, :]).astype(jnp.float32)
    injected = jnp.einsum(
        "txyn,nz->txyz", spread, receiver_z, precision=lax.Precision.HIGHEST,
        preferred_element_type=jnp.float32,
    )
    lo_x, hi_x = neighbours(forward_field, "gx", 2)
    fpad = jnp.concatenate([lo_x, forward_field, hi_x], axis=2)
    up = [(i, i + 1) for i in range(lax.axis_size("gy") - 1)]
    down = [(i + 1, i) for i in range(lax.axis_size("gy") - 1)]
    lo_y = lax.ppermute(forward_field[:, :, :, width_y - 1:width_y, :], "gy", up)
    hi_y = lax.ppermute(forward_field[:, :, :, 0:1, :], "gy", down)
    fyr = jnp.stack([lo_y, hi_y], axis=1)

    vmem = pl.BlockSpec(memory_space=pltpu.VMEM)
    kernel = functools.partial(
        stencil_kernel, lax.axis_size("gx"), lax.axis_size("gy"), steps_total
    )
    state_new, kernels = pl.pallas_call(
        kernel,
        out_shape=(
            jax.ShapeDtypeStruct((4, width_x, width_y, depth), jnp.float32),
            jax.ShapeDtypeStruct((4, width_x, width_y, depth // 2), jnp.float32),
        ),
        in_specs=[vmem] * 6,
        out_specs=(vmem, vmem),
        scratch_shapes=[
            pltpu.VMEM((2, 4, width_x + 2, width_y, depth), jnp.float32),
            pltpu.VMEM((width_x + 2, width_y, depth), jnp.float32),
            pltpu.VMEM((2, 2, 4, width_x, 1, depth), jnp.float32),
            pltpu.VMEM((2, 2, 4, width_x, 1, depth), jnp.float32),
            pltpu.VMEM((2, width_x, 1, depth), jnp.float32),
            pltpu.VMEM((2, width_x, 1, depth), jnp.float32),
            pltpu.VMEM((4, width_x, width_y, depth), jnp.float32),
            pltpu.VMEM((width_x, 4, width_y, depth // 2), jnp.float32),
            pltpu.VMEM((width_x, 4, width_y, depth // 2), jnp.float32),
            pltpu.SemaphoreType.DMA((2, 4)),
            pltpu.SemaphoreType.DMA((2, 4)),
            pltpu.SemaphoreType.DMA((4,)),
            pltpu.SemaphoreType.DMA((4,)),
            pltpu.SemaphoreType.DMA((width_x,)),
            pltpu.SemaphoreType.DMA((width_x,)),
        ],
        compiler_params=pltpu.CompilerParams(
            collective_id=0, has_side_effects=True, vmem_limit_bytes=48 * 1024 * 1024
        ),
    )(adjoint_state[0], sound_speed_sq, wind_profile, fpad, fyr, injected)
    return (kernels, state_new[None])


def solution(mesh):
    in_specs = (
        P("gx", "gy", None),
        P(),
        P(None, None, "gx", "gy", None),
        P("pair", None, "gx", "gy", None),
        P("pair"),
        P("pair", None),
        P("pair", None),
        P("pair", None),
    )
    out_specs = (P(None, "gx", "gy", "pair"), P("pair", None, "gx", "gy", None))
    return jax.shard_map(shards, mesh=mesh, in_specs=in_specs, out_specs=out_specs, check_vma=False)
```

```python
import functools

import jax
import jax.numpy as jnp
from jax import lax
from jax.experimental import pallas as pl
from jax.experimental.pallas import tpu as pltpu
from jax.sharding import PartitionSpec as P

step_length = 0.25
MESH = pl.DeviceIdType.MESH


def neighbours(shard, axis, dim):
    size, length = (lax.axis_size(axis), shard.shape[dim])
    up = [(i, i + 1) for i in range(size - 1)]
    down = [(i + 1, i) for i in range(size - 1)]
    last = lax.slice_in_dim(shard, length - 1, length, axis=dim)
    first = lax.slice_in_dim(shard, 0, 1, axis=dim)
    before = lax.ppermute(last, axis, up)
    after = lax.ppermute(first, axis, down)
    return (before, after)


def local_cells(cells, width_x, width_y):
    local_x = cells[:, 0] - lax.axis_index("gx") * width_x
    local_y = cells[:, 1] - lax.axis_index("gy") * width_y
    inside = (local_x >= 0) & (local_x < width_x) & (local_y >= 0) & (local_y < width_y)
    return (
        jnp.clip(local_x, 0, width_x - 1),
        jnp.clip(local_y, 0, width_y - 1),
        cells[:, 2],
        inside.astype(jnp.float32),
    )


def stencil_kernel(
    nx, ny, steps,
    state_in, sound, wind, forward, inj,
    state_out, kernel_out,
    pads, pbuf, ysend, yrecv, ypsend, yprecv, acc_out, ksend, krecv, fpad, fysend, fyr,
    ss, rs, ps, pr, ks, kr, fs, fr, local_sem,
):
    _, width_x, width_y, depth = state_in.shape
    me_p = lax.axis_index("pair")
    gx = lax.axis_index("gx")
    gy = lax.axis_index("gy")
    has_lo_x = gx > 0
    has_hi_x = gx < nx - 1
    has_lo_y = gy > 0
    has_hi_y = gy < ny - 1
    dev_lo_x = (me_p, gx - 1, gy)
    dev_hi_x = (me_p, gx + 1, gy)
    dev_lo_y = (me_p, gx, gy - 1)
    dev_hi_y = (me_p, gx, gy + 1)
    dev_pair = (1 - me_p, gx, gy)
    half = depth // 2

    zero_slab = jnp.zeros((width_y, depth), jnp.float32)
    for par in range(2):
        for c in range(4):
            pads[par, c, 0] = zero_slab
            pads[par, c, width_x + 1] = zero_slab
            for side in range(2):
                yrecv[par, side, c] = jnp.zeros((width_x, 1, depth), jnp.float32)
    pbuf[0] = zero_slab
    pbuf[width_x + 1] = zero_slab
    zero_forward = jnp.zeros((width_y, depth), fpad.dtype)
    for t in range(steps):
        for c in range(4):
            fpad[t, c, 0] = zero_forward
            fpad[t, c, width_x + 1] = zero_forward
            for side in range(2):
                fyr[side, t, c] = jnp.zeros((width_x, 1, depth), jnp.float32)

    def forward_rows(x, carry):
        for t in range(steps):
            for c in range(4):
                f = forward[t, c, x].astype(jnp.float32)
                fysend[0, t, c, x] = f[width_y - 1:width_y, :]
                fysend[1, t, c, x] = f[0:1, :]
        return carry

    lax.fori_loop(0, width_x, forward_rows, 0)
    interior = pltpu.make_async_copy(forward, fpad.at[:, :, pl.ds(1, width_x)], local_sem.at[0])
    interior.start()
    for side in range(2):
        yprecv[side] = jnp.zeros((width_x, 1, depth), jnp.float32)

    barrier = pltpu.get_barrier_semaphore()
    pl.semaphore_signal(barrier, 1, device_id=dev_pair, device_id_type=MESH)
    for cond, dev in ((has_lo_x, dev_lo_x), (has_hi_x, dev_hi_x), (has_lo_y, dev_lo_y), (has_hi_y, dev_hi_y)):
        @pl.when(cond)
        def _():
            pl.semaphore_signal(barrier, 1, device_id=dev, device_id_type=MESH)
    peers = 1 + (
        (gx + nx - 1) // nx + (2 * nx - 2 - gx) // nx
        + (gy + ny - 1) // ny + (2 * ny - 2 - gy) // ny
    )
    pl.semaphore_wait(barrier, peers)

    iy = lax.broadcasted_iota(jnp.int32, (width_y, depth), 0)
    iz = lax.broadcasted_iota(jnp.int32, (width_y, depth), 1)
    we = wind[0:1, :]
    wn = wind[1:2, :]
    wv = wind[2:3, :]

    def dy(v, lo, hi):
        up = jnp.where(iy == width_y - 1, hi, pltpu.roll(v, width_y - 1, 0))
        down = jnp.where(iy == 0, lo, pltpu.roll(v, 1, 0))
        return (up - down) * 0.5

    def dz(v):
        up = jnp.where(iz == depth - 1, 0.0, pltpu.roll(v, depth - 1, 1))
        down = jnp.where(iz == 0, 0.0, pltpu.roll(v, 1, 1))
        return (up - down) * 0.5

    def exchange(src_lo_x, src_hi_x, dst_lo_x, dst_hi_x, src_y_hi, src_y_lo, dst_y_lo, dst_y_hi, send, recv):
        outs = (
            (has_hi_x, src_hi_x, dst_lo_x, 0, dev_hi_x),
            (has_lo_x, src_lo_x, dst_hi_x, 1, dev_lo_x),
            (has_hi_y, src_y_hi, dst_y_lo, 2, dev_hi_y),
            (has_lo_y, src_y_lo, dst_y_hi, 3, dev_lo_y),
        )
        copies = []
        for cond, src, dst, slot, dev in outs:
            copy = pltpu.make_async_remote_copy(
                src_ref=src, dst_ref=dst, send_sem=send.at[slot], recv_sem=recv.at[slot],
                device_id=dev, device_id_type=MESH,
            )
            copies.append((cond, copy))

            @pl.when(cond)
            def _():
                copy.start()
        incoming = (has_lo_x, has_hi_x, has_lo_y, has_hi_y)
        for (cond, copy), arrives in zip(copies, incoming):
            @pl.when(cond)
            def _():
                copy.wait_send()

            @pl.when(arrives)
            def _():
                copy.wait_recv()

    forward_copies = []
    for cond, src, dst, slot, dev in (
        (has_hi_x, forward.at[:, :, pl.ds(width_x - 1, 1)], fpad.at[:, :, pl.ds(0, 1)], 0, dev_hi_x),
        (has_lo_x, forward.at[:, :, pl.ds(0, 1)], fpad.at[:, :, pl.ds(width_x + 1, 1)], 1, dev_lo_x),
        (has_hi_y, fysend.at[0], fyr.at[0], 2, dev_hi_y),
        (has_lo_y, fysend.at[1], fyr.at[1], 3, dev_lo_y),
    ):
        copy = pltpu.make_async_remote_copy(
            src_ref=src, dst_ref=dst, send_sem=fs.at[slot], recv_sem=fr.at[slot],
            device_id=dev, device_id_type=MESH,
        )
        forward_copies.append((cond, copy))

        @pl.when(cond)
        def _():
            copy.start()

    def fill_state(par, x, c, v):
        pads[par, c, x + 1] = v
        ysend[par, 0, c, x] = v[width_y - 1:width_y, :]
        ysend[par, 1, c, x] = v[0:1, :]

    def copy_in(x, carry):
        for c in range(4):
            fill_state(0, x, c, state_in[c, x])
        return carry

    lax.fori_loop(0, width_x, copy_in, 0)

    for step in range(steps):
        par = step % 2
        nxt = 1 - par
        snap = steps - 1 - step
        last = step == steps - 1
        exchange(
            pads.at[par, :, pl.ds(1, 1)], pads.at[par, :, pl.ds(width_x, 1)],
            pads.at[par, :, pl.ds(0, 1)], pads.at[par, :, pl.ds(width_x + 1, 1)],
            ysend.at[par, 0], ysend.at[par, 1], yrecv.at[par, 0], yrecv.at[par, 1],
            ss.at[par], rs.at[par],
        )

        def pressure_slab(x, carry, par=par, snap=snap):
            xp = x + 1
            old = pads.at[par]
            p = old[0, xp]
            dxp = (old[0, xp + 1] - old[0, x]) * 0.5
            dxa = (old[1, xp + 1] - old[1, x]) * 0.5
            dyp = dy(p, yrecv[par, 0, 0, x], yrecv[par, 1, 0, x])
            dya = dy(old[2, xp], yrecv[par, 0, 2, x], yrecv[par, 1, 2, x])
            dzp = dz(p)
            dza = dz(old[3, xp])
            divergence = dxa + dya + dza
            p_new = (
                p
                + step_length * (sound[x] * divergence + we * dxp + wn * dyp + wv * dzp)
                + inj[snap, x]
            )
            pbuf[xp] = p_new
            ypsend[0, x] = p_new[width_y - 1:width_y, :]
            ypsend[1, x] = p_new[0:1, :]
            return carry

        lax.fori_loop(0, width_x, pressure_slab, 0)
        if step == 0:
            interior.wait()
            for (cond, copy), arrives in zip(forward_copies, (has_lo_x, has_hi_x, has_lo_y, has_hi_y)):
                @pl.when(cond)
                def _():
                    copy.wait_send()

                @pl.when(arrives)
                def _():
                    copy.wait_recv()
        exchange(
            pbuf.at[pl.ds(1, 1)], pbuf.at[pl.ds(width_x, 1)],
            pbuf.at[pl.ds(0, 1)], pbuf.at[pl.ds(width_x + 1, 1)],
            ypsend.at[0], ypsend.at[1], yprecv.at[0], yprecv.at[1],
            ps, pr,
        )

        def velocity_slab(x, carry, par=par, nxt=nxt, snap=snap, last=last, step=step):
            xp = x + 1
            old = pads.at[par]
            p_new = pbuf[xp]
            grad = (
                (pbuf[xp + 1] - pbuf[x]) * 0.5,
                dy(p_new, yprecv[0, x], yprecv[1, x]),
                dz(p_new),
            )
            a_new = []
            for i in range(3):
                a = old[1 + i, xp]
                dxa = (old[1 + i, xp + 1] - old[1 + i, x]) * 0.5
                dya = dy(a, yrecv[par, 0, 1 + i, x], yrecv[par, 1, 1 + i, x])
                dza = dz(a)
                a_new.append(a + step_length * (grad[i] + we * dxa + wn * dya + wv * dza))
            fe, fn, fu = [], [], []
            for c in range(4):
                f = fpad[snap, c, xp].astype(jnp.float32)
                fe.append((fpad[snap, c, xp + 1].astype(jnp.float32) - fpad[snap, c, x].astype(jnp.float32)) * 0.5)
                fn.append(dy(f, fyr[0, snap, c, x], fyr[1, snap, c, x]))
                fu.append(dz(f))
            pieces = [p_new * (fe[1] + fn[2] + fu[3])]
            for along in (fe, fn, fu):
                pieces.append(p_new * along[0] + a_new[0] * along[1] + a_new[1] * along[2] + a_new[2] * along[3])
            for c in range(4):
                total = pieces[c] if step == 0 else acc_out[c, x] + pieces[c]
                if not last:
                    acc_out[c, x] = total
                    continue
                low, high = total[:, :half], total[:, half:]
                kernel_out[c, x] = jnp.where(me_p == 0, low, high)
                ksend[x, c] = jnp.where(me_p == 0, high, low)
            if last:
                pltpu.make_async_remote_copy(
                    src_ref=ksend.at[x], dst_ref=krecv.at[x], send_sem=ks.at[x], recv_sem=kr.at[x],
                    device_id=dev_pair, device_id_type=MESH,
                ).start()
            new_state = [p_new] + a_new
            for c in range(4):
                if last:
                    state_out[c, x] = new_state[c]
                else:
                    fill_state(nxt, x, c, new_state[c])
            return carry

        lax.fori_loop(0, width_x, velocity_slab, 0)

    for x in range(width_x):
        copy = pltpu.make_async_remote_copy(
            src_ref=ksend.at[x], dst_ref=krecv.at[x], send_sem=ks.at[x], recv_sem=kr.at[x],
            device_id=dev_pair, device_id_type=MESH,
        )
        copy.wait_send()
        copy.wait_recv()

    def add_partner(x, carry):
        for c in range(4):
            kernel_out[c, x] = kernel_out[c, x] + krecv[x, c]
        return carry

    lax.fori_loop(0, width_x, add_partner, 0)


def samples_kernel(nx, ny, local_ref, out_ref, sent, got_x, got_y, send_sem, recv_sem):
    me_p = lax.axis_index("pair")
    gx = lax.axis_index("gx")
    gy = lax.axis_index("gy")
    peers_x = [(me_p, (gx + d) % nx, gy) for d in range(1, nx)]
    peers_y = [(me_p, gx, (gy + d) % ny) for d in range(1, ny)]
    barrier = pltpu.get_barrier_semaphore()
    for dev in peers_x + peers_y:
        pl.semaphore_signal(barrier, 1, device_id=dev, device_id_type=MESH)
    pl.semaphore_wait(barrier, len(peers_x) + len(peers_y))
    rounds = ((local_ref, got_x, peers_x, 0), (sent, got_y, peers_y, nx - 1))
    total = local_ref[...]
    for src, got, peers, base in rounds:
        copies = []
        for i, dev in enumerate(peers):
            copy = pltpu.make_async_remote_copy(
                src_ref=src, dst_ref=got.at[i], send_sem=send_sem.at[base + i],
                recv_sem=recv_sem.at[base + i], device_id=dev, device_id_type=MESH,
            )
            copy.start()
            copies.append(copy)
        for copy in copies:
            copy.wait_send()
            copy.wait_recv()
        for i in range(len(peers)):
            total = total + got[i]
        if base == 0:
            sent[...] = total
    out_ref[...] = total


def gathered_samples(local_samples):
    nx, ny = lax.axis_size("gx"), lax.axis_size("gy")
    if nx < 2 or ny < 2:
        return lax.psum(local_samples, ("gx", "gy"))
    vmem = pl.BlockSpec(memory_space=pltpu.VMEM)
    return pl.pallas_call(
        functools.partial(samples_kernel, nx, ny),
        out_shape=jax.ShapeDtypeStruct(local_samples.shape, jnp.float32),
        in_specs=[vmem],
        out_specs=vmem,
        scratch_shapes=[
            pltpu.VMEM(local_samples.shape, jnp.float32),
            pltpu.VMEM((nx - 1,) + local_samples.shape, jnp.float32),
            pltpu.VMEM((ny - 1,) + local_samples.shape, jnp.float32),
            pltpu.SemaphoreType.DMA((nx + ny - 2,)),
            pltpu.SemaphoreType.DMA((nx + ny - 2,)),
        ],
        compiler_params=pltpu.CompilerParams(collective_id=1, has_side_effects=True),
    )(local_samples)


def shards(
    sound_speed_sq,
    wind_profile,
    forward_field,
    adjoint_state,
    pair_counts,
    source_cells,
    receiver_cells,
    residuals,
):
    steps_total = forward_field.shape[0]
    width_x, width_y, depth = sound_speed_sq.shape
    slots = residuals.shape[0]
    live = (jnp.arange(slots, dtype=jnp.int32) < pair_counts[0]).astype(jnp.float32)
    gx_first = lax.axis_index("gx") * width_x
    gy_first = lax.axis_index("gy") * width_y
    x_range = jnp.arange(width_x, dtype=jnp.int32)
    y_range = jnp.arange(width_y, dtype=jnp.int32)
    z_range = jnp.arange(depth, dtype=jnp.int32)

    def tile_mask(cells):
        on_x = (cells[:, 0][None, :] - gx_first) == x_range[:, None]
        on_y = (cells[:, 1][None, :] - gy_first) == y_range[:, None]
        return (on_x[:, None, :] & on_y[None, :, :]).astype(jnp.float32)

    source_z = (source_cells[:, 2][None, :] == z_range[:, None]).astype(jnp.bfloat16)
    along_z = jnp.einsum(
        "txyz,zn->txyn", forward_field[:, 0], source_z, preferred_element_type=jnp.float32
    )
    local_samples = jnp.sum(along_z * tile_mask(source_cells)[None], axis=(1, 2))
    samples = gathered_samples(local_samples)
    amplitude = jnp.transpose(residuals) * samples * live[None, :]
    spread = amplitude[:, None, None, :] * tile_mask(receiver_cells)[None]
    receiver_z = (receiver_cells[:, 2][:, None] == z_range[None, :]).astype(jnp.float32)
    injected = jnp.einsum(
        "txyn,nz->txyz", spread, receiver_z, precision=lax.Precision.HIGHEST,
        preferred_element_type=jnp.float32,
    )
    vmem = pl.BlockSpec(memory_space=pltpu.VMEM)
    kernel = functools.partial(
        stencil_kernel, lax.axis_size("gx"), lax.axis_size("gy"), steps_total
    )
    state_new, kernels = pl.pallas_call(
        kernel,
        out_shape=(
            jax.ShapeDtypeStruct((4, width_x, width_y, depth), jnp.float32),
            jax.ShapeDtypeStruct((4, width_x, width_y, depth // 2), jnp.float32),
        ),
        in_specs=[vmem] * 5,
        out_specs=(vmem, vmem),
        scratch_shapes=[
            pltpu.VMEM((2, 4, width_x + 2, width_y, depth), jnp.float32),
            pltpu.VMEM((width_x + 2, width_y, depth), jnp.float32),
            pltpu.VMEM((2, 2, 4, width_x, 1, depth), jnp.float32),
            pltpu.VMEM((2, 2, 4, width_x, 1, depth), jnp.float32),
            pltpu.VMEM((2, width_x, 1, depth), jnp.float32),
            pltpu.VMEM((2, width_x, 1, depth), jnp.float32),
            pltpu.VMEM((4, width_x, width_y, depth), jnp.float32),
            pltpu.VMEM((width_x, 4, width_y, depth // 2), jnp.float32),
            pltpu.VMEM((width_x, 4, width_y, depth // 2), jnp.float32),
            pltpu.VMEM((steps_total, 4, width_x + 2, width_y, depth), forward_field.dtype),
            pltpu.VMEM((2, steps_total, 4, width_x, 1, depth), jnp.float32),
            pltpu.VMEM((2, steps_total, 4, width_x, 1, depth), jnp.float32),
            pltpu.SemaphoreType.DMA((2, 4)),
            pltpu.SemaphoreType.DMA((2, 4)),
            pltpu.SemaphoreType.DMA((4,)),
            pltpu.SemaphoreType.DMA((4,)),
            pltpu.SemaphoreType.DMA((width_x,)),
            pltpu.SemaphoreType.DMA((width_x,)),
            pltpu.SemaphoreType.DMA((4,)),
            pltpu.SemaphoreType.DMA((4,)),
            pltpu.SemaphoreType.DMA((1,)),
        ],
        compiler_params=pltpu.CompilerParams(
            collective_id=0, has_side_effects=True, vmem_limit_bytes=48 * 1024 * 1024
        ),
    )(adjoint_state[0], sound_speed_sq, wind_profile, forward_field, injected)
    return (kernels, state_new[None])


def solution(mesh):
    in_specs = (
        P("gx", "gy", None),
        P(),
        P(None, None, "gx", "gy", None),
        P("pair", None, "gx", "gy", None),
        P("pair"),
        P("pair", None),
        P("pair", None),
        P("pair", None),
    )
    out_specs = (P(None, "gx", "gy", "pair"), P("pair", None, "gx", "gy", None))
    return jax.shard_map(shards, mesh=mesh, in_specs=in_specs, out_specs=out_specs, check_vma=False)
```

```python
import functools

import jax
import jax.numpy as jnp
from jax import lax
from jax.experimental import pallas as pl
from jax.experimental.pallas import tpu as pltpu
from jax.sharding import PartitionSpec as P

step_length = 0.25
MESH = pl.DeviceIdType.MESH


def neighbours(shard, axis, dim):
    size, length = (lax.axis_size(axis), shard.shape[dim])
    up = [(i, i + 1) for i in range(size - 1)]
    down = [(i + 1, i) for i in range(size - 1)]
    last = lax.slice_in_dim(shard, length - 1, length, axis=dim)
    first = lax.slice_in_dim(shard, 0, 1, axis=dim)
    before = lax.ppermute(last, axis, up)
    after = lax.ppermute(first, axis, down)
    return (before, after)


def local_cells(cells, width_x, width_y):
    local_x = cells[:, 0] - lax.axis_index("gx") * width_x
    local_y = cells[:, 1] - lax.axis_index("gy") * width_y
    inside = (local_x >= 0) & (local_x < width_x) & (local_y >= 0) & (local_y < width_y)
    return (
        jnp.clip(local_x, 0, width_x - 1),
        jnp.clip(local_y, 0, width_y - 1),
        cells[:, 2],
        inside.astype(jnp.float32),
    )


def stencil_kernel(
    nx, ny, steps,
    state_in, sound, wind, forward, inj,
    state_out, kernel_out,
    pads, pbuf, ysend, yrecv, ypsend, yprecv, acc_out, ksend, krecv, fpad, fysend, fyr,
    ss, rs, ps, pr, ks, kr, fs, fr, local_sem,
):
    _, width_x, width_y, depth = state_in.shape
    me_p = lax.axis_index("pair")
    gx = lax.axis_index("gx")
    gy = lax.axis_index("gy")
    has_lo_x = gx > 0
    has_hi_x = gx < nx - 1
    has_lo_y = gy > 0
    has_hi_y = gy < ny - 1
    dev_lo_x = (me_p, gx - 1, gy)
    dev_hi_x = (me_p, gx + 1, gy)
    dev_lo_y = (me_p, gx, gy - 1)
    dev_hi_y = (me_p, gx, gy + 1)
    dev_pair = (1 - me_p, gx, gy)
    half = depth // 2

    zero_slab = jnp.zeros((width_y, depth), jnp.float32)
    for par in range(2):
        for c in range(4):
            pads[par, c, 0] = zero_slab
            pads[par, c, width_x + 1] = zero_slab
            for side in range(2):
                yrecv[par, side, c] = jnp.zeros((width_x, 1, depth), jnp.float32)
    pbuf[0] = zero_slab
    pbuf[width_x + 1] = zero_slab
    zero_forward = jnp.zeros((width_y, depth), fpad.dtype)
    for t in range(steps):
        for c in range(4):
            fpad[t, c, 0] = zero_forward
            fpad[t, c, width_x + 1] = zero_forward
            for side in range(2):
                fyr[side, t, c] = jnp.zeros((width_x, 1, depth), jnp.float32)

    def forward_rows(x, carry):
        for t in range(steps):
            for c in range(4):
                f = forward[t, c, x].astype(jnp.float32)
                fysend[0, t, c, x] = f[width_y - 1:width_y, :]
                fysend[1, t, c, x] = f[0:1, :]
        return carry

    lax.fori_loop(0, width_x, forward_rows, 0)
    interior = pltpu.make_async_copy(forward, fpad.at[:, :, pl.ds(1, width_x)], local_sem.at[0])
    interior.start()
    for side in range(2):
        yprecv[side] = jnp.zeros((width_x, 1, depth), jnp.float32)

    barrier = pltpu.get_barrier_semaphore()
    pl.semaphore_signal(barrier, 1, device_id=dev_pair, device_id_type=MESH)
    for cond, dev in ((has_lo_x, dev_lo_x), (has_hi_x, dev_hi_x), (has_lo_y, dev_lo_y), (has_hi_y, dev_hi_y)):
        @pl.when(cond)
        def _():
            pl.semaphore_signal(barrier, 1, device_id=dev, device_id_type=MESH)
    peers = 1 + (
        (gx + nx - 1) // nx + (2 * nx - 2 - gx) // nx
        + (gy + ny - 1) // ny + (2 * ny - 2 - gy) // ny
    )
    pl.semaphore_wait(barrier, peers)

    iy = lax.broadcasted_iota(jnp.int32, (width_y, depth), 0)
    iz = lax.broadcasted_iota(jnp.int32, (width_y, depth), 1)
    we = wind[0:1, :]
    wn = wind[1:2, :]
    wv = wind[2:3, :]

    def dy(v, lo, hi):
        up = jnp.where(iy == width_y - 1, hi, pltpu.roll(v, width_y - 1, 0))
        down = jnp.where(iy == 0, lo, pltpu.roll(v, 1, 0))
        return (up - down) * 0.5

    def dz(v):
        up = jnp.where(iz == depth - 1, 0.0, pltpu.roll(v, depth - 1, 1))
        down = jnp.where(iz == 0, 0.0, pltpu.roll(v, 1, 1))
        return (up - down) * 0.5

    def exchange(src_lo_x, src_hi_x, dst_lo_x, dst_hi_x, src_y_hi, src_y_lo, dst_y_lo, dst_y_hi, send, recv):
        outs = (
            (has_hi_x, src_hi_x, dst_lo_x, 0, dev_hi_x),
            (has_lo_x, src_lo_x, dst_hi_x, 1, dev_lo_x),
            (has_hi_y, src_y_hi, dst_y_lo, 2, dev_hi_y),
            (has_lo_y, src_y_lo, dst_y_hi, 3, dev_lo_y),
        )
        copies = []
        for cond, src, dst, slot, dev in outs:
            copy = pltpu.make_async_remote_copy(
                src_ref=src, dst_ref=dst, send_sem=send.at[slot], recv_sem=recv.at[slot],
                device_id=dev, device_id_type=MESH,
            )
            copies.append((cond, copy))

            @pl.when(cond)
            def _():
                copy.start()
        return copies

    def settle(copies):
        incoming = (has_lo_x, has_hi_x, has_lo_y, has_hi_y)
        for (cond, copy), arrives in zip(copies, incoming):
            @pl.when(cond)
            def _():
                copy.wait_send()

            @pl.when(arrives)
            def _():
                copy.wait_recv()

    def fill_state(par, x, c, v):
        pads[par, c, x + 1] = v
        ysend[par, 0, c, x] = v[width_y - 1:width_y, :]
        ysend[par, 1, c, x] = v[0:1, :]

    def copy_in(x, carry):
        for c in range(4):
            fill_state(0, x, c, state_in[c, x])
        return carry

    lax.fori_loop(0, width_x, copy_in, 0)
    forward_copies = exchange(
        forward.at[:, :, pl.ds(0, 1)], forward.at[:, :, pl.ds(width_x - 1, 1)],
        fpad.at[:, :, pl.ds(0, 1)], fpad.at[:, :, pl.ds(width_x + 1, 1)],
        fysend.at[0], fysend.at[1], fyr.at[0], fyr.at[1], fs, fr,
    )

    def increment_slab(x, carry, get, snap, first, last):
        xp = x + 1
        p_new = get(0, x)
        a_new = [get(1 + i, x) for i in range(3)]
        fe, fn, fu = [], [], []
        for c in range(4):
            f = fpad[snap, c, xp].astype(jnp.float32)
            fe.append((fpad[snap, c, xp + 1].astype(jnp.float32) - fpad[snap, c, x].astype(jnp.float32)) * 0.5)
            fn.append(dy(f, fyr[0, snap, c, x], fyr[1, snap, c, x]))
            fu.append(dz(f))
        pieces = [p_new * (fe[1] + fn[2] + fu[3])]
        for along in (fe, fn, fu):
            pieces.append(p_new * along[0] + a_new[0] * along[1] + a_new[1] * along[2] + a_new[2] * along[3])
        for c in range(4):
            total = pieces[c] if first else acc_out[c, x] + pieces[c]
            if not last:
                acc_out[c, x] = total
                continue
            low, high = total[:, :half], total[:, half:]
            kernel_out[c, x] = jnp.where(me_p == 0, low, high)
            ksend[x, c] = jnp.where(me_p == 0, high, low)
        if last:
            pltpu.make_async_remote_copy(
                src_ref=ksend.at[x], dst_ref=krecv.at[x], send_sem=ks.at[x], recv_sem=kr.at[x],
                device_id=dev_pair, device_id_type=MESH,
            ).start()
        return carry

    def forward_ready():
        interior.wait()
        settle(forward_copies)

    for step in range(steps):
        par = step % 2
        nxt = 1 - par
        snap = steps - 1 - step
        last = step == steps - 1
        state_copies = exchange(
            pads.at[par, :, pl.ds(1, 1)], pads.at[par, :, pl.ds(width_x, 1)],
            pads.at[par, :, pl.ds(0, 1)], pads.at[par, :, pl.ds(width_x + 1, 1)],
            ysend.at[par, 0], ysend.at[par, 1], yrecv.at[par, 0], yrecv.at[par, 1],
            ss.at[par], rs.at[par],
        )
        if step > 0:
            if step == 1:
                forward_ready()
            lax.fori_loop(0, width_x, functools.partial(
                increment_slab, get=lambda c, x, par=par: pads[par, c, x + 1],
                snap=snap + 1, first=step == 1, last=False), 0)
        settle(state_copies)

        def pressure_slab(x, carry, par=par, snap=snap):
            xp = x + 1
            old = pads.at[par]
            p = old[0, xp]
            dxp = (old[0, xp + 1] - old[0, x]) * 0.5
            dxa = (old[1, xp + 1] - old[1, x]) * 0.5
            dyp = dy(p, yrecv[par, 0, 0, x], yrecv[par, 1, 0, x])
            dya = dy(old[2, xp], yrecv[par, 0, 2, x], yrecv[par, 1, 2, x])
            dzp = dz(p)
            dza = dz(old[3, xp])
            divergence = dxa + dya + dza
            p_new = (
                p
                + step_length * (sound[x] * divergence + we * dxp + wn * dyp + wv * dzp)
                + inj[snap, x]
            )
            pbuf[xp] = p_new
            ypsend[0, x] = p_new[width_y - 1:width_y, :]
            ypsend[1, x] = p_new[0:1, :]
            return carry

        lax.fori_loop(0, width_x, pressure_slab, 0)
        settle(exchange(
            pbuf.at[pl.ds(1, 1)], pbuf.at[pl.ds(width_x, 1)],
            pbuf.at[pl.ds(0, 1)], pbuf.at[pl.ds(width_x + 1, 1)],
            ypsend.at[0], ypsend.at[1], yprecv.at[0], yprecv.at[1],
            ps, pr,
        ))

        def velocity_slab(x, carry, par=par, nxt=nxt, last=last):
            xp = x + 1
            old = pads.at[par]
            p_new = pbuf[xp]
            grad = (
                (pbuf[xp + 1] - pbuf[x]) * 0.5,
                dy(p_new, yprecv[0, x], yprecv[1, x]),
                dz(p_new),
            )
            new_state = [p_new]
            for i in range(3):
                a = old[1 + i, xp]
                dxa = (old[1 + i, xp + 1] - old[1 + i, x]) * 0.5
                dya = dy(a, yrecv[par, 0, 1 + i, x], yrecv[par, 1, 1 + i, x])
                dza = dz(a)
                new_state.append(a + step_length * (grad[i] + we * dxa + wn * dya + wv * dza))
            for c in range(4):
                if last:
                    state_out[c, x] = new_state[c]
                else:
                    fill_state(nxt, x, c, new_state[c])
            return carry

        lax.fori_loop(0, width_x, velocity_slab, 0)

    if steps == 1:
        forward_ready()
    lax.fori_loop(0, width_x, functools.partial(
        increment_slab, get=lambda c, x: state_out[c, x], snap=0, first=steps == 1, last=True), 0)

    for x in range(width_x):
        copy = pltpu.make_async_remote_copy(
            src_ref=ksend.at[x], dst_ref=krecv.at[x], send_sem=ks.at[x], recv_sem=kr.at[x],
            device_id=dev_pair, device_id_type=MESH,
        )
        copy.wait_send()
        copy.wait_recv()

    def add_partner(x, carry):
        for c in range(4):
            kernel_out[c, x] = kernel_out[c, x] + krecv[x, c]
        return carry

    lax.fori_loop(0, width_x, add_partner, 0)


def samples_kernel(nx, ny, local_ref, out_ref, sent, got_x, got_y, send_sem, recv_sem):
    me_p = lax.axis_index("pair")
    gx = lax.axis_index("gx")
    gy = lax.axis_index("gy")
    peers_x = [(me_p, (gx + d) % nx, gy) for d in range(1, nx)]
    peers_y = [(me_p, gx, (gy + d) % ny) for d in range(1, ny)]
    barrier = pltpu.get_barrier_semaphore()
    for dev in peers_x + peers_y:
        pl.semaphore_signal(barrier, 1, device_id=dev, device_id_type=MESH)
    pl.semaphore_wait(barrier, len(peers_x) + len(peers_y))
    rounds = ((local_ref, got_x, peers_x, 0), (sent, got_y, peers_y, nx - 1))
    total = local_ref[...]
    for src, got, peers, base in rounds:
        copies = []
        for i, dev in enumerate(peers):
            copy = pltpu.make_async_remote_copy(
                src_ref=src, dst_ref=got.at[i], send_sem=send_sem.at[base + i],
                recv_sem=recv_sem.at[base + i], device_id=dev, device_id_type=MESH,
            )
            copy.start()
            copies.append(copy)
        for copy in copies:
            copy.wait_send()
            copy.wait_recv()
        for i in range(len(peers)):
            total = total + got[i]
        if base == 0:
            sent[...] = total
    out_ref[...] = total


def gathered_samples(local_samples):
    nx, ny = lax.axis_size("gx"), lax.axis_size("gy")
    if nx < 2 or ny < 2:
        return lax.psum(local_samples, ("gx", "gy"))
    vmem = pl.BlockSpec(memory_space=pltpu.VMEM)
    return pl.pallas_call(
        functools.partial(samples_kernel, nx, ny),
        out_shape=jax.ShapeDtypeStruct(local_samples.shape, jnp.float32),
        in_specs=[vmem],
        out_specs=vmem,
        scratch_shapes=[
            pltpu.VMEM(local_samples.shape, jnp.float32),
            pltpu.VMEM((nx - 1,) + local_samples.shape, jnp.float32),
            pltpu.VMEM((ny - 1,) + local_samples.shape, jnp.float32),
            pltpu.SemaphoreType.DMA((nx + ny - 2,)),
            pltpu.SemaphoreType.DMA((nx + ny - 2,)),
        ],
        compiler_params=pltpu.CompilerParams(collective_id=1, has_side_effects=True),
    )(local_samples)


def shards(
    sound_speed_sq,
    wind_profile,
    forward_field,
    adjoint_state,
    pair_counts,
    source_cells,
    receiver_cells,
    residuals,
):
    steps_total = forward_field.shape[0]
    width_x, width_y, depth = sound_speed_sq.shape
    slots = residuals.shape[0]
    live = (jnp.arange(slots, dtype=jnp.int32) < pair_counts[0]).astype(jnp.float32)
    gx_first = lax.axis_index("gx") * width_x
    gy_first = lax.axis_index("gy") * width_y
    x_range = jnp.arange(width_x, dtype=jnp.int32)
    y_range = jnp.arange(width_y, dtype=jnp.int32)
    z_range = jnp.arange(depth, dtype=jnp.int32)

    def tile_mask(cells):
        on_x = (cells[:, 0][None, :] - gx_first) == x_range[:, None]
        on_y = (cells[:, 1][None, :] - gy_first) == y_range[:, None]
        return (on_x[:, None, :] & on_y[None, :, :]).astype(jnp.float32)

    source_z = (source_cells[:, 2][None, :] == z_range[:, None]).astype(jnp.bfloat16)
    along_z = jnp.einsum(
        "txyz,zn->txyn", forward_field[:, 0], source_z, preferred_element_type=jnp.float32
    )
    local_samples = jnp.sum(along_z * tile_mask(source_cells)[None], axis=(1, 2))
    samples = gathered_samples(local_samples)
    amplitude = jnp.transpose(residuals) * samples * live[None, :]
    spread = amplitude[:, None, None, :] * tile_mask(receiver_cells)[None]
    receiver_z = (receiver_cells[:, 2][:, None] == z_range[None, :]).astype(jnp.float32)
    injected = jnp.einsum(
        "txyn,nz->txyz", spread, receiver_z, precision=lax.Precision.HIGHEST,
        preferred_element_type=jnp.float32,
    )
    vmem = pl.BlockSpec(memory_space=pltpu.VMEM)
    kernel = functools.partial(
        stencil_kernel, lax.axis_size("gx"), lax.axis_size("gy"), steps_total
    )
    state_new, kernels = pl.pallas_call(
        kernel,
        out_shape=(
            jax.ShapeDtypeStruct((4, width_x, width_y, depth), jnp.float32),
            jax.ShapeDtypeStruct((4, width_x, width_y, depth // 2), jnp.float32),
        ),
        in_specs=[vmem] * 5,
        out_specs=(vmem, vmem),
        scratch_shapes=[
            pltpu.VMEM((2, 4, width_x + 2, width_y, depth), jnp.float32),
            pltpu.VMEM((width_x + 2, width_y, depth), jnp.float32),
            pltpu.VMEM((2, 2, 4, width_x, 1, depth), jnp.float32),
            pltpu.VMEM((2, 2, 4, width_x, 1, depth), jnp.float32),
            pltpu.VMEM((2, width_x, 1, depth), jnp.float32),
            pltpu.VMEM((2, width_x, 1, depth), jnp.float32),
            pltpu.VMEM((4, width_x, width_y, depth), jnp.float32),
            pltpu.VMEM((width_x, 4, width_y, depth // 2), jnp.float32),
            pltpu.VMEM((width_x, 4, width_y, depth // 2), jnp.float32),
            pltpu.VMEM((steps_total, 4, width_x + 2, width_y, depth), forward_field.dtype),
            pltpu.VMEM((2, steps_total, 4, width_x, 1, depth), jnp.float32),
            pltpu.VMEM((2, steps_total, 4, width_x, 1, depth), jnp.float32),
            pltpu.SemaphoreType.DMA((2, 4)),
            pltpu.SemaphoreType.DMA((2, 4)),
            pltpu.SemaphoreType.DMA((4,)),
            pltpu.SemaphoreType.DMA((4,)),
            pltpu.SemaphoreType.DMA((width_x,)),
            pltpu.SemaphoreType.DMA((width_x,)),
            pltpu.SemaphoreType.DMA((4,)),
            pltpu.SemaphoreType.DMA((4,)),
            pltpu.SemaphoreType.DMA((1,)),
        ],
        compiler_params=pltpu.CompilerParams(
            collective_id=0, has_side_effects=True, vmem_limit_bytes=48 * 1024 * 1024
        ),
    )(adjoint_state[0], sound_speed_sq, wind_profile, forward_field, injected)
    return (kernels, state_new[None])


def solution(mesh):
    in_specs = (
        P("gx", "gy", None),
        P(),
        P(None, None, "gx", "gy", None),
        P("pair", None, "gx", "gy", None),
        P("pair"),
        P("pair", None),
        P("pair", None),
        P("pair", None),
    )
    out_specs = (P(None, "gx", "gy", "pair"), P("pair", None, "gx", "gy", None))
    return jax.shard_map(shards, mesh=mesh, in_specs=in_specs, out_specs=out_specs, check_vma=False)
```

```python
import functools

import jax
import jax.numpy as jnp
from jax import lax
from jax.experimental import pallas as pl
from jax.experimental.pallas import tpu as pltpu
from jax.sharding import PartitionSpec as P

step_length = 0.25
MESH = pl.DeviceIdType.MESH


def neighbours(shard, axis, dim):
    size, length = (lax.axis_size(axis), shard.shape[dim])
    up = [(i, i + 1) for i in range(size - 1)]
    down = [(i + 1, i) for i in range(size - 1)]
    last = lax.slice_in_dim(shard, length - 1, length, axis=dim)
    first = lax.slice_in_dim(shard, 0, 1, axis=dim)
    before = lax.ppermute(last, axis, up)
    after = lax.ppermute(first, axis, down)
    return (before, after)


def local_cells(cells, width_x, width_y):
    local_x = cells[:, 0] - lax.axis_index("gx") * width_x
    local_y = cells[:, 1] - lax.axis_index("gy") * width_y
    inside = (local_x >= 0) & (local_x < width_x) & (local_y >= 0) & (local_y < width_y)
    return (
        jnp.clip(local_x, 0, width_x - 1),
        jnp.clip(local_y, 0, width_y - 1),
        cells[:, 2],
        inside.astype(jnp.float32),
    )


def stencil_kernel(
    nx, ny, steps,
    state_in, sound, wind, forward, inj,
    state_out, kernel_out,
    pads, pbuf, ysend, yrecv, ypsend, yprecv, acc_out, ksend, krecv, fpad, fysend, fyr,
    ss, rs, ps, pr, ks, kr, fs, fr, local_sem,
):
    _, width_x, width_y, depth = state_in.shape
    me_p = lax.axis_index("pair")
    gx = lax.axis_index("gx")
    gy = lax.axis_index("gy")
    has_lo_x = gx > 0
    has_hi_x = gx < nx - 1
    has_lo_y = gy > 0
    has_hi_y = gy < ny - 1
    dev_lo_x = (me_p, gx - 1, gy)
    dev_hi_x = (me_p, gx + 1, gy)
    dev_lo_y = (me_p, gx, gy - 1)
    dev_hi_y = (me_p, gx, gy + 1)
    dev_pair = (1 - me_p, gx, gy)
    half = depth // 2

    zero_slab = jnp.zeros((width_y, depth), jnp.float32)
    for par in range(2):
        for c in range(4):
            pads[par, c, 0] = zero_slab
            pads[par, c, width_x + 1] = zero_slab
            for side in range(2):
                yrecv[par, side, c] = jnp.zeros((width_x, depth), jnp.float32)
    pbuf[0] = zero_slab
    pbuf[width_x + 1] = zero_slab
    zero_forward = jnp.zeros((width_y, depth), fpad.dtype)
    for t in range(steps):
        for c in range(4):
            fpad[t, c, 0] = zero_forward
            fpad[t, c, width_x + 1] = zero_forward
            for side in range(2):
                fyr[side, t, c] = jnp.zeros((width_x, depth), jnp.float32)

    def forward_rows(x, carry):
        for t in range(steps):
            for c in range(4):
                f = forward[t, c, x].astype(jnp.float32)
                fysend[0, t, c, x:x + 1, :] = f[width_y - 1:width_y, :]
                fysend[1, t, c, x:x + 1, :] = f[0:1, :]
        return carry

    [forward_rows(x, 0) for x in range(width_x)]
    interior = pltpu.make_async_copy(forward, fpad.at[:, :, pl.ds(1, width_x)], local_sem.at[0])
    interior.start()
    for side in range(2):
        yprecv[side] = jnp.zeros((width_x, depth), jnp.float32)

    barrier = pltpu.get_barrier_semaphore()
    pl.semaphore_signal(barrier, 1, device_id=dev_pair, device_id_type=MESH)
    for cond, dev in ((has_lo_x, dev_lo_x), (has_hi_x, dev_hi_x), (has_lo_y, dev_lo_y), (has_hi_y, dev_hi_y)):
        @pl.when(cond)
        def _():
            pl.semaphore_signal(barrier, 1, device_id=dev, device_id_type=MESH)
    peers = 1 + (
        (gx + nx - 1) // nx + (2 * nx - 2 - gx) // nx
        + (gy + ny - 1) // ny + (2 * ny - 2 - gy) // ny
    )
    pl.semaphore_wait(barrier, peers)

    iy = lax.broadcasted_iota(jnp.int32, (width_y, depth), 0)
    iz = lax.broadcasted_iota(jnp.int32, (width_y, depth), 1)
    we = wind[0:1, :]
    wn = wind[1:2, :]
    wv = wind[2:3, :]

    def dy(v, lo, hi):
        up = jnp.where(iy == width_y - 1, hi, pltpu.roll(v, width_y - 1, 0))
        down = jnp.where(iy == 0, lo, pltpu.roll(v, 1, 0))
        return (up - down) * 0.5

    def dz(v):
        up = jnp.where(iz == depth - 1, 0.0, pltpu.roll(v, depth - 1, 1))
        down = jnp.where(iz == 0, 0.0, pltpu.roll(v, 1, 1))
        return (up - down) * 0.5

    def exchange(src_lo_x, src_hi_x, dst_lo_x, dst_hi_x, src_y_hi, src_y_lo, dst_y_lo, dst_y_hi, send, recv):
        outs = (
            (has_hi_x, src_hi_x, dst_lo_x, 0, dev_hi_x),
            (has_lo_x, src_lo_x, dst_hi_x, 1, dev_lo_x),
            (has_hi_y, src_y_hi, dst_y_lo, 2, dev_hi_y),
            (has_lo_y, src_y_lo, dst_y_hi, 3, dev_lo_y),
        )
        copies = []
        for cond, src, dst, slot, dev in outs:
            copy = pltpu.make_async_remote_copy(
                src_ref=src, dst_ref=dst, send_sem=send.at[slot], recv_sem=recv.at[slot],
                device_id=dev, device_id_type=MESH,
            )
            copies.append((cond, copy))

            @pl.when(cond)
            def _():
                copy.start()
        return copies

    def settle(copies):
        incoming = (has_lo_x, has_hi_x, has_lo_y, has_hi_y)
        for (cond, copy), arrives in zip(copies, incoming):
            @pl.when(cond)
            def _():
                copy.wait_send()

            @pl.when(arrives)
            def _():
                copy.wait_recv()

    def fill_state(par, x, c, v):
        pads[par, c, x + 1] = v
        ysend[par, 0, c, x:x + 1, :] = v[width_y - 1:width_y, :]
        ysend[par, 1, c, x:x + 1, :] = v[0:1, :]

    def copy_in(x, carry):
        for c in range(4):
            fill_state(0, x, c, state_in[c, x])
        return carry

    [copy_in(x, 0) for x in range(width_x)]
    forward_copies = exchange(
        forward.at[:, :, pl.ds(0, 1)], forward.at[:, :, pl.ds(width_x - 1, 1)],
        fpad.at[:, :, pl.ds(0, 1)], fpad.at[:, :, pl.ds(width_x + 1, 1)],
        fysend.at[0], fysend.at[1], fyr.at[0], fyr.at[1], fs, fr,
    )

    def increment_slab(x, carry, get, snap, first, last):
        xp = x + 1
        p_new = get(0, x)
        a_new = [get(1 + i, x) for i in range(3)]
        fe, fn, fu = [], [], []
        for c in range(4):
            f = fpad[snap, c, xp].astype(jnp.float32)
            fe.append((fpad[snap, c, xp + 1].astype(jnp.float32) - fpad[snap, c, x].astype(jnp.float32)) * 0.5)
            fn.append(dy(f, fyr[0, snap, c, x:x + 1, :], fyr[1, snap, c, x:x + 1, :]))
            fu.append(dz(f))
        pieces = [p_new * (fe[1] + fn[2] + fu[3])]
        for along in (fe, fn, fu):
            pieces.append(p_new * along[0] + a_new[0] * along[1] + a_new[1] * along[2] + a_new[2] * along[3])
        for c in range(4):
            total = pieces[c] if first else acc_out[c, x] + pieces[c]
            if not last:
                acc_out[c, x] = total
                continue
            low, high = total[:, :half], total[:, half:]
            kernel_out[c, x] = jnp.where(me_p == 0, low, high)
            ksend[x, c] = jnp.where(me_p == 0, high, low)
        if last:
            pltpu.make_async_remote_copy(
                src_ref=ksend.at[x], dst_ref=krecv.at[x], send_sem=ks.at[x], recv_sem=kr.at[x],
                device_id=dev_pair, device_id_type=MESH,
            ).start()
        return carry

    def forward_ready():
        interior.wait()
        settle(forward_copies)

    for step in range(steps):
        par = step % 2
        nxt = 1 - par
        snap = steps - 1 - step
        last = step == steps - 1
        state_copies = exchange(
            pads.at[par, :, pl.ds(1, 1)], pads.at[par, :, pl.ds(width_x, 1)],
            pads.at[par, :, pl.ds(0, 1)], pads.at[par, :, pl.ds(width_x + 1, 1)],
            ysend.at[par, 0], ysend.at[par, 1], yrecv.at[par, 0], yrecv.at[par, 1],
            ss.at[par], rs.at[par],
        )
        if step > 0:
            if step == 1:
                forward_ready()
            [(functools.partial(
                increment_slab, get=lambda c, x, par=par: pads[par, c, x + 1],
                snap=snap + 1, first=step == 1, last=False))(x, 0) for x in range(width_x)]
        settle(state_copies)

        def pressure_slab(x, carry, par=par, snap=snap):
            xp = x + 1
            old = pads.at[par]
            p = old[0, xp]
            dxp = (old[0, xp + 1] - old[0, x]) * 0.5
            dxa = (old[1, xp + 1] - old[1, x]) * 0.5
            dyp = dy(p, yrecv[par, 0, 0, x:x + 1, :], yrecv[par, 1, 0, x:x + 1, :])
            dya = dy(old[2, xp], yrecv[par, 0, 2, x:x + 1, :], yrecv[par, 1, 2, x:x + 1, :])
            dzp = dz(p)
            dza = dz(old[3, xp])
            divergence = dxa + dya + dza
            p_new = (
                p
                + step_length * (sound[x] * divergence + we * dxp + wn * dyp + wv * dzp)
                + inj[snap, x]
            )
            pbuf[xp] = p_new
            ypsend[0, x:x + 1, :] = p_new[width_y - 1:width_y, :]
            ypsend[1, x:x + 1, :] = p_new[0:1, :]
            return carry

        [pressure_slab(x, 0) for x in range(width_x)]
        settle(exchange(
            pbuf.at[pl.ds(1, 1)], pbuf.at[pl.ds(width_x, 1)],
            pbuf.at[pl.ds(0, 1)], pbuf.at[pl.ds(width_x + 1, 1)],
            ypsend.at[0], ypsend.at[1], yprecv.at[0], yprecv.at[1],
            ps, pr,
        ))

        def velocity_slab(x, carry, par=par, nxt=nxt, last=last):
            xp = x + 1
            old = pads.at[par]
            p_new = pbuf[xp]
            grad = (
                (pbuf[xp + 1] - pbuf[x]) * 0.5,
                dy(p_new, yprecv[0, x:x + 1, :], yprecv[1, x:x + 1, :]),
                dz(p_new),
            )
            new_state = [p_new]
            for i in range(3):
                a = old[1 + i, xp]
                dxa = (old[1 + i, xp + 1] - old[1 + i, x]) * 0.5
                dya = dy(a, yrecv[par, 0, 1 + i, x:x + 1, :], yrecv[par, 1, 1 + i, x:x + 1, :])
                dza = dz(a)
                new_state.append(a + step_length * (grad[i] + we * dxa + wn * dya + wv * dza))
            for c in range(4):
                if last:
                    state_out[c, x] = new_state[c]
                else:
                    fill_state(nxt, x, c, new_state[c])
            return carry

        [velocity_slab(x, 0) for x in range(width_x)]

    if steps == 1:
        forward_ready()
    [(functools.partial(
        increment_slab, get=lambda c, x: state_out[c, x], snap=0, first=steps == 1, last=True))(x, 0) for x in range(width_x)]

    for x in range(width_x):
        copy = pltpu.make_async_remote_copy(
            src_ref=ksend.at[x], dst_ref=krecv.at[x], send_sem=ks.at[x], recv_sem=kr.at[x],
            device_id=dev_pair, device_id_type=MESH,
        )
        copy.wait_send()
        copy.wait_recv()

    def add_partner(x, carry):
        for c in range(4):
            kernel_out[c, x] = kernel_out[c, x] + krecv[x, c]
        return carry

    [add_partner(x, 0) for x in range(width_x)]


def samples_kernel(nx, ny, local_ref, out_ref, sent, got_x, got_y, send_sem, recv_sem):
    me_p = lax.axis_index("pair")
    gx = lax.axis_index("gx")
    gy = lax.axis_index("gy")
    peers_x = [(me_p, (gx + d) % nx, gy) for d in range(1, nx)]
    peers_y = [(me_p, gx, (gy + d) % ny) for d in range(1, ny)]
    barrier = pltpu.get_barrier_semaphore()
    for dev in peers_x + peers_y:
        pl.semaphore_signal(barrier, 1, device_id=dev, device_id_type=MESH)
    pl.semaphore_wait(barrier, len(peers_x) + len(peers_y))
    rounds = ((local_ref, got_x, peers_x, 0), (sent, got_y, peers_y, nx - 1))
    total = local_ref[...]
    for src, got, peers, base in rounds:
        copies = []
        for i, dev in enumerate(peers):
            copy = pltpu.make_async_remote_copy(
                src_ref=src, dst_ref=got.at[i], send_sem=send_sem.at[base + i],
                recv_sem=recv_sem.at[base + i], device_id=dev, device_id_type=MESH,
            )
            copy.start()
            copies.append(copy)
        for copy in copies:
            copy.wait_send()
            copy.wait_recv()
        for i in range(len(peers)):
            total = total + got[i]
        if base == 0:
            sent[...] = total
    out_ref[...] = total


def gathered_samples(local_samples):
    nx, ny = lax.axis_size("gx"), lax.axis_size("gy")
    if nx < 2 or ny < 2:
        return lax.psum(local_samples, ("gx", "gy"))
    vmem = pl.BlockSpec(memory_space=pltpu.VMEM)
    return pl.pallas_call(
        functools.partial(samples_kernel, nx, ny),
        out_shape=jax.ShapeDtypeStruct(local_samples.shape, jnp.float32),
        in_specs=[vmem],
        out_specs=vmem,
        scratch_shapes=[
            pltpu.VMEM(local_samples.shape, jnp.float32),
            pltpu.VMEM((nx - 1,) + local_samples.shape, jnp.float32),
            pltpu.VMEM((ny - 1,) + local_samples.shape, jnp.float32),
            pltpu.SemaphoreType.DMA((nx + ny - 2,)),
            pltpu.SemaphoreType.DMA((nx + ny - 2,)),
        ],
        compiler_params=pltpu.CompilerParams(collective_id=1, has_side_effects=True),
    )(local_samples)


def shards(
    sound_speed_sq,
    wind_profile,
    forward_field,
    adjoint_state,
    pair_counts,
    source_cells,
    receiver_cells,
    residuals,
):
    steps_total = forward_field.shape[0]
    width_x, width_y, depth = sound_speed_sq.shape
    slots = residuals.shape[0]
    live = (jnp.arange(slots, dtype=jnp.int32) < pair_counts[0]).astype(jnp.float32)
    gx_first = lax.axis_index("gx") * width_x
    gy_first = lax.axis_index("gy") * width_y
    x_range = jnp.arange(width_x, dtype=jnp.int32)
    y_range = jnp.arange(width_y, dtype=jnp.int32)
    z_range = jnp.arange(depth, dtype=jnp.int32)

    def tile_mask(cells):
        on_x = (cells[:, 0][None, :] - gx_first) == x_range[:, None]
        on_y = (cells[:, 1][None, :] - gy_first) == y_range[:, None]
        return (on_x[:, None, :] & on_y[None, :, :]).astype(jnp.float32)

    source_z = (source_cells[:, 2][None, :] == z_range[:, None]).astype(jnp.bfloat16)
    along_z = jnp.einsum(
        "txyz,zn->txyn", forward_field[:, 0], source_z, preferred_element_type=jnp.float32
    )
    local_samples = jnp.sum(along_z * tile_mask(source_cells)[None], axis=(1, 2))
    samples = gathered_samples(local_samples)
    amplitude = jnp.transpose(residuals) * samples * live[None, :]
    spread = amplitude[:, None, None, :] * tile_mask(receiver_cells)[None]
    receiver_z = (receiver_cells[:, 2][:, None] == z_range[None, :]).astype(jnp.float32)
    injected = jnp.einsum(
        "txyn,nz->txyz", spread, receiver_z, precision=lax.Precision.HIGHEST,
        preferred_element_type=jnp.float32,
    )
    vmem = pl.BlockSpec(memory_space=pltpu.VMEM)
    kernel = functools.partial(
        stencil_kernel, lax.axis_size("gx"), lax.axis_size("gy"), steps_total
    )
    state_new, kernels = pl.pallas_call(
        kernel,
        out_shape=(
            jax.ShapeDtypeStruct((4, width_x, width_y, depth), jnp.float32),
            jax.ShapeDtypeStruct((4, width_x, width_y, depth // 2), jnp.float32),
        ),
        in_specs=[vmem] * 5,
        out_specs=(vmem, vmem),
        scratch_shapes=[
            pltpu.VMEM((2, 4, width_x + 2, width_y, depth), jnp.float32),
            pltpu.VMEM((width_x + 2, width_y, depth), jnp.float32),
            pltpu.VMEM((2, 2, 4, width_x, depth), jnp.float32),
            pltpu.VMEM((2, 2, 4, width_x, depth), jnp.float32),
            pltpu.VMEM((2, width_x, depth), jnp.float32),
            pltpu.VMEM((2, width_x, depth), jnp.float32),
            pltpu.VMEM((4, width_x, width_y, depth), jnp.float32),
            pltpu.VMEM((width_x, 4, width_y, depth // 2), jnp.float32),
            pltpu.VMEM((width_x, 4, width_y, depth // 2), jnp.float32),
            pltpu.VMEM((steps_total, 4, width_x + 2, width_y, depth), forward_field.dtype),
            pltpu.VMEM((2, steps_total, 4, width_x, depth), jnp.float32),
            pltpu.VMEM((2, steps_total, 4, width_x, depth), jnp.float32),
            pltpu.SemaphoreType.DMA((2, 4)),
            pltpu.SemaphoreType.DMA((2, 4)),
            pltpu.SemaphoreType.DMA((4,)),
            pltpu.SemaphoreType.DMA((4,)),
            pltpu.SemaphoreType.DMA((width_x,)),
            pltpu.SemaphoreType.DMA((width_x,)),
            pltpu.SemaphoreType.DMA((4,)),
            pltpu.SemaphoreType.DMA((4,)),
            pltpu.SemaphoreType.DMA((1,)),
        ],
        compiler_params=pltpu.CompilerParams(
            collective_id=0, has_side_effects=True, vmem_limit_bytes=48 * 1024 * 1024
        ),
    )(adjoint_state[0], sound_speed_sq, wind_profile, forward_field, injected)
    return (kernels, state_new[None])


def solution(mesh):
    in_specs = (
        P("gx", "gy", None),
        P(),
        P(None, None, "gx", "gy", None),
        P("pair", None, "gx", "gy", None),
        P("pair"),
        P("pair", None),
        P("pair", None),
        P("pair", None),
    )
    out_specs = (P(None, "gx", "gy", "pair"), P("pair", None, "gx", "gy", None))
    return jax.shard_map(shards, mesh=mesh, in_specs=in_specs, out_specs=out_specs, check_vma=False)
```

```python
import functools

import jax
import jax.numpy as jnp
from jax import lax
from jax.experimental import pallas as pl
from jax.experimental.pallas import tpu as pltpu
from jax.sharding import PartitionSpec as P

step_length = 0.25
MESH = pl.DeviceIdType.MESH


def neighbours(shard, axis, dim):
    size, length = (lax.axis_size(axis), shard.shape[dim])
    up = [(i, i + 1) for i in range(size - 1)]
    down = [(i + 1, i) for i in range(size - 1)]
    last = lax.slice_in_dim(shard, length - 1, length, axis=dim)
    first = lax.slice_in_dim(shard, 0, 1, axis=dim)
    before = lax.ppermute(last, axis, up)
    after = lax.ppermute(first, axis, down)
    return (before, after)


def local_cells(cells, width_x, width_y):
    local_x = cells[:, 0] - lax.axis_index("gx") * width_x
    local_y = cells[:, 1] - lax.axis_index("gy") * width_y
    inside = (local_x >= 0) & (local_x < width_x) & (local_y >= 0) & (local_y < width_y)
    return (
        jnp.clip(local_x, 0, width_x - 1),
        jnp.clip(local_y, 0, width_y - 1),
        cells[:, 2],
        inside.astype(jnp.float32),
    )


def stencil_kernel(
    nx, ny, steps,
    state_in, sound, wind, forward, inj,
    state_out, kernel_out,
    pads, pbuf, ysend, yrecv, ypsend, yprecv, acc_out, ksend, krecv, fpad, fysend, fyr,
    ss, rs, ps, pr, ks, kr, fs, fr, local_sem,
):
    _, width_x, width_y, depth = state_in.shape
    me_p = lax.axis_index("pair")
    gx = lax.axis_index("gx")
    gy = lax.axis_index("gy")
    has_lo_x = gx > 0
    has_hi_x = gx < nx - 1
    has_lo_y = gy > 0
    has_hi_y = gy < ny - 1
    dev_lo_x = (me_p, gx - 1, gy)
    dev_hi_x = (me_p, gx + 1, gy)
    dev_lo_y = (me_p, gx, gy - 1)
    dev_hi_y = (me_p, gx, gy + 1)
    dev_pair = (1 - me_p, gx, gy)
    half = depth // 2

    zero_slab = jnp.zeros((width_y, depth), jnp.float32)
    for par in range(2):
        for c in range(4):
            pads[par, c, 0] = zero_slab
            pads[par, c, width_x + 1] = zero_slab
            for side in range(2):
                yrecv[par, side, c] = jnp.zeros((width_x, depth), jnp.float32)
    pbuf[0] = zero_slab
    pbuf[width_x + 1] = zero_slab
    zero_forward = jnp.zeros((width_y, depth), fpad.dtype)
    for t in range(steps):
        for c in range(4):
            fpad[t, c, 0] = zero_forward
            fpad[t, c, width_x + 1] = zero_forward
            for side in range(2):
                fyr[side, t, c // 2, pl.ds((c % 2) * width_x, width_x), :] = jnp.zeros((width_x, depth), fyr.dtype)

    def forward_rows(x, carry):
        for t in range(steps):
            for c in range(4):
                f = forward[t, c, x]
                row = (c % 2) * width_x + x
                fysend[0, t, c // 2, row:row + 1, :] = f[width_y - 1:width_y, :]
                fysend[1, t, c // 2, row:row + 1, :] = f[0:1, :]
        return carry

    [forward_rows(x, 0) for x in range(width_x)]
    interior = pltpu.make_async_copy(forward, fpad.at[:, :, pl.ds(1, width_x)], local_sem.at[0])
    interior.start()
    for side in range(2):
        yprecv[side] = jnp.zeros((width_x, depth), jnp.float32)

    barrier = pltpu.get_barrier_semaphore()
    pl.semaphore_signal(barrier, 1, device_id=dev_pair, device_id_type=MESH)
    for cond, dev in ((has_lo_x, dev_lo_x), (has_hi_x, dev_hi_x), (has_lo_y, dev_lo_y), (has_hi_y, dev_hi_y)):
        @pl.when(cond)
        def _():
            pl.semaphore_signal(barrier, 1, device_id=dev, device_id_type=MESH)
    peers = 1 + (
        (gx + nx - 1) // nx + (2 * nx - 2 - gx) // nx
        + (gy + ny - 1) // ny + (2 * ny - 2 - gy) // ny
    )
    pl.semaphore_wait(barrier, peers)

    iy = lax.broadcasted_iota(jnp.int32, (width_y, depth), 0)
    iz = lax.broadcasted_iota(jnp.int32, (width_y, depth), 1)
    we = wind[0:1, :]
    wn = wind[1:2, :]
    wv = wind[2:3, :]

    def dy(v, lo, hi):
        up = jnp.where(iy == width_y - 1, hi, pltpu.roll(v, width_y - 1, 0))
        down = jnp.where(iy == 0, lo, pltpu.roll(v, 1, 0))
        return (up - down) * 0.5

    def dz(v):
        up = jnp.where(iz == depth - 1, 0.0, pltpu.roll(v, depth - 1, 1))
        down = jnp.where(iz == 0, 0.0, pltpu.roll(v, 1, 1))
        return (up - down) * 0.5

    def exchange(src_lo_x, src_hi_x, dst_lo_x, dst_hi_x, src_y_hi, src_y_lo, dst_y_lo, dst_y_hi, send, recv):
        outs = (
            (has_hi_x, src_hi_x, dst_lo_x, 0, dev_hi_x),
            (has_lo_x, src_lo_x, dst_hi_x, 1, dev_lo_x),
            (has_hi_y, src_y_hi, dst_y_lo, 2, dev_hi_y),
            (has_lo_y, src_y_lo, dst_y_hi, 3, dev_lo_y),
        )
        copies = []
        for cond, src, dst, slot, dev in outs:
            copy = pltpu.make_async_remote_copy(
                src_ref=src, dst_ref=dst, send_sem=send.at[slot], recv_sem=recv.at[slot],
                device_id=dev, device_id_type=MESH,
            )
            copies.append((cond, copy))

            @pl.when(cond)
            def _():
                copy.start()
        return copies

    def settle(copies):
        incoming = (has_lo_x, has_hi_x, has_lo_y, has_hi_y)
        for (cond, copy), arrives in zip(copies, incoming):
            @pl.when(cond)
            def _():
                copy.wait_send()

            @pl.when(arrives)
            def _():
                copy.wait_recv()

    def fill_state(par, x, c, v):
        pads[par, c, x + 1] = v
        ysend[par, 0, c, x:x + 1, :] = v[width_y - 1:width_y, :]
        ysend[par, 1, c, x:x + 1, :] = v[0:1, :]

    def copy_in(x, carry):
        for c in range(4):
            fill_state(0, x, c, state_in[c, x])
        return carry

    [copy_in(x, 0) for x in range(width_x)]
    forward_copies = exchange(
        forward.at[:, :, pl.ds(0, 1)], forward.at[:, :, pl.ds(width_x - 1, 1)],
        fpad.at[:, :, pl.ds(0, 1)], fpad.at[:, :, pl.ds(width_x + 1, 1)],
        fysend.at[0], fysend.at[1], fyr.at[0], fyr.at[1], fs, fr,
    )

    def increment_slab(x, carry, get, snap, first, last):
        xp = x + 1
        p_new = get(0, x)
        a_new = [get(1 + i, x) for i in range(3)]
        fe, fn, fu = [], [], []
        for c in range(4):
            f = fpad[snap, c, xp].astype(jnp.float32)
            fe.append((fpad[snap, c, xp + 1].astype(jnp.float32) - fpad[snap, c, x].astype(jnp.float32)) * 0.5)
            row = (c % 2) * width_x + x
            fn.append(dy(f, fyr[0, snap, c // 2, row:row + 1, :].astype(jnp.float32),
                         fyr[1, snap, c // 2, row:row + 1, :].astype(jnp.float32)))
            fu.append(dz(f))
        pieces = [p_new * (fe[1] + fn[2] + fu[3])]
        for along in (fe, fn, fu):
            pieces.append(p_new * along[0] + a_new[0] * along[1] + a_new[1] * along[2] + a_new[2] * along[3])
        for c in range(4):
            total = pieces[c] if first else acc_out[c, x] + pieces[c]
            if not last:
                acc_out[c, x] = total
                continue
            low, high = total[:, :half], total[:, half:]
            kernel_out[c, x] = jnp.where(me_p == 0, low, high)
            ksend[x, c] = jnp.where(me_p == 0, high, low)
        if last:
            pltpu.make_async_remote_copy(
                src_ref=ksend.at[x], dst_ref=krecv.at[x], send_sem=ks.at[x], recv_sem=kr.at[x],
                device_id=dev_pair, device_id_type=MESH,
            ).start()
        return carry

    def forward_ready():
        interior.wait()
        settle(forward_copies)

    for step in range(steps):
        par = step % 2
        nxt = 1 - par
        snap = steps - 1 - step
        last = step == steps - 1
        state_copies = exchange(
            pads.at[par, :, pl.ds(1, 1)], pads.at[par, :, pl.ds(width_x, 1)],
            pads.at[par, :, pl.ds(0, 1)], pads.at[par, :, pl.ds(width_x + 1, 1)],
            ysend.at[par, 0], ysend.at[par, 1], yrecv.at[par, 0], yrecv.at[par, 1],
            ss.at[par], rs.at[par],
        )
        if step > 0:
            if step == 1:
                forward_ready()
            [(functools.partial(
                increment_slab, get=lambda c, x, par=par: pads[par, c, x + 1],
                snap=snap + 1, first=step == 1, last=False))(x, 0) for x in range(width_x)]
        settle(state_copies)

        def pressure_slab(x, carry, par=par, snap=snap):
            xp = x + 1
            old = pads.at[par]
            p = old[0, xp]
            dxp = (old[0, xp + 1] - old[0, x]) * 0.5
            dxa = (old[1, xp + 1] - old[1, x]) * 0.5
            dyp = dy(p, yrecv[par, 0, 0, x:x + 1, :], yrecv[par, 1, 0, x:x + 1, :])
            dya = dy(old[2, xp], yrecv[par, 0, 2, x:x + 1, :], yrecv[par, 1, 2, x:x + 1, :])
            dzp = dz(p)
            dza = dz(old[3, xp])
            divergence = dxa + dya + dza
            p_new = (
                p
                + step_length * (sound[x] * divergence + we * dxp + wn * dyp + wv * dzp)
                + inj[snap, x]
            )
            pbuf[xp] = p_new
            ypsend[0, x:x + 1, :] = p_new[width_y - 1:width_y, :]
            ypsend[1, x:x + 1, :] = p_new[0:1, :]
            return carry

        [pressure_slab(x, 0) for x in range(width_x)]
        settle(exchange(
            pbuf.at[pl.ds(1, 1)], pbuf.at[pl.ds(width_x, 1)],
            pbuf.at[pl.ds(0, 1)], pbuf.at[pl.ds(width_x + 1, 1)],
            ypsend.at[0], ypsend.at[1], yprecv.at[0], yprecv.at[1],
            ps, pr,
        ))

        def velocity_slab(x, carry, par=par, nxt=nxt, last=last):
            xp = x + 1
            old = pads.at[par]
            p_new = pbuf[xp]
            grad = (
                (pbuf[xp + 1] - pbuf[x]) * 0.5,
                dy(p_new, yprecv[0, x:x + 1, :], yprecv[1, x:x + 1, :]),
                dz(p_new),
            )
            new_state = [p_new]
            for i in range(3):
                a = old[1 + i, xp]
                dxa = (old[1 + i, xp + 1] - old[1 + i, x]) * 0.5
                dya = dy(a, yrecv[par, 0, 1 + i, x:x + 1, :], yrecv[par, 1, 1 + i, x:x + 1, :])
                dza = dz(a)
                new_state.append(a + step_length * (grad[i] + we * dxa + wn * dya + wv * dza))
            for c in range(4):
                if last:
                    state_out[c, x] = new_state[c]
                else:
                    fill_state(nxt, x, c, new_state[c])
            return carry

        [velocity_slab(x, 0) for x in range(width_x)]

    if steps == 1:
        forward_ready()
    [(functools.partial(
        increment_slab, get=lambda c, x: state_out[c, x], snap=0, first=steps == 1, last=True))(x, 0) for x in range(width_x)]

    for x in range(width_x):
        copy = pltpu.make_async_remote_copy(
            src_ref=ksend.at[x], dst_ref=krecv.at[x], send_sem=ks.at[x], recv_sem=kr.at[x],
            device_id=dev_pair, device_id_type=MESH,
        )
        copy.wait_send()
        copy.wait_recv()

    def add_partner(x, carry):
        for c in range(4):
            kernel_out[c, x] = kernel_out[c, x] + krecv[x, c]
        return carry

    [add_partner(x, 0) for x in range(width_x)]


def samples_kernel(nx, ny, local_ref, out_ref, sent, got_x, got_y, send_sem, recv_sem):
    me_p = lax.axis_index("pair")
    gx = lax.axis_index("gx")
    gy = lax.axis_index("gy")
    peers_x = [(me_p, (gx + d) % nx, gy) for d in range(1, nx)]
    peers_y = [(me_p, gx, (gy + d) % ny) for d in range(1, ny)]
    barrier = pltpu.get_barrier_semaphore()
    for dev in peers_x + peers_y:
        pl.semaphore_signal(barrier, 1, device_id=dev, device_id_type=MESH)
    pl.semaphore_wait(barrier, len(peers_x) + len(peers_y))
    rounds = ((local_ref, got_x, peers_x, 0), (sent, got_y, peers_y, nx - 1))
    total = local_ref[...]
    for src, got, peers, base in rounds:
        copies = []
        for i, dev in enumerate(peers):
            copy = pltpu.make_async_remote_copy(
                src_ref=src, dst_ref=got.at[i], send_sem=send_sem.at[base + i],
                recv_sem=recv_sem.at[base + i], device_id=dev, device_id_type=MESH,
            )
            copy.start()
            copies.append(copy)
        for copy in copies:
            copy.wait_send()
            copy.wait_recv()
        for i in range(len(peers)):
            total = total + got[i]
        if base == 0:
            sent[...] = total
    out_ref[...] = total


def gathered_samples(local_samples):
    nx, ny = lax.axis_size("gx"), lax.axis_size("gy")
    if nx < 2 or ny < 2:
        return lax.psum(local_samples, ("gx", "gy"))
    vmem = pl.BlockSpec(memory_space=pltpu.VMEM)
    return pl.pallas_call(
        functools.partial(samples_kernel, nx, ny),
        out_shape=jax.ShapeDtypeStruct(local_samples.shape, jnp.float32),
        in_specs=[vmem],
        out_specs=vmem,
        scratch_shapes=[
            pltpu.VMEM(local_samples.shape, jnp.float32),
            pltpu.VMEM((nx - 1,) + local_samples.shape, jnp.float32),
            pltpu.VMEM((ny - 1,) + local_samples.shape, jnp.float32),
            pltpu.SemaphoreType.DMA((nx + ny - 2,)),
            pltpu.SemaphoreType.DMA((nx + ny - 2,)),
        ],
        compiler_params=pltpu.CompilerParams(collective_id=1, has_side_effects=True),
    )(local_samples)


def shards(
    sound_speed_sq,
    wind_profile,
    forward_field,
    adjoint_state,
    pair_counts,
    source_cells,
    receiver_cells,
    residuals,
):
    steps_total = forward_field.shape[0]
    width_x, width_y, depth = sound_speed_sq.shape
    slots = residuals.shape[0]
    live = (jnp.arange(slots, dtype=jnp.int32) < pair_counts[0]).astype(jnp.float32)
    gx_first = lax.axis_index("gx") * width_x
    gy_first = lax.axis_index("gy") * width_y
    x_range = jnp.arange(width_x, dtype=jnp.int32)
    y_range = jnp.arange(width_y, dtype=jnp.int32)
    z_range = jnp.arange(depth, dtype=jnp.int32)

    def tile_mask(cells):
        on_x = (cells[:, 0][None, :] - gx_first) == x_range[:, None]
        on_y = (cells[:, 1][None, :] - gy_first) == y_range[:, None]
        return (on_x[:, None, :] & on_y[None, :, :]).astype(jnp.float32)

    source_z = (source_cells[:, 2][None, :] == z_range[:, None]).astype(jnp.bfloat16)
    along_z = jnp.einsum(
        "txyz,zn->txyn", forward_field[:, 0], source_z, preferred_element_type=jnp.float32
    )
    local_samples = jnp.sum(along_z * tile_mask(source_cells)[None], axis=(1, 2))
    samples = gathered_samples(local_samples)
    amplitude = jnp.transpose(residuals) * samples * live[None, :]
    spread = amplitude[:, None, None, :] * tile_mask(receiver_cells)[None]
    receiver_z = (receiver_cells[:, 2][:, None] == z_range[None, :]).astype(jnp.float32)
    injected = jnp.einsum(
        "txyn,nz->txyz", spread, receiver_z, precision=lax.Precision.HIGHEST,
        preferred_element_type=jnp.float32,
    )
    vmem = pl.BlockSpec(memory_space=pltpu.VMEM)
    kernel = functools.partial(
        stencil_kernel, lax.axis_size("gx"), lax.axis_size("gy"), steps_total
    )
    state_new, kernels = pl.pallas_call(
        kernel,
        out_shape=(
            jax.ShapeDtypeStruct((4, width_x, width_y, depth), jnp.float32),
            jax.ShapeDtypeStruct((4, width_x, width_y, depth // 2), jnp.float32),
        ),
        in_specs=[vmem] * 5,
        out_specs=(vmem, vmem),
        scratch_shapes=[
            pltpu.VMEM((2, 4, width_x + 2, width_y, depth), jnp.float32),
            pltpu.VMEM((width_x + 2, width_y, depth), jnp.float32),
            pltpu.VMEM((2, 2, 4, width_x, depth), jnp.float32),
            pltpu.VMEM((2, 2, 4, width_x, depth), jnp.float32),
            pltpu.VMEM((2, width_x, depth), jnp.float32),
            pltpu.VMEM((2, width_x, depth), jnp.float32),
            pltpu.VMEM((4, width_x, width_y, depth), jnp.float32),
            pltpu.VMEM((width_x, 4, width_y, depth // 2), jnp.float32),
            pltpu.VMEM((width_x, 4, width_y, depth // 2), jnp.float32),
            pltpu.VMEM((steps_total, 4, width_x + 2, width_y, depth), forward_field.dtype),
            pltpu.VMEM((2, steps_total, 2, 2 * width_x, depth), forward_field.dtype),
            pltpu.VMEM((2, steps_total, 2, 2 * width_x, depth), forward_field.dtype),
            pltpu.SemaphoreType.DMA((2, 4)),
            pltpu.SemaphoreType.DMA((2, 4)),
            pltpu.SemaphoreType.DMA((4,)),
            pltpu.SemaphoreType.DMA((4,)),
            pltpu.SemaphoreType.DMA((width_x,)),
            pltpu.SemaphoreType.DMA((width_x,)),
            pltpu.SemaphoreType.DMA((4,)),
            pltpu.SemaphoreType.DMA((4,)),
            pltpu.SemaphoreType.DMA((1,)),
        ],
        compiler_params=pltpu.CompilerParams(
            collective_id=0, has_side_effects=True, vmem_limit_bytes=48 * 1024 * 1024
        ),
    )(adjoint_state[0], sound_speed_sq, wind_profile, forward_field, injected)
    return (kernels, state_new[None])


def solution(mesh):
    in_specs = (
        P("gx", "gy", None),
        P(),
        P(None, None, "gx", "gy", None),
        P("pair", None, "gx", "gy", None),
        P("pair"),
        P("pair", None),
        P("pair", None),
        P("pair", None),
    )
    out_specs = (P(None, "gx", "gy", "pair"), P("pair", None, "gx", "gy", None))
    return jax.shard_map(shards, mesh=mesh, in_specs=in_specs, out_specs=out_specs, check_vma=False)
```

```python
import functools

import jax
import jax.numpy as jnp
from jax import lax
from jax.experimental import pallas as pl
from jax.experimental.pallas import tpu as pltpu
from jax.sharding import PartitionSpec as P

step_length = 0.25
Y_SLOT = (0, 2, 1, 3)
MESH = pl.DeviceIdType.MESH


def neighbours(shard, axis, dim):
    size, length = (lax.axis_size(axis), shard.shape[dim])
    up = [(i, i + 1) for i in range(size - 1)]
    down = [(i + 1, i) for i in range(size - 1)]
    last = lax.slice_in_dim(shard, length - 1, length, axis=dim)
    first = lax.slice_in_dim(shard, 0, 1, axis=dim)
    before = lax.ppermute(last, axis, up)
    after = lax.ppermute(first, axis, down)
    return (before, after)


def local_cells(cells, width_x, width_y):
    local_x = cells[:, 0] - lax.axis_index("gx") * width_x
    local_y = cells[:, 1] - lax.axis_index("gy") * width_y
    inside = (local_x >= 0) & (local_x < width_x) & (local_y >= 0) & (local_y < width_y)
    return (
        jnp.clip(local_x, 0, width_x - 1),
        jnp.clip(local_y, 0, width_y - 1),
        cells[:, 2],
        inside.astype(jnp.float32),
    )


def stencil_kernel(
    nx, ny, steps,
    state_in, sound, wind, forward, inj,
    state_out, kernel_out,
    pads, pbuf, ysend, yrecv, ypsend, yprecv, acc_out, ksend, krecv, fpad, fysend, fyr,
    ss, rs, ps, pr, ks, kr, fs, fr, local_sem,
):
    _, width_x, width_y, depth = state_in.shape
    me_p = lax.axis_index("pair")
    gx = lax.axis_index("gx")
    gy = lax.axis_index("gy")
    has_lo_x = gx > 0
    has_hi_x = gx < nx - 1
    has_lo_y = gy > 0
    has_hi_y = gy < ny - 1
    dev_lo_x = (me_p, gx - 1, gy)
    dev_hi_x = (me_p, gx + 1, gy)
    dev_lo_y = (me_p, gx, gy - 1)
    dev_hi_y = (me_p, gx, gy + 1)
    dev_pair = (1 - me_p, gx, gy)
    half = depth // 2

    zero_slab = jnp.zeros((width_y, depth), jnp.float32)
    for par in range(2):
        for c in range(4):
            pads[par, c, 0] = zero_slab
            pads[par, c, width_x + 1] = zero_slab
            for side in range(2):
                yrecv[par, side, c] = jnp.zeros((width_x, depth), jnp.float32)
    pbuf[0] = zero_slab
    pbuf[width_x + 1] = zero_slab
    zero_forward = jnp.zeros((width_y, depth), fpad.dtype)
    for t in range(steps):
        for c in range(4):
            fpad[t, c, 0] = zero_forward
            fpad[t, c, width_x + 1] = zero_forward
            for side in range(2):
                fyr[side, t, c // 2, pl.ds((c % 2) * width_x, width_x), :] = jnp.zeros((width_x, depth), fyr.dtype)

    def forward_rows(x, carry):
        for t in range(steps):
            for c in range(4):
                f = forward[t, c, x]
                row = (c % 2) * width_x + x
                fysend[0, t, c // 2, row:row + 1, :] = f[width_y - 1:width_y, :]
                fysend[1, t, c // 2, row:row + 1, :] = f[0:1, :]
        return carry

    [forward_rows(x, 0) for x in range(width_x)]
    interior = pltpu.make_async_copy(forward, fpad.at[:, :, pl.ds(1, width_x)], local_sem.at[0])
    interior.start()
    for side in range(2):
        yprecv[side] = jnp.zeros((width_x, depth), jnp.float32)

    barrier = pltpu.get_barrier_semaphore()
    pl.semaphore_signal(barrier, 1, device_id=dev_pair, device_id_type=MESH)
    for cond, dev in ((has_lo_x, dev_lo_x), (has_hi_x, dev_hi_x), (has_lo_y, dev_lo_y), (has_hi_y, dev_hi_y)):
        @pl.when(cond)
        def _():
            pl.semaphore_signal(barrier, 1, device_id=dev, device_id_type=MESH)
    peers = 1 + (
        (gx + nx - 1) // nx + (2 * nx - 2 - gx) // nx
        + (gy + ny - 1) // ny + (2 * ny - 2 - gy) // ny
    )
    pl.semaphore_wait(barrier, peers)

    iy = lax.broadcasted_iota(jnp.int32, (width_y, depth), 0)
    iz = lax.broadcasted_iota(jnp.int32, (width_y, depth), 1)
    we = wind[0:1, :]
    wn = wind[1:2, :]
    wv = wind[2:3, :]

    def dy(v, lo, hi):
        up = jnp.where(iy == width_y - 1, hi, pltpu.roll(v, width_y - 1, 0))
        down = jnp.where(iy == 0, lo, pltpu.roll(v, 1, 0))
        return (up - down) * 0.5

    def dz(v):
        up = jnp.where(iz == depth - 1, 0.0, pltpu.roll(v, depth - 1, 1))
        down = jnp.where(iz == 0, 0.0, pltpu.roll(v, 1, 1))
        return (up - down) * 0.5

    def exchange(src_lo_x, src_hi_x, dst_lo_x, dst_hi_x, src_y_hi, src_y_lo, dst_y_lo, dst_y_hi, send, recv):
        outs = (
            (has_hi_x, src_hi_x, dst_lo_x, 0, dev_hi_x),
            (has_lo_x, src_lo_x, dst_hi_x, 1, dev_lo_x),
            (has_hi_y, src_y_hi, dst_y_lo, 2, dev_hi_y),
            (has_lo_y, src_y_lo, dst_y_hi, 3, dev_lo_y),
        )
        copies = []
        for cond, src, dst, slot, dev in outs:
            copy = pltpu.make_async_remote_copy(
                src_ref=src, dst_ref=dst, send_sem=send.at[slot], recv_sem=recv.at[slot],
                device_id=dev, device_id_type=MESH,
            )
            copies.append((cond, copy))

            @pl.when(cond)
            def _():
                copy.start()
        return copies

    def settle(copies):
        incoming = (has_lo_x, has_hi_x, has_lo_y, has_hi_y)
        for (cond, copy), arrives in zip(copies, incoming):
            @pl.when(cond)
            def _():
                copy.wait_send()

            @pl.when(arrives)
            def _():
                copy.wait_recv()

    def fill_state(par, x, c, v):
        pads[par, c, x + 1] = v
        ysend[par, 0, Y_SLOT[c], x:x + 1, :] = v[width_y - 1:width_y, :]
        ysend[par, 1, Y_SLOT[c], x:x + 1, :] = v[0:1, :]

    def copy_in(x, carry):
        for c in range(4):
            fill_state(0, x, c, state_in[c, x])
        return carry

    [copy_in(x, 0) for x in range(width_x)]
    forward_copies = exchange(
        forward.at[:, :, pl.ds(0, 1)], forward.at[:, :, pl.ds(width_x - 1, 1)],
        fpad.at[:, :, pl.ds(0, 1)], fpad.at[:, :, pl.ds(width_x + 1, 1)],
        fysend.at[0], fysend.at[1], fyr.at[0], fyr.at[1], fs, fr,
    )

    def increment_slab(x, carry, get, snap, first, last):
        xp = x + 1
        p_new = get(0, x)
        a_new = [get(1 + i, x) for i in range(3)]
        fe, fn, fu = [], [], []
        for c in range(4):
            f = fpad[snap, c, xp].astype(jnp.float32)
            fe.append((fpad[snap, c, xp + 1].astype(jnp.float32) - fpad[snap, c, x].astype(jnp.float32)) * 0.5)
            row = (c % 2) * width_x + x
            fn.append(dy(f, fyr[0, snap, c // 2, row:row + 1, :].astype(jnp.float32),
                         fyr[1, snap, c // 2, row:row + 1, :].astype(jnp.float32)))
            fu.append(dz(f))
        pieces = [p_new * (fe[1] + fn[2] + fu[3])]
        for along in (fe, fn, fu):
            pieces.append(p_new * along[0] + a_new[0] * along[1] + a_new[1] * along[2] + a_new[2] * along[3])
        for c in range(4):
            total = pieces[c] if first else acc_out[c, x] + pieces[c]
            if not last:
                acc_out[c, x] = total
                continue
            low, high = total[:, :half], total[:, half:]
            kernel_out[c, x] = jnp.where(me_p == 0, low, high)
            ksend[x, c] = jnp.where(me_p == 0, high, low)
        if last:
            pltpu.make_async_remote_copy(
                src_ref=ksend.at[x], dst_ref=krecv.at[x], send_sem=ks.at[x], recv_sem=kr.at[x],
                device_id=dev_pair, device_id_type=MESH,
            ).start()
        return carry

    def forward_ready():
        interior.wait()
        settle(forward_copies)

    for step in range(steps):
        par = step % 2
        nxt = 1 - par
        snap = steps - 1 - step
        last = step == steps - 1
        halves = []
        for part in range(2):
            comps = pl.ds(2 * part, 2)
            halves.append(exchange(
                pads.at[par, comps, pl.ds(1, 1)], pads.at[par, comps, pl.ds(width_x, 1)],
                pads.at[par, comps, pl.ds(0, 1)], pads.at[par, comps, pl.ds(width_x + 1, 1)],
                ysend.at[par, 0, comps], ysend.at[par, 1, comps],
                yrecv.at[par, 0, comps], yrecv.at[par, 1, comps],
                ss.at[par, part], rs.at[par, part],
            ))
        state_copies, velocity_copies = halves
        if step > 0:
            if step == 1:
                forward_ready()
            [(functools.partial(
                increment_slab, get=lambda c, x, par=par: pads[par, c, x + 1],
                snap=snap + 1, first=step == 1, last=False))(x, 0) for x in range(width_x)]
        settle(state_copies)

        def pressure_slab(x, carry, par=par, snap=snap):
            xp = x + 1
            old = pads.at[par]
            p = old[0, xp]
            dxp = (old[0, xp + 1] - old[0, x]) * 0.5
            dxa = (old[1, xp + 1] - old[1, x]) * 0.5
            dyp = dy(p, yrecv[par, 0, Y_SLOT[0], x:x + 1, :], yrecv[par, 1, Y_SLOT[0], x:x + 1, :])
            dya = dy(old[2, xp], yrecv[par, 0, Y_SLOT[2], x:x + 1, :], yrecv[par, 1, Y_SLOT[2], x:x + 1, :])
            dzp = dz(p)
            dza = dz(old[3, xp])
            divergence = dxa + dya + dza
            p_new = (
                p
                + step_length * (sound[x] * divergence + we * dxp + wn * dyp + wv * dzp)
                + inj[snap, x]
            )
            pbuf[xp] = p_new
            ypsend[0, x:x + 1, :] = p_new[width_y - 1:width_y, :]
            ypsend[1, x:x + 1, :] = p_new[0:1, :]
            return carry

        [pressure_slab(x, 0) for x in range(width_x)]
        settle(exchange(
            pbuf.at[pl.ds(1, 1)], pbuf.at[pl.ds(width_x, 1)],
            pbuf.at[pl.ds(0, 1)], pbuf.at[pl.ds(width_x + 1, 1)],
            ypsend.at[0], ypsend.at[1], yprecv.at[0], yprecv.at[1],
            ps, pr,
        ))

        settle(velocity_copies)

        def velocity_slab(x, carry, par=par, nxt=nxt, last=last):
            xp = x + 1
            old = pads.at[par]
            p_new = pbuf[xp]
            grad = (
                (pbuf[xp + 1] - pbuf[x]) * 0.5,
                dy(p_new, yprecv[0, x:x + 1, :], yprecv[1, x:x + 1, :]),
                dz(p_new),
            )
            new_state = [p_new]
            for i in range(3):
                a = old[1 + i, xp]
                dxa = (old[1 + i, xp + 1] - old[1 + i, x]) * 0.5
                dya = dy(a, yrecv[par, 0, Y_SLOT[1 + i], x:x + 1, :], yrecv[par, 1, Y_SLOT[1 + i], x:x + 1, :])
                dza = dz(a)
                new_state.append(a + step_length * (grad[i] + we * dxa + wn * dya + wv * dza))
            for c in range(4):
                if last:
                    state_out[c, x] = new_state[c]
                else:
                    fill_state(nxt, x, c, new_state[c])
            return carry

        [velocity_slab(x, 0) for x in range(width_x)]

    if steps == 1:
        forward_ready()
    [(functools.partial(
        increment_slab, get=lambda c, x: state_out[c, x], snap=0, first=steps == 1, last=True))(x, 0) for x in range(width_x)]

    for x in range(width_x):
        copy = pltpu.make_async_remote_copy(
            src_ref=ksend.at[x], dst_ref=krecv.at[x], send_sem=ks.at[x], recv_sem=kr.at[x],
            device_id=dev_pair, device_id_type=MESH,
        )
        copy.wait_send()
        copy.wait_recv()

    def add_partner(x, carry):
        for c in range(4):
            kernel_out[c, x] = kernel_out[c, x] + krecv[x, c]
        return carry

    [add_partner(x, 0) for x in range(width_x)]


def samples_kernel(nx, ny, local_ref, out_ref, sent, got_x, got_y, send_sem, recv_sem):
    me_p = lax.axis_index("pair")
    gx = lax.axis_index("gx")
    gy = lax.axis_index("gy")
    peers_x = [(me_p, (gx + d) % nx, gy) for d in range(1, nx)]
    peers_y = [(me_p, gx, (gy + d) % ny) for d in range(1, ny)]
    barrier = pltpu.get_barrier_semaphore()
    for dev in peers_x + peers_y:
        pl.semaphore_signal(barrier, 1, device_id=dev, device_id_type=MESH)
    pl.semaphore_wait(barrier, len(peers_x) + len(peers_y))
    rounds = ((local_ref, got_x, peers_x, 0), (sent, got_y, peers_y, nx - 1))
    total = local_ref[...]
    for src, got, peers, base in rounds:
        copies = []
        for i, dev in enumerate(peers):
            copy = pltpu.make_async_remote_copy(
                src_ref=src, dst_ref=got.at[i], send_sem=send_sem.at[base + i],
                recv_sem=recv_sem.at[base + i], device_id=dev, device_id_type=MESH,
            )
            copy.start()
            copies.append(copy)
        for copy in copies:
            copy.wait_send()
            copy.wait_recv()
        for i in range(len(peers)):
            total = total + got[i]
        if base == 0:
            sent[...] = total
    out_ref[...] = total


def gathered_samples(local_samples):
    nx, ny = lax.axis_size("gx"), lax.axis_size("gy")
    if nx < 2 or ny < 2:
        return lax.psum(local_samples, ("gx", "gy"))
    vmem = pl.BlockSpec(memory_space=pltpu.VMEM)
    return pl.pallas_call(
        functools.partial(samples_kernel, nx, ny),
        out_shape=jax.ShapeDtypeStruct(local_samples.shape, jnp.float32),
        in_specs=[vmem],
        out_specs=vmem,
        scratch_shapes=[
            pltpu.VMEM(local_samples.shape, jnp.float32),
            pltpu.VMEM((nx - 1,) + local_samples.shape, jnp.float32),
            pltpu.VMEM((ny - 1,) + local_samples.shape, jnp.float32),
            pltpu.SemaphoreType.DMA((nx + ny - 2,)),
            pltpu.SemaphoreType.DMA((nx + ny - 2,)),
        ],
        compiler_params=pltpu.CompilerParams(collective_id=1, has_side_effects=True),
    )(local_samples)


def shards(
    sound_speed_sq,
    wind_profile,
    forward_field,
    adjoint_state,
    pair_counts,
    source_cells,
    receiver_cells,
    residuals,
):
    steps_total = forward_field.shape[0]
    width_x, width_y, depth = sound_speed_sq.shape
    slots = residuals.shape[0]
    live = (jnp.arange(slots, dtype=jnp.int32) < pair_counts[0]).astype(jnp.float32)
    gx_first = lax.axis_index("gx") * width_x
    gy_first = lax.axis_index("gy") * width_y
    x_range = jnp.arange(width_x, dtype=jnp.int32)
    y_range = jnp.arange(width_y, dtype=jnp.int32)
    z_range = jnp.arange(depth, dtype=jnp.int32)

    def tile_mask(cells):
        on_x = (cells[:, 0][None, :] - gx_first) == x_range[:, None]
        on_y = (cells[:, 1][None, :] - gy_first) == y_range[:, None]
        return (on_x[:, None, :] & on_y[None, :, :]).astype(jnp.float32)

    source_z = (source_cells[:, 2][None, :] == z_range[:, None]).astype(jnp.bfloat16)
    along_z = jnp.einsum(
        "txyz,zn->txyn", forward_field[:, 0], source_z, preferred_element_type=jnp.float32
    )
    local_samples = jnp.sum(along_z * tile_mask(source_cells)[None], axis=(1, 2))
    samples = gathered_samples(local_samples)
    amplitude = jnp.transpose(residuals) * samples * live[None, :]
    spread = amplitude[:, None, None, :] * tile_mask(receiver_cells)[None]
    receiver_z = (receiver_cells[:, 2][:, None] == z_range[None, :]).astype(jnp.float32)
    injected = jnp.einsum(
        "txyn,nz->txyz", spread, receiver_z, precision=lax.Precision.HIGHEST,
        preferred_element_type=jnp.float32,
    )
    vmem = pl.BlockSpec(memory_space=pltpu.VMEM)
    kernel = functools.partial(
        stencil_kernel, lax.axis_size("gx"), lax.axis_size("gy"), steps_total
    )
    state_new, kernels = pl.pallas_call(
        kernel,
        out_shape=(
            jax.ShapeDtypeStruct((4, width_x, width_y, depth), jnp.float32),
            jax.ShapeDtypeStruct((4, width_x, width_y, depth // 2), jnp.float32),
        ),
        in_specs=[vmem] * 5,
        out_specs=(vmem, vmem),
        scratch_shapes=[
            pltpu.VMEM((2, 4, width_x + 2, width_y, depth), jnp.float32),
            pltpu.VMEM((width_x + 2, width_y, depth), jnp.float32),
            pltpu.VMEM((2, 2, 4, width_x, depth), jnp.float32),
            pltpu.VMEM((2, 2, 4, width_x, depth), jnp.float32),
            pltpu.VMEM((2, width_x, depth), jnp.float32),
            pltpu.VMEM((2, width_x, depth), jnp.float32),
            pltpu.VMEM((4, width_x, width_y, depth), jnp.float32),
            pltpu.VMEM((width_x, 4, width_y, depth // 2), jnp.float32),
            pltpu.VMEM((width_x, 4, width_y, depth // 2), jnp.float32),
            pltpu.VMEM((steps_total, 4, width_x + 2, width_y, depth), forward_field.dtype),
            pltpu.VMEM((2, steps_total, 2, 2 * width_x, depth), forward_field.dtype),
            pltpu.VMEM((2, steps_total, 2, 2 * width_x, depth), forward_field.dtype),
            pltpu.SemaphoreType.DMA((2, 2, 4)),
            pltpu.SemaphoreType.DMA((2, 2, 4)),
            pltpu.SemaphoreType.DMA((4,)),
            pltpu.SemaphoreType.DMA((4,)),
            pltpu.SemaphoreType.DMA((width_x,)),
            pltpu.SemaphoreType.DMA((width_x,)),
            pltpu.SemaphoreType.DMA((4,)),
            pltpu.SemaphoreType.DMA((4,)),
            pltpu.SemaphoreType.DMA((1,)),
        ],
        compiler_params=pltpu.CompilerParams(
            collective_id=0, has_side_effects=True, vmem_limit_bytes=48 * 1024 * 1024
        ),
    )(adjoint_state[0], sound_speed_sq, wind_profile, forward_field, injected)
    return (kernels, state_new[None])


def solution(mesh):
    in_specs = (
        P("gx", "gy", None),
        P(),
        P(None, None, "gx", "gy", None),
        P("pair", None, "gx", "gy", None),
        P("pair"),
        P("pair", None),
        P("pair", None),
        P("pair", None),
    )
    out_specs = (P(None, "gx", "gy", "pair"), P("pair", None, "gx", "gy", None))
    return jax.shard_map(shards, mesh=mesh, in_specs=in_specs, out_specs=out_specs, check_vma=False)
```

```python
import functools

import jax
import jax.numpy as jnp
from jax import lax
from jax.experimental import pallas as pl
from jax.experimental.pallas import tpu as pltpu
from jax.sharding import PartitionSpec as P

step_length = 0.25
Y_SLOT = (0, 2, 1, 3)
MESH = pl.DeviceIdType.MESH


def neighbours(shard, axis, dim):
    size, length = (lax.axis_size(axis), shard.shape[dim])
    up = [(i, i + 1) for i in range(size - 1)]
    down = [(i + 1, i) for i in range(size - 1)]
    last = lax.slice_in_dim(shard, length - 1, length, axis=dim)
    first = lax.slice_in_dim(shard, 0, 1, axis=dim)
    before = lax.ppermute(last, axis, up)
    after = lax.ppermute(first, axis, down)
    return (before, after)


def local_cells(cells, width_x, width_y):
    local_x = cells[:, 0] - lax.axis_index("gx") * width_x
    local_y = cells[:, 1] - lax.axis_index("gy") * width_y
    inside = (local_x >= 0) & (local_x < width_x) & (local_y >= 0) & (local_y < width_y)
    return (
        jnp.clip(local_x, 0, width_x - 1),
        jnp.clip(local_y, 0, width_y - 1),
        cells[:, 2],
        inside.astype(jnp.float32),
    )


def stencil_kernel(
    nx, ny, steps,
    state_in, sound, wind, forward, inj,
    state_out, kernel_out,
    pads, pbuf, ysend, yrecv, ypsend, yprecv, acc_out, ksend, krecv, fpad, fysend, fyr,
    ss, rs, ps, pr, ks, kr, fs, fr, local_sem,
):
    _, width_x, width_y, depth = state_in.shape
    me_p = lax.axis_index("pair")
    gx = lax.axis_index("gx")
    gy = lax.axis_index("gy")
    has_lo_x = gx > 0
    has_hi_x = gx < nx - 1
    has_lo_y = gy > 0
    has_hi_y = gy < ny - 1
    dev_lo_x = (me_p, gx - 1, gy)
    dev_hi_x = (me_p, gx + 1, gy)
    dev_lo_y = (me_p, gx, gy - 1)
    dev_hi_y = (me_p, gx, gy + 1)
    dev_pair = (1 - me_p, gx, gy)
    half = depth // 2

    zero_slab = jnp.zeros((width_y, depth), jnp.float32)
    for par in range(2):
        for c in range(4):
            pads[par, c, 0] = zero_slab
            pads[par, c, width_x + 1] = zero_slab
            for side in range(2):
                yrecv[par, side, c] = jnp.zeros((width_x, depth), jnp.float32)
    for par in range(2):
        pbuf[par, 0] = zero_slab
        pbuf[par, width_x + 1] = zero_slab
    zero_forward = jnp.zeros((width_y, depth), fpad.dtype)
    for t in range(steps):
        for c in range(4):
            fpad[t, c, 0] = zero_forward
            fpad[t, c, width_x + 1] = zero_forward
            for side in range(2):
                fyr[side, t, c // 2, pl.ds((c % 2) * width_x, width_x), :] = jnp.zeros((width_x, depth), fyr.dtype)

    def forward_rows(x, carry):
        for t in range(steps):
            for c in range(4):
                f = forward[t, c, x]
                row = (c % 2) * width_x + x
                fysend[0, t, c // 2, row:row + 1, :] = f[width_y - 1:width_y, :]
                fysend[1, t, c // 2, row:row + 1, :] = f[0:1, :]
        return carry

    [forward_rows(x, 0) for x in range(width_x)]
    interior = pltpu.make_async_copy(forward, fpad.at[:, :, pl.ds(1, width_x)], local_sem.at[0])
    interior.start()
    for par in range(2):
        for side in range(2):
            yprecv[par, side] = jnp.zeros((width_x, depth), jnp.float32)

    barrier = pltpu.get_barrier_semaphore()
    pl.semaphore_signal(barrier, 1, device_id=dev_pair, device_id_type=MESH)
    for cond, dev in ((has_lo_x, dev_lo_x), (has_hi_x, dev_hi_x), (has_lo_y, dev_lo_y), (has_hi_y, dev_hi_y)):
        @pl.when(cond)
        def _():
            pl.semaphore_signal(barrier, 1, device_id=dev, device_id_type=MESH)
    peers = 1 + (
        (gx + nx - 1) // nx + (2 * nx - 2 - gx) // nx
        + (gy + ny - 1) // ny + (2 * ny - 2 - gy) // ny
    )
    pl.semaphore_wait(barrier, peers)

    iy = lax.broadcasted_iota(jnp.int32, (width_y, depth), 0)
    iz = lax.broadcasted_iota(jnp.int32, (width_y, depth), 1)
    we = wind[0:1, :]
    wn = wind[1:2, :]
    wv = wind[2:3, :]

    def dy(v, lo, hi):
        up = jnp.where(iy == width_y - 1, hi, pltpu.roll(v, width_y - 1, 0))
        down = jnp.where(iy == 0, lo, pltpu.roll(v, 1, 0))
        return (up - down) * 0.5

    def dz(v):
        up = jnp.where(iz == depth - 1, 0.0, pltpu.roll(v, depth - 1, 1))
        down = jnp.where(iz == 0, 0.0, pltpu.roll(v, 1, 1))
        return (up - down) * 0.5

    def exchange(src_lo_x, src_hi_x, dst_lo_x, dst_hi_x, src_y_hi, src_y_lo, dst_y_lo, dst_y_hi, send, recv):
        outs = (
            (has_hi_x, src_hi_x, dst_lo_x, 0, dev_hi_x),
            (has_lo_x, src_lo_x, dst_hi_x, 1, dev_lo_x),
            (has_hi_y, src_y_hi, dst_y_lo, 2, dev_hi_y),
            (has_lo_y, src_y_lo, dst_y_hi, 3, dev_lo_y),
        )
        copies = []
        for cond, src, dst, slot, dev in outs:
            copy = pltpu.make_async_remote_copy(
                src_ref=src, dst_ref=dst, send_sem=send.at[slot], recv_sem=recv.at[slot],
                device_id=dev, device_id_type=MESH,
            )
            copies.append((cond, copy))

            @pl.when(cond)
            def _():
                copy.start()
        return copies

    def settle(copies):
        incoming = (has_lo_x, has_hi_x, has_lo_y, has_hi_y)
        for (cond, copy), arrives in zip(copies, incoming):
            @pl.when(cond)
            def _():
                copy.wait_send()

            @pl.when(arrives)
            def _():
                copy.wait_recv()

    def fill_state(par, x, c, v):
        pads[par, c, x + 1] = v
        ysend[par, 0, Y_SLOT[c], x:x + 1, :] = v[width_y - 1:width_y, :]
        ysend[par, 1, Y_SLOT[c], x:x + 1, :] = v[0:1, :]

    def copy_in(x, carry):
        for c in range(4):
            fill_state(0, x, c, state_in[c, x])
        return carry

    [copy_in(x, 0) for x in range(width_x)]
    forward_copies = exchange(
        forward.at[:, :, pl.ds(0, 1)], forward.at[:, :, pl.ds(width_x - 1, 1)],
        fpad.at[:, :, pl.ds(0, 1)], fpad.at[:, :, pl.ds(width_x + 1, 1)],
        fysend.at[0], fysend.at[1], fyr.at[0], fyr.at[1], fs, fr,
    )

    def increment_slab(x, carry, get, snap, first, last):
        xp = x + 1
        p_new = get(0, x)
        a_new = [get(1 + i, x) for i in range(3)]
        fe, fn, fu = [], [], []
        for c in range(4):
            f = fpad[snap, c, xp].astype(jnp.float32)
            fe.append((fpad[snap, c, xp + 1].astype(jnp.float32) - fpad[snap, c, x].astype(jnp.float32)) * 0.5)
            row = (c % 2) * width_x + x
            fn.append(dy(f, fyr[0, snap, c // 2, row:row + 1, :].astype(jnp.float32),
                         fyr[1, snap, c // 2, row:row + 1, :].astype(jnp.float32)))
            fu.append(dz(f))
        pieces = [p_new * (fe[1] + fn[2] + fu[3])]
        for along in (fe, fn, fu):
            pieces.append(p_new * along[0] + a_new[0] * along[1] + a_new[1] * along[2] + a_new[2] * along[3])
        for c in range(4):
            total = pieces[c] if first else acc_out[c, x] + pieces[c]
            if not last:
                acc_out[c, x] = total
                continue
            low, high = total[:, :half], total[:, half:]
            kernel_out[c, x] = jnp.where(me_p == 0, low, high)
            ksend[x, c] = jnp.where(me_p == 0, high, low)
        if last:
            pltpu.make_async_remote_copy(
                src_ref=ksend.at[x], dst_ref=krecv.at[x], send_sem=ks.at[x], recv_sem=kr.at[x],
                device_id=dev_pair, device_id_type=MESH,
            ).start()
        return carry

    def forward_ready():
        interior.wait()
        settle(forward_copies)

    for step in range(steps):
        par = step % 2
        nxt = 1 - par
        snap = steps - 1 - step
        last = step == steps - 1
        halves = []
        for part in range(2):
            comps = pl.ds(2 * part, 2) if (part or step == 0) else pl.ds(1, 1)
            halves.append(exchange(
                pads.at[par, comps, pl.ds(1, 1)], pads.at[par, comps, pl.ds(width_x, 1)],
                pads.at[par, comps, pl.ds(0, 1)], pads.at[par, comps, pl.ds(width_x + 1, 1)],
                ysend.at[par, 0, comps], ysend.at[par, 1, comps],
                yrecv.at[par, 0, comps], yrecv.at[par, 1, comps],
                ss.at[par, part], rs.at[par, part],
            ))
        state_copies, velocity_copies = halves
        if step > 0:
            if step == 1:
                forward_ready()
            [(functools.partial(
                increment_slab, get=lambda c, x, par=par: pads[par, c, x + 1],
                snap=snap + 1, first=step == 1, last=False))(x, 0) for x in range(width_x)]
        settle(state_copies)

        def pressure_slab(x, carry, par=par, snap=snap, step=step):
            xp = x + 1
            old = pads.at[par]
            if step == 0:
                p = old[0, xp]
                dxp = (old[0, xp + 1] - old[0, x]) * 0.5
                dyp = dy(p, yrecv[par, 0, Y_SLOT[0], x:x + 1, :], yrecv[par, 1, Y_SLOT[0], x:x + 1, :])
            else:
                held = pbuf.at[1 - par]
                p = held[xp]
                dxp = (held[xp + 1] - held[x]) * 0.5
                dyp = dy(p, yprecv[1 - par, 0, x:x + 1, :], yprecv[1 - par, 1, x:x + 1, :])
            dxa = (old[1, xp + 1] - old[1, x]) * 0.5
            dya = dy(old[2, xp], yrecv[par, 0, Y_SLOT[2], x:x + 1, :], yrecv[par, 1, Y_SLOT[2], x:x + 1, :])
            dzp = dz(p)
            dza = dz(old[3, xp])
            divergence = dxa + dya + dza
            p_new = (
                p
                + step_length * (sound[x] * divergence + we * dxp + wn * dyp + wv * dzp)
                + inj[snap, x]
            )
            pbuf[par, xp] = p_new
            ypsend[0, x:x + 1, :] = p_new[width_y - 1:width_y, :]
            ypsend[1, x:x + 1, :] = p_new[0:1, :]
            return carry

        [pressure_slab(x, 0) for x in range(width_x)]
        settle(exchange(
            pbuf.at[par, pl.ds(1, 1)], pbuf.at[par, pl.ds(width_x, 1)],
            pbuf.at[par, pl.ds(0, 1)], pbuf.at[par, pl.ds(width_x + 1, 1)],
            ypsend.at[0], ypsend.at[1], yprecv.at[par, 0], yprecv.at[par, 1],
            ps, pr,
        ))

        settle(velocity_copies)

        def velocity_slab(x, carry, par=par, nxt=nxt, last=last):
            xp = x + 1
            old = pads.at[par]
            p_new = pbuf[par, xp]
            grad = (
                (pbuf[par, xp + 1] - pbuf[par, x]) * 0.5,
                dy(p_new, yprecv[par, 0, x:x + 1, :], yprecv[par, 1, x:x + 1, :]),
                dz(p_new),
            )
            new_state = [p_new]
            for i in range(3):
                a = old[1 + i, xp]
                dxa = (old[1 + i, xp + 1] - old[1 + i, x]) * 0.5
                dya = dy(a, yrecv[par, 0, Y_SLOT[1 + i], x:x + 1, :], yrecv[par, 1, Y_SLOT[1 + i], x:x + 1, :])
                dza = dz(a)
                new_state.append(a + step_length * (grad[i] + we * dxa + wn * dya + wv * dza))
            for c in range(4):
                if last:
                    state_out[c, x] = new_state[c]
                else:
                    fill_state(nxt, x, c, new_state[c])
            return carry

        [velocity_slab(x, 0) for x in range(width_x)]

    if steps == 1:
        forward_ready()
    [(functools.partial(
        increment_slab, get=lambda c, x: state_out[c, x], snap=0, first=steps == 1, last=True))(x, 0) for x in range(width_x)]

    for x in range(width_x):
        copy = pltpu.make_async_remote_copy(
            src_ref=ksend.at[x], dst_ref=krecv.at[x], send_sem=ks.at[x], recv_sem=kr.at[x],
            device_id=dev_pair, device_id_type=MESH,
        )
        copy.wait_send()
        copy.wait_recv()

    def add_partner(x, carry):
        for c in range(4):
            kernel_out[c, x] = kernel_out[c, x] + krecv[x, c]
        return carry

    [add_partner(x, 0) for x in range(width_x)]


def samples_kernel(nx, ny, local_ref, out_ref, sent, got_x, got_y, send_sem, recv_sem):
    me_p = lax.axis_index("pair")
    gx = lax.axis_index("gx")
    gy = lax.axis_index("gy")
    peers_x = [(me_p, (gx + d) % nx, gy) for d in range(1, nx)]
    peers_y = [(me_p, gx, (gy + d) % ny) for d in range(1, ny)]
    barrier = pltpu.get_barrier_semaphore()
    for dev in peers_x + peers_y:
        pl.semaphore_signal(barrier, 1, device_id=dev, device_id_type=MESH)
    pl.semaphore_wait(barrier, len(peers_x) + len(peers_y))
    rounds = ((local_ref, got_x, peers_x, 0), (sent, got_y, peers_y, nx - 1))
    total = local_ref[...]
    for src, got, peers, base in rounds:
        copies = []
        for i, dev in enumerate(peers):
            copy = pltpu.make_async_remote_copy(
                src_ref=src, dst_ref=got.at[i], send_sem=send_sem.at[base + i],
                recv_sem=recv_sem.at[base + i], device_id=dev, device_id_type=MESH,
            )
            copy.start()
            copies.append(copy)
        for copy in copies:
            copy.wait_send()
            copy.wait_recv()
        for i in range(len(peers)):
            total = total + got[i]
        if base == 0:
            sent[...] = total
    out_ref[...] = total


def gathered_samples(local_samples):
    nx, ny = lax.axis_size("gx"), lax.axis_size("gy")
    if nx < 2 or ny < 2:
        return lax.psum(local_samples, ("gx", "gy"))
    vmem = pl.BlockSpec(memory_space=pltpu.VMEM)
    return pl.pallas_call(
        functools.partial(samples_kernel, nx, ny),
        out_shape=jax.ShapeDtypeStruct(local_samples.shape, jnp.float32),
        in_specs=[vmem],
        out_specs=vmem,
        scratch_shapes=[
            pltpu.VMEM(local_samples.shape, jnp.float32),
            pltpu.VMEM((nx - 1,) + local_samples.shape, jnp.float32),
            pltpu.VMEM((ny - 1,) + local_samples.shape, jnp.float32),
            pltpu.SemaphoreType.DMA((nx + ny - 2,)),
            pltpu.SemaphoreType.DMA((nx + ny - 2,)),
        ],
        compiler_params=pltpu.CompilerParams(collective_id=1, has_side_effects=True),
    )(local_samples)


def shards(
    sound_speed_sq,
    wind_profile,
    forward_field,
    adjoint_state,
    pair_counts,
    source_cells,
    receiver_cells,
    residuals,
):
    steps_total = forward_field.shape[0]
    width_x, width_y, depth = sound_speed_sq.shape
    slots = residuals.shape[0]
    live = (jnp.arange(slots, dtype=jnp.int32) < pair_counts[0]).astype(jnp.float32)
    gx_first = lax.axis_index("gx") * width_x
    gy_first = lax.axis_index("gy") * width_y
    x_range = jnp.arange(width_x, dtype=jnp.int32)
    y_range = jnp.arange(width_y, dtype=jnp.int32)
    z_range = jnp.arange(depth, dtype=jnp.int32)

    def tile_mask(cells):
        on_x = (cells[:, 0][None, :] - gx_first) == x_range[:, None]
        on_y = (cells[:, 1][None, :] - gy_first) == y_range[:, None]
        return (on_x[:, None, :] & on_y[None, :, :]).astype(jnp.float32)

    source_z = (source_cells[:, 2][None, :] == z_range[:, None]).astype(jnp.bfloat16)
    along_z = jnp.einsum(
        "txyz,zn->txyn", forward_field[:, 0], source_z, preferred_element_type=jnp.float32
    )
    local_samples = jnp.sum(along_z * tile_mask(source_cells)[None], axis=(1, 2))
    samples = gathered_samples(local_samples)
    amplitude = jnp.transpose(residuals) * samples * live[None, :]
    spread = amplitude[:, None, None, :] * tile_mask(receiver_cells)[None]
    receiver_z = (receiver_cells[:, 2][:, None] == z_range[None, :]).astype(jnp.float32)
    injected = jnp.einsum(
        "txyn,nz->txyz", spread, receiver_z, precision=lax.Precision.HIGHEST,
        preferred_element_type=jnp.float32,
    )
    vmem = pl.BlockSpec(memory_space=pltpu.VMEM)
    kernel = functools.partial(
        stencil_kernel, lax.axis_size("gx"), lax.axis_size("gy"), steps_total
    )
    state_new, kernels = pl.pallas_call(
        kernel,
        out_shape=(
            jax.ShapeDtypeStruct((4, width_x, width_y, depth), jnp.float32),
            jax.ShapeDtypeStruct((4, width_x, width_y, depth // 2), jnp.float32),
        ),
        in_specs=[vmem] * 5,
        out_specs=(vmem, vmem),
        scratch_shapes=[
            pltpu.VMEM((2, 4, width_x + 2, width_y, depth), jnp.float32),
            pltpu.VMEM((2, width_x + 2, width_y, depth), jnp.float32),
            pltpu.VMEM((2, 2, 4, width_x, depth), jnp.float32),
            pltpu.VMEM((2, 2, 4, width_x, depth), jnp.float32),
            pltpu.VMEM((2, width_x, depth), jnp.float32),
            pltpu.VMEM((2, 2, width_x, depth), jnp.float32),
            pltpu.VMEM((4, width_x, width_y, depth), jnp.float32),
            pltpu.VMEM((width_x, 4, width_y, depth // 2), jnp.float32),
            pltpu.VMEM((width_x, 4, width_y, depth // 2), jnp.float32),
            pltpu.VMEM((steps_total, 4, width_x + 2, width_y, depth), forward_field.dtype),
            pltpu.VMEM((2, steps_total, 2, 2 * width_x, depth), forward_field.dtype),
            pltpu.VMEM((2, steps_total, 2, 2 * width_x, depth), forward_field.dtype),
            pltpu.SemaphoreType.DMA((2, 2, 4)),
            pltpu.SemaphoreType.DMA((2, 2, 4)),
            pltpu.SemaphoreType.DMA((4,)),
            pltpu.SemaphoreType.DMA((4,)),
            pltpu.SemaphoreType.DMA((width_x,)),
            pltpu.SemaphoreType.DMA((width_x,)),
            pltpu.SemaphoreType.DMA((4,)),
            pltpu.SemaphoreType.DMA((4,)),
            pltpu.SemaphoreType.DMA((1,)),
        ],
        compiler_params=pltpu.CompilerParams(
            collective_id=0, has_side_effects=True, vmem_limit_bytes=48 * 1024 * 1024
        ),
    )(adjoint_state[0], sound_speed_sq, wind_profile, forward_field, injected)
    return (kernels, state_new[None])


def solution(mesh):
    in_specs = (
        P("gx", "gy", None),
        P(),
        P(None, None, "gx", "gy", None),
        P("pair", None, "gx", "gy", None),
        P("pair"),
        P("pair", None),
        P("pair", None),
        P("pair", None),
    )
    out_specs = (P(None, "gx", "gy", "pair"), P("pair", None, "gx", "gy", None))
    return jax.shard_map(shards, mesh=mesh, in_specs=in_specs, out_specs=out_specs, check_vma=False)
```

```python
import functools

import jax
import jax.numpy as jnp
from jax import lax
from jax.experimental import pallas as pl
from jax.experimental.pallas import tpu as pltpu
from jax.sharding import PartitionSpec as P

step_length = 0.25
Y_SLOT = (0, 2, 1, 3)
MESH = pl.DeviceIdType.MESH


def neighbours(shard, axis, dim):
    size, length = (lax.axis_size(axis), shard.shape[dim])
    up = [(i, i + 1) for i in range(size - 1)]
    down = [(i + 1, i) for i in range(size - 1)]
    last = lax.slice_in_dim(shard, length - 1, length, axis=dim)
    first = lax.slice_in_dim(shard, 0, 1, axis=dim)
    before = lax.ppermute(last, axis, up)
    after = lax.ppermute(first, axis, down)
    return (before, after)


def local_cells(cells, width_x, width_y):
    local_x = cells[:, 0] - lax.axis_index("gx") * width_x
    local_y = cells[:, 1] - lax.axis_index("gy") * width_y
    inside = (local_x >= 0) & (local_x < width_x) & (local_y >= 0) & (local_y < width_y)
    return (
        jnp.clip(local_x, 0, width_x - 1),
        jnp.clip(local_y, 0, width_y - 1),
        cells[:, 2],
        inside.astype(jnp.float32),
    )


def stencil_kernel(
    nx, ny, steps,
    state_in, sound, wind, forward, inj,
    state_out, kernel_out,
    pads, pbuf, ysend, yrecv, ypsend, yprecv, acc_out, ksend, krecv, fpad, fysend, fyr,
    ss, rs, ps, pr, ks, kr, fs, fr, local_sem,
):
    _, width_x, width_y, depth = state_in.shape
    me_p = lax.axis_index("pair")
    gx = lax.axis_index("gx")
    gy = lax.axis_index("gy")
    has_lo_x = gx > 0
    has_hi_x = gx < nx - 1
    has_lo_y = gy > 0
    has_hi_y = gy < ny - 1
    dev_lo_x = (me_p, gx - 1, gy)
    dev_hi_x = (me_p, gx + 1, gy)
    dev_lo_y = (me_p, gx, gy - 1)
    dev_hi_y = (me_p, gx, gy + 1)
    dev_pair = (1 - me_p, gx, gy)
    half = depth // 2

    zero_slab = jnp.zeros((width_y, depth), jnp.float32)
    for par in range(2):
        for c in range(4):
            pads[par, c, 0] = zero_slab
            pads[par, c, width_x + 1] = zero_slab
            for side in range(2):
                yrecv[par, side, c] = jnp.zeros((width_x, depth), jnp.float32)
    for par in range(2):
        pbuf[par, 0] = zero_slab
        pbuf[par, width_x + 1] = zero_slab
    zero_forward = jnp.zeros((width_y, depth), fpad.dtype)
    for t in range(steps):
        for c in range(4):
            fpad[t, c, 0] = zero_forward
            fpad[t, c, width_x + 1] = zero_forward
            for side in range(2):
                fyr[side, t, c // 2, pl.ds((c % 2) * width_x, width_x), :] = jnp.zeros((width_x, depth), fyr.dtype)

    def forward_rows(x, carry):
        for t in range(steps):
            for c in range(4):
                f = forward[t, c, x]
                row = (c % 2) * width_x + x
                fysend[0, t, c // 2, row:row + 1, :] = f[width_y - 1:width_y, :]
                fysend[1, t, c // 2, row:row + 1, :] = f[0:1, :]
        return carry

    [forward_rows(x, 0) for x in range(width_x)]
    interior = pltpu.make_async_copy(forward, fpad.at[:, :, pl.ds(1, width_x)], local_sem.at[0])
    interior.start()
    for par in range(2):
        for side in range(2):
            yprecv[par, side] = jnp.zeros((width_x, depth), jnp.float32)

    barrier = pltpu.get_barrier_semaphore()
    pl.semaphore_signal(barrier, 1, device_id=dev_pair, device_id_type=MESH)
    for cond, dev in ((has_lo_x, dev_lo_x), (has_hi_x, dev_hi_x), (has_lo_y, dev_lo_y), (has_hi_y, dev_hi_y)):
        @pl.when(cond)
        def _():
            pl.semaphore_signal(barrier, 1, device_id=dev, device_id_type=MESH)
    peers = 1 + (
        (gx + nx - 1) // nx + (2 * nx - 2 - gx) // nx
        + (gy + ny - 1) // ny + (2 * ny - 2 - gy) // ny
    )
    pl.semaphore_wait(barrier, peers)

    iy = lax.broadcasted_iota(jnp.int32, (width_y, depth), 0)
    iz = lax.broadcasted_iota(jnp.int32, (width_y, depth), 1)
    we = wind[0:1, :]
    wn = wind[1:2, :]
    wv = wind[2:3, :]

    def dy(v, lo, hi):
        up = jnp.where(iy == width_y - 1, hi, pltpu.roll(v, width_y - 1, 0))
        down = jnp.where(iy == 0, lo, pltpu.roll(v, 1, 0))
        return (up - down) * 0.5

    def dz(v):
        up = jnp.where(iz == depth - 1, 0.0, pltpu.roll(v, depth - 1, 1))
        down = jnp.where(iz == 0, 0.0, pltpu.roll(v, 1, 1))
        return (up - down) * 0.5

    def exchange(src_lo_x, src_hi_x, dst_lo_x, dst_hi_x, src_y_hi, src_y_lo, dst_y_lo, dst_y_hi, send, recv):
        outs = (
            (has_hi_x, src_hi_x, dst_lo_x, 0, dev_hi_x),
            (has_lo_x, src_lo_x, dst_hi_x, 1, dev_lo_x),
            (has_hi_y, src_y_hi, dst_y_lo, 2, dev_hi_y),
            (has_lo_y, src_y_lo, dst_y_hi, 3, dev_lo_y),
        )
        copies = []
        for cond, src, dst, slot, dev in outs:
            copy = pltpu.make_async_remote_copy(
                src_ref=src, dst_ref=dst, send_sem=send.at[slot], recv_sem=recv.at[slot],
                device_id=dev, device_id_type=MESH,
            )
            copies.append((cond, copy))

            @pl.when(cond)
            def _():
                copy.start()
        return copies

    def settle(copies):
        incoming = (has_lo_x, has_hi_x, has_lo_y, has_hi_y)
        for (cond, copy), arrives in zip(copies, incoming):
            @pl.when(cond)
            def _():
                copy.wait_send()

            @pl.when(arrives)
            def _():
                copy.wait_recv()

    def fill_state(par, x, c, v):
        pads[par, c, x + 1] = v
        ysend[par, 0, Y_SLOT[c], x:x + 1, :] = v[width_y - 1:width_y, :]
        ysend[par, 1, Y_SLOT[c], x:x + 1, :] = v[0:1, :]

    def copy_in(x, carry):
        for c in range(4):
            fill_state(0, x, c, state_in[c, x])
        return carry

    [copy_in(x, 0) for x in range(width_x)]
    forward_copies = {}

    def send_forward(t):
        forward_copies[t] = exchange(
            forward.at[t, :, pl.ds(0, 1)], forward.at[t, :, pl.ds(width_x - 1, 1)],
            fpad.at[t, :, pl.ds(0, 1)], fpad.at[t, :, pl.ds(width_x + 1, 1)],
            fysend.at[0, t], fysend.at[1, t], fyr.at[0, t], fyr.at[1, t], fs.at[t], fr.at[t],
        )

    def increment_slab(x, carry, get, snap, first, last):
        xp = x + 1
        p_new = get(0, x)
        a_new = [get(1 + i, x) for i in range(3)]
        fe, fn, fu = [], [], []
        for c in range(4):
            f = fpad[snap, c, xp].astype(jnp.float32)
            fe.append((fpad[snap, c, xp + 1].astype(jnp.float32) - fpad[snap, c, x].astype(jnp.float32)) * 0.5)
            row = (c % 2) * width_x + x
            fn.append(dy(f, fyr[0, snap, c // 2, row:row + 1, :].astype(jnp.float32),
                         fyr[1, snap, c // 2, row:row + 1, :].astype(jnp.float32)))
            fu.append(dz(f))
        pieces = [p_new * (fe[1] + fn[2] + fu[3])]
        for along in (fe, fn, fu):
            pieces.append(p_new * along[0] + a_new[0] * along[1] + a_new[1] * along[2] + a_new[2] * along[3])
        for c in range(4):
            total = pieces[c] if first else acc_out[c, x] + pieces[c]
            if not last:
                acc_out[c, x] = total
                continue
            low, high = total[:, :half], total[:, half:]
            kernel_out[c, x] = jnp.where(me_p == 0, low, high)
            ksend[x, c] = jnp.where(me_p == 0, high, low)
        if last:
            pltpu.make_async_remote_copy(
                src_ref=ksend.at[x], dst_ref=krecv.at[x], send_sem=ks.at[x], recv_sem=kr.at[x],
                device_id=dev_pair, device_id_type=MESH,
            ).start()
        return carry

    def forward_ready(t, first):
        if first:
            interior.wait()
        settle(forward_copies[t])

    for step in range(steps):
        par = step % 2
        nxt = 1 - par
        snap = steps - 1 - step
        last = step == steps - 1
        halves = []
        for part in range(2):
            comps = pl.ds(2 * part, 2) if (part or step == 0) else pl.ds(1, 1)
            halves.append(exchange(
                pads.at[par, comps, pl.ds(1, 1)], pads.at[par, comps, pl.ds(width_x, 1)],
                pads.at[par, comps, pl.ds(0, 1)], pads.at[par, comps, pl.ds(width_x + 1, 1)],
                ysend.at[par, 0, comps], ysend.at[par, 1, comps],
                yrecv.at[par, 0, comps], yrecv.at[par, 1, comps],
                ss.at[par, part], rs.at[par, part],
            ))
        state_copies, velocity_copies = halves
        if step > 0:
            forward_ready(snap + 1, step == 1)
            [(functools.partial(
                increment_slab, get=lambda c, x, par=par: pads[par, c, x + 1],
                snap=snap + 1, first=step == 1, last=False))(x, 0) for x in range(width_x)]
        settle(state_copies)

        def pressure_slab(x, carry, par=par, snap=snap, step=step):
            xp = x + 1
            old = pads.at[par]
            if step == 0:
                p = old[0, xp]
                dxp = (old[0, xp + 1] - old[0, x]) * 0.5
                dyp = dy(p, yrecv[par, 0, Y_SLOT[0], x:x + 1, :], yrecv[par, 1, Y_SLOT[0], x:x + 1, :])
            else:
                held = pbuf.at[1 - par]
                p = held[xp]
                dxp = (held[xp + 1] - held[x]) * 0.5
                dyp = dy(p, yprecv[1 - par, 0, x:x + 1, :], yprecv[1 - par, 1, x:x + 1, :])
            dxa = (old[1, xp + 1] - old[1, x]) * 0.5
            dya = dy(old[2, xp], yrecv[par, 0, Y_SLOT[2], x:x + 1, :], yrecv[par, 1, Y_SLOT[2], x:x + 1, :])
            dzp = dz(p)
            dza = dz(old[3, xp])
            divergence = dxa + dya + dza
            p_new = (
                p
                + step_length * (sound[x] * divergence + we * dxp + wn * dyp + wv * dzp)
                + inj[snap, x]
            )
            pbuf[par, xp] = p_new
            ypsend[0, x:x + 1, :] = p_new[width_y - 1:width_y, :]
            ypsend[1, x:x + 1, :] = p_new[0:1, :]
            return carry

        [pressure_slab(x, 0) for x in range(width_x)]
        pressure_copies = exchange(
            pbuf.at[par, pl.ds(1, 1)], pbuf.at[par, pl.ds(width_x, 1)],
            pbuf.at[par, pl.ds(0, 1)], pbuf.at[par, pl.ds(width_x + 1, 1)],
            ypsend.at[0], ypsend.at[1], yprecv.at[par, 0], yprecv.at[par, 1],
            ps, pr,
        )
        send_forward(snap)
        settle(pressure_copies)

        settle(velocity_copies)

        def velocity_slab(x, carry, par=par, nxt=nxt, last=last):
            xp = x + 1
            old = pads.at[par]
            p_new = pbuf[par, xp]
            grad = (
                (pbuf[par, xp + 1] - pbuf[par, x]) * 0.5,
                dy(p_new, yprecv[par, 0, x:x + 1, :], yprecv[par, 1, x:x + 1, :]),
                dz(p_new),
            )
            new_state = [p_new]
            for i in range(3):
                a = old[1 + i, xp]
                dxa = (old[1 + i, xp + 1] - old[1 + i, x]) * 0.5
                dya = dy(a, yrecv[par, 0, Y_SLOT[1 + i], x:x + 1, :], yrecv[par, 1, Y_SLOT[1 + i], x:x + 1, :])
                dza = dz(a)
                new_state.append(a + step_length * (grad[i] + we * dxa + wn * dya + wv * dza))
            for c in range(4):
                if last:
                    state_out[c, x] = new_state[c]
                else:
                    fill_state(nxt, x, c, new_state[c])
            return carry

        [velocity_slab(x, 0) for x in range(width_x)]

    forward_ready(0, steps == 1)
    [(functools.partial(
        increment_slab, get=lambda c, x: state_out[c, x], snap=0, first=steps == 1, last=True))(x, 0) for x in range(width_x)]

    for x in range(width_x):
        copy = pltpu.make_async_remote_copy(
            src_ref=ksend.at[x], dst_ref=krecv.at[x], send_sem=ks.at[x], recv_sem=kr.at[x],
            device_id=dev_pair, device_id_type=MESH,
        )
        copy.wait_send()
        copy.wait_recv()

    def add_partner(x, carry):
        for c in range(4):
            kernel_out[c, x] = kernel_out[c, x] + krecv[x, c]
        return carry

    [add_partner(x, 0) for x in range(width_x)]


def samples_kernel(nx, ny, local_ref, out_ref, sent, got_x, got_y, send_sem, recv_sem):
    me_p = lax.axis_index("pair")
    gx = lax.axis_index("gx")
    gy = lax.axis_index("gy")
    peers_x = [(me_p, (gx + d) % nx, gy) for d in range(1, nx)]
    peers_y = [(me_p, gx, (gy + d) % ny) for d in range(1, ny)]
    barrier = pltpu.get_barrier_semaphore()
    for dev in peers_x + peers_y:
        pl.semaphore_signal(barrier, 1, device_id=dev, device_id_type=MESH)
    pl.semaphore_wait(barrier, len(peers_x) + len(peers_y))
    rounds = ((local_ref, got_x, peers_x, 0), (sent, got_y, peers_y, nx - 1))
    total = local_ref[...]
    for src, got, peers, base in rounds:
        copies = []
        for i, dev in enumerate(peers):
            copy = pltpu.make_async_remote_copy(
                src_ref=src, dst_ref=got.at[i], send_sem=send_sem.at[base + i],
                recv_sem=recv_sem.at[base + i], device_id=dev, device_id_type=MESH,
            )
            copy.start()
            copies.append(copy)
        for copy in copies:
            copy.wait_send()
            copy.wait_recv()
        for i in range(len(peers)):
            total = total + got[i]
        if base == 0:
            sent[...] = total
    out_ref[...] = total


def gathered_samples(local_samples):
    nx, ny = lax.axis_size("gx"), lax.axis_size("gy")
    if nx < 2 or ny < 2:
        return lax.psum(local_samples, ("gx", "gy"))
    vmem = pl.BlockSpec(memory_space=pltpu.VMEM)
    return pl.pallas_call(
        functools.partial(samples_kernel, nx, ny),
        out_shape=jax.ShapeDtypeStruct(local_samples.shape, jnp.float32),
        in_specs=[vmem],
        out_specs=vmem,
        scratch_shapes=[
            pltpu.VMEM(local_samples.shape, jnp.float32),
            pltpu.VMEM((nx - 1,) + local_samples.shape, jnp.float32),
            pltpu.VMEM((ny - 1,) + local_samples.shape, jnp.float32),
            pltpu.SemaphoreType.DMA((nx + ny - 2,)),
            pltpu.SemaphoreType.DMA((nx + ny - 2,)),
        ],
        compiler_params=pltpu.CompilerParams(collective_id=1, has_side_effects=True),
    )(local_samples)


def shards(
    sound_speed_sq,
    wind_profile,
    forward_field,
    adjoint_state,
    pair_counts,
    source_cells,
    receiver_cells,
    residuals,
):
    steps_total = forward_field.shape[0]
    width_x, width_y, depth = sound_speed_sq.shape
    slots = residuals.shape[0]
    live = (jnp.arange(slots, dtype=jnp.int32) < pair_counts[0]).astype(jnp.float32)
    gx_first = lax.axis_index("gx") * width_x
    gy_first = lax.axis_index("gy") * width_y
    x_range = jnp.arange(width_x, dtype=jnp.int32)
    y_range = jnp.arange(width_y, dtype=jnp.int32)
    z_range = jnp.arange(depth, dtype=jnp.int32)

    def tile_mask(cells):
        on_x = (cells[:, 0][None, :] - gx_first) == x_range[:, None]
        on_y = (cells[:, 1][None, :] - gy_first) == y_range[:, None]
        return (on_x[:, None, :] & on_y[None, :, :]).astype(jnp.float32)

    source_z = (source_cells[:, 2][None, :] == z_range[:, None]).astype(jnp.bfloat16)
    along_z = jnp.einsum(
        "txyz,zn->txyn", forward_field[:, 0], source_z, preferred_element_type=jnp.float32
    )
    local_samples = jnp.sum(along_z * tile_mask(source_cells)[None], axis=(1, 2))
    samples = gathered_samples(local_samples)
    amplitude = jnp.transpose(residuals) * samples * live[None, :]
    spread = amplitude[:, None, None, :] * tile_mask(receiver_cells)[None]
    receiver_z = (receiver_cells[:, 2][:, None] == z_range[None, :]).astype(jnp.float32)
    injected = jnp.einsum(
        "txyn,nz->txyz", spread, receiver_z, precision=lax.Precision.HIGHEST,
        preferred_element_type=jnp.float32,
    )
    vmem = pl.BlockSpec(memory_space=pltpu.VMEM)
    kernel = functools.partial(
        stencil_kernel, lax.axis_size("gx"), lax.axis_size("gy"), steps_total
    )
    state_new, kernels = pl.pallas_call(
        kernel,
        out_shape=(
            jax.ShapeDtypeStruct((4, width_x, width_y, depth), jnp.float32),
            jax.ShapeDtypeStruct((4, width_x, width_y, depth // 2), jnp.float32),
        ),
        in_specs=[vmem] * 5,
        out_specs=(vmem, vmem),
        scratch_shapes=[
            pltpu.VMEM((2, 4, width_x + 2, width_y, depth), jnp.float32),
            pltpu.VMEM((2, width_x + 2, width_y, depth), jnp.float32),
            pltpu.VMEM((2, 2, 4, width_x, depth), jnp.float32),
            pltpu.VMEM((2, 2, 4, width_x, depth), jnp.float32),
            pltpu.VMEM((2, width_x, depth), jnp.float32),
            pltpu.VMEM((2, 2, width_x, depth), jnp.float32),
            pltpu.VMEM((4, width_x, width_y, depth), jnp.float32),
            pltpu.VMEM((width_x, 4, width_y, depth // 2), jnp.float32),
            pltpu.VMEM((width_x, 4, width_y, depth // 2), jnp.float32),
            pltpu.VMEM((steps_total, 4, width_x + 2, width_y, depth), forward_field.dtype),
            pltpu.VMEM((2, steps_total, 2, 2 * width_x, depth), forward_field.dtype),
            pltpu.VMEM((2, steps_total, 2, 2 * width_x, depth), forward_field.dtype),
            pltpu.SemaphoreType.DMA((2, 2, 4)),
            pltpu.SemaphoreType.DMA((2, 2, 4)),
            pltpu.SemaphoreType.DMA((4,)),
            pltpu.SemaphoreType.DMA((4,)),
            pltpu.SemaphoreType.DMA((width_x,)),
            pltpu.SemaphoreType.DMA((width_x,)),
            pltpu.SemaphoreType.DMA((steps_total, 4)),
            pltpu.SemaphoreType.DMA((steps_total, 4)),
            pltpu.SemaphoreType.DMA((1,)),
        ],
        compiler_params=pltpu.CompilerParams(
            collective_id=0, has_side_effects=True, vmem_limit_bytes=48 * 1024 * 1024
        ),
    )(adjoint_state[0], sound_speed_sq, wind_profile, forward_field, injected)
    return (kernels, state_new[None])


def solution(mesh):
    in_specs = (
        P("gx", "gy", None),
        P(),
        P(None, None, "gx", "gy", None),
        P("pair", None, "gx", "gy", None),
        P("pair"),
        P("pair", None),
        P("pair", None),
        P("pair", None),
    )
    out_specs = (P(None, "gx", "gy", "pair"), P("pair", None, "gx", "gy", None))
    return jax.shard_map(shards, mesh=mesh, in_specs=in_specs, out_specs=out_specs, check_vma=False)
```

```python
import functools

import jax
import jax.numpy as jnp
from jax import lax
from jax.experimental import pallas as pl
from jax.experimental.pallas import tpu as pltpu
from jax.sharding import PartitionSpec as P

step_length = 0.25
Y_SLOT = (0, 2, 1, 3)
MESH = pl.DeviceIdType.MESH


def neighbours(shard, axis, dim):
    size, length = (lax.axis_size(axis), shard.shape[dim])
    up = [(i, i + 1) for i in range(size - 1)]
    down = [(i + 1, i) for i in range(size - 1)]
    last = lax.slice_in_dim(shard, length - 1, length, axis=dim)
    first = lax.slice_in_dim(shard, 0, 1, axis=dim)
    before = lax.ppermute(last, axis, up)
    after = lax.ppermute(first, axis, down)
    return (before, after)


def local_cells(cells, width_x, width_y):
    local_x = cells[:, 0] - lax.axis_index("gx") * width_x
    local_y = cells[:, 1] - lax.axis_index("gy") * width_y
    inside = (local_x >= 0) & (local_x < width_x) & (local_y >= 0) & (local_y < width_y)
    return (
        jnp.clip(local_x, 0, width_x - 1),
        jnp.clip(local_y, 0, width_y - 1),
        cells[:, 2],
        inside.astype(jnp.float32),
    )


def stencil_kernel(
    nx, ny, steps,
    state_in, sound, wind, forward, inj,
    state_out, kernel_out,
    pads, pbuf, ysend, yrecv, ypsend, yprecv, acc_out, ksend, krecv, fpad, fysend, fyr,
    ss, rs, ps, pr, ks, kr, fs, fr, local_sem,
):
    _, width_x, width_y, depth = state_in.shape
    me_p = lax.axis_index("pair")
    gx = lax.axis_index("gx")
    gy = lax.axis_index("gy")
    has_lo_x = gx > 0
    has_hi_x = gx < nx - 1
    has_lo_y = gy > 0
    has_hi_y = gy < ny - 1
    dev_lo_x = (me_p, gx - 1, gy)
    dev_hi_x = (me_p, gx + 1, gy)
    dev_lo_y = (me_p, gx, gy - 1)
    dev_hi_y = (me_p, gx, gy + 1)
    dev_pair = (1 - me_p, gx, gy)
    half = depth // 2

    zero_slab = jnp.zeros((width_y, depth), jnp.float32)
    for par in range(2):
        for c in range(4):
            pads[par, c, 0] = zero_slab
            pads[par, c, width_x + 1] = zero_slab
            for side in range(2):
                yrecv[par, side, c] = jnp.zeros((width_x, depth), jnp.float32)
    for par in range(2):
        pbuf[par, 0] = zero_slab
        pbuf[par, width_x + 1] = zero_slab
    zero_forward = jnp.zeros((width_y, depth), fpad.dtype)
    for t in range(steps):
        for c in range(4):
            fpad[t, c, 0] = zero_forward
            fpad[t, c, width_x + 1] = zero_forward
            for side in range(2):
                fyr[side, t, c // 2, pl.ds((c % 2) * width_x, width_x), :] = jnp.zeros((width_x, depth), fyr.dtype)

    def forward_rows(x, carry):
        for t in range(steps):
            for c in range(4):
                f = forward[t, c, x]
                row = (c % 2) * width_x + x
                fysend[0, t, c // 2, row:row + 1, :] = f[width_y - 1:width_y, :]
                fysend[1, t, c // 2, row:row + 1, :] = f[0:1, :]
        return carry

    interior = pltpu.make_async_copy(forward, fpad.at[:, :, pl.ds(1, width_x)], local_sem.at[0])
    interior.start()
    for par in range(2):
        for side in range(2):
            yprecv[par, side] = jnp.zeros((width_x, depth), jnp.float32)

    barrier = pltpu.get_barrier_semaphore()
    pl.semaphore_signal(barrier, 1, device_id=dev_pair, device_id_type=MESH)
    for cond, dev in ((has_lo_x, dev_lo_x), (has_hi_x, dev_hi_x), (has_lo_y, dev_lo_y), (has_hi_y, dev_hi_y)):
        @pl.when(cond)
        def _():
            pl.semaphore_signal(barrier, 1, device_id=dev, device_id_type=MESH)
    peers = 1 + (
        (gx + nx - 1) // nx + (2 * nx - 2 - gx) // nx
        + (gy + ny - 1) // ny + (2 * ny - 2 - gy) // ny
    )

    iy = lax.broadcasted_iota(jnp.int32, (width_y, depth), 0)
    iz = lax.broadcasted_iota(jnp.int32, (width_y, depth), 1)
    we = wind[0:1, :]
    wn = wind[1:2, :]
    wv = wind[2:3, :]

    def dy(v, lo, hi):
        up = jnp.where(iy == width_y - 1, hi, pltpu.roll(v, width_y - 1, 0))
        down = jnp.where(iy == 0, lo, pltpu.roll(v, 1, 0))
        return (up - down) * 0.5

    def dz(v):
        up = jnp.where(iz == depth - 1, 0.0, pltpu.roll(v, depth - 1, 1))
        down = jnp.where(iz == 0, 0.0, pltpu.roll(v, 1, 1))
        return (up - down) * 0.5

    def exchange(src_lo_x, src_hi_x, dst_lo_x, dst_hi_x, src_y_hi, src_y_lo, dst_y_lo, dst_y_hi, send, recv):
        outs = (
            (has_hi_x, src_hi_x, dst_lo_x, 0, dev_hi_x),
            (has_lo_x, src_lo_x, dst_hi_x, 1, dev_lo_x),
            (has_hi_y, src_y_hi, dst_y_lo, 2, dev_hi_y),
            (has_lo_y, src_y_lo, dst_y_hi, 3, dev_lo_y),
        )
        copies = []
        for cond, src, dst, slot, dev in outs:
            copy = pltpu.make_async_remote_copy(
                src_ref=src, dst_ref=dst, send_sem=send.at[slot], recv_sem=recv.at[slot],
                device_id=dev, device_id_type=MESH,
            )
            copies.append((cond, copy))

            @pl.when(cond)
            def _():
                copy.start()
        return copies

    def settle(copies):
        incoming = (has_lo_x, has_hi_x, has_lo_y, has_hi_y)
        for (cond, copy), arrives in zip(copies, incoming):
            @pl.when(cond)
            def _():
                copy.wait_send()

            @pl.when(arrives)
            def _():
                copy.wait_recv()

    def fill_state(par, x, c, v):
        pads[par, c, x + 1] = v
        ysend[par, 0, Y_SLOT[c], x:x + 1, :] = v[width_y - 1:width_y, :]
        ysend[par, 1, Y_SLOT[c], x:x + 1, :] = v[0:1, :]

    def copy_in(x, carry):
        for c in range(4):
            fill_state(0, x, c, state_in[c, x])
        return carry

    [copy_in(x, 0) for x in range(width_x)]
    pl.semaphore_wait(barrier, peers)
    forward_copies = {}

    def send_forward(t):
        forward_copies[t] = exchange(
            forward.at[t, :, pl.ds(0, 1)], forward.at[t, :, pl.ds(width_x - 1, 1)],
            fpad.at[t, :, pl.ds(0, 1)], fpad.at[t, :, pl.ds(width_x + 1, 1)],
            fysend.at[0, t], fysend.at[1, t], fyr.at[0, t], fyr.at[1, t], fs.at[t], fr.at[t],
        )

    def increment_slab(x, carry, get, snap, first, last):
        xp = x + 1
        p_new = get(0, x)
        a_new = [get(1 + i, x) for i in range(3)]
        fe, fn, fu = [], [], []
        for c in range(4):
            f = fpad[snap, c, xp].astype(jnp.float32)
            fe.append((fpad[snap, c, xp + 1].astype(jnp.float32) - fpad[snap, c, x].astype(jnp.float32)) * 0.5)
            row = (c % 2) * width_x + x
            fn.append(dy(f, fyr[0, snap, c // 2, row:row + 1, :].astype(jnp.float32),
                         fyr[1, snap, c // 2, row:row + 1, :].astype(jnp.float32)))
            fu.append(dz(f))
        pieces = [p_new * (fe[1] + fn[2] + fu[3])]
        for along in (fe, fn, fu):
            pieces.append(p_new * along[0] + a_new[0] * along[1] + a_new[1] * along[2] + a_new[2] * along[3])
        for c in range(4):
            total = pieces[c] if first else acc_out[c, x] + pieces[c]
            if not last:
                acc_out[c, x] = total
                continue
            low, high = total[:, :half], total[:, half:]
            kernel_out[c, x] = jnp.where(me_p == 0, low, high)
            ksend[x, c] = jnp.where(me_p == 0, high, low)
        if last:
            pltpu.make_async_remote_copy(
                src_ref=ksend.at[x], dst_ref=krecv.at[x], send_sem=ks.at[x], recv_sem=kr.at[x],
                device_id=dev_pair, device_id_type=MESH,
            ).start()
        return carry

    def forward_ready(t, first):
        if first:
            interior.wait()
        settle(forward_copies[t])

    for step in range(steps):
        par = step % 2
        nxt = 1 - par
        snap = steps - 1 - step
        last = step == steps - 1
        halves = []
        for part in range(2):
            comps = pl.ds(2 * part, 2) if (part or step == 0) else pl.ds(1, 1)
            halves.append(exchange(
                pads.at[par, comps, pl.ds(1, 1)], pads.at[par, comps, pl.ds(width_x, 1)],
                pads.at[par, comps, pl.ds(0, 1)], pads.at[par, comps, pl.ds(width_x + 1, 1)],
                ysend.at[par, 0, comps], ysend.at[par, 1, comps],
                yrecv.at[par, 0, comps], yrecv.at[par, 1, comps],
                ss.at[par, part], rs.at[par, part],
            ))
        state_copies, velocity_copies = halves
        if step == 0:
            [forward_rows(x, 0) for x in range(width_x)]
        if step > 0:
            forward_ready(snap + 1, step == 1)
            [(functools.partial(
                increment_slab, get=lambda c, x, par=par: pads[par, c, x + 1],
                snap=snap + 1, first=step == 1, last=False))(x, 0) for x in range(width_x)]
        settle(state_copies)

        def pressure_slab(x, carry, par=par, snap=snap, step=step):
            xp = x + 1
            old = pads.at[par]
            if step == 0:
                p = old[0, xp]
                dxp = (old[0, xp + 1] - old[0, x]) * 0.5
                dyp = dy(p, yrecv[par, 0, Y_SLOT[0], x:x + 1, :], yrecv[par, 1, Y_SLOT[0], x:x + 1, :])
            else:
                held = pbuf.at[1 - par]
                p = held[xp]
                dxp = (held[xp + 1] - held[x]) * 0.5
                dyp = dy(p, yprecv[1 - par, 0, x:x + 1, :], yprecv[1 - par, 1, x:x + 1, :])
            dxa = (old[1, xp + 1] - old[1, x]) * 0.5
            dya = dy(old[2, xp], yrecv[par, 0, Y_SLOT[2], x:x + 1, :], yrecv[par, 1, Y_SLOT[2], x:x + 1, :])
            dzp = dz(p)
            dza = dz(old[3, xp])
            divergence = dxa + dya + dza
            p_new = (
                p
                + step_length * (sound[x] * divergence + we * dxp + wn * dyp + wv * dzp)
                + inj[snap, x]
            )
            pbuf[par, xp] = p_new
            ypsend[0, x:x + 1, :] = p_new[width_y - 1:width_y, :]
            ypsend[1, x:x + 1, :] = p_new[0:1, :]
            return carry

        [pressure_slab(x, 0) for x in range(width_x)]
        pressure_copies = exchange(
            pbuf.at[par, pl.ds(1, 1)], pbuf.at[par, pl.ds(width_x, 1)],
            pbuf.at[par, pl.ds(0, 1)], pbuf.at[par, pl.ds(width_x + 1, 1)],
            ypsend.at[0], ypsend.at[1], yprecv.at[par, 0], yprecv.at[par, 1],
            ps, pr,
        )
        send_forward(snap)
        settle(pressure_copies)

        settle(velocity_copies)

        def velocity_slab(x, carry, par=par, nxt=nxt, last=last):
            xp = x + 1
            old = pads.at[par]
            p_new = pbuf[par, xp]
            grad = (
                (pbuf[par, xp + 1] - pbuf[par, x]) * 0.5,
                dy(p_new, yprecv[par, 0, x:x + 1, :], yprecv[par, 1, x:x + 1, :]),
                dz(p_new),
            )
            new_state = [p_new]
            for i in range(3):
                a = old[1 + i, xp]
                dxa = (old[1 + i, xp + 1] - old[1 + i, x]) * 0.5
                dya = dy(a, yrecv[par, 0, Y_SLOT[1 + i], x:x + 1, :], yrecv[par, 1, Y_SLOT[1 + i], x:x + 1, :])
                dza = dz(a)
                new_state.append(a + step_length * (grad[i] + we * dxa + wn * dya + wv * dza))
            for c in range(4):
                if last:
                    state_out[c, x] = new_state[c]
                else:
                    fill_state(nxt, x, c, new_state[c])
            return carry

        [velocity_slab(x, 0) for x in range(width_x)]

    forward_ready(0, steps == 1)
    [(functools.partial(
        increment_slab, get=lambda c, x: state_out[c, x], snap=0, first=steps == 1, last=True))(x, 0) for x in range(width_x)]

    for x in range(width_x):
        copy = pltpu.make_async_remote_copy(
            src_ref=ksend.at[x], dst_ref=krecv.at[x], send_sem=ks.at[x], recv_sem=kr.at[x],
            device_id=dev_pair, device_id_type=MESH,
        )
        copy.wait_send()
        copy.wait_recv()

    def add_partner(x, carry):
        for c in range(4):
            kernel_out[c, x] = kernel_out[c, x] + krecv[x, c]
        return carry

    [add_partner(x, 0) for x in range(width_x)]


def samples_kernel(nx, ny, local_ref, out_ref, sent, got_x, got_y, send_sem, recv_sem):
    me_p = lax.axis_index("pair")
    gx = lax.axis_index("gx")
    gy = lax.axis_index("gy")
    peers_x = [(me_p, (gx + d) % nx, gy) for d in range(1, nx)]
    peers_y = [(me_p, gx, (gy + d) % ny) for d in range(1, ny)]
    barrier = pltpu.get_barrier_semaphore()
    for dev in peers_x + peers_y:
        pl.semaphore_signal(barrier, 1, device_id=dev, device_id_type=MESH)
    pl.semaphore_wait(barrier, len(peers_x) + len(peers_y))
    rounds = ((local_ref, got_x, peers_x, 0), (sent, got_y, peers_y, nx - 1))
    total = local_ref[...]
    for src, got, peers, base in rounds:
        copies = []
        for i, dev in enumerate(peers):
            copy = pltpu.make_async_remote_copy(
                src_ref=src, dst_ref=got.at[i], send_sem=send_sem.at[base + i],
                recv_sem=recv_sem.at[base + i], device_id=dev, device_id_type=MESH,
            )
            copy.start()
            copies.append(copy)
        for copy in copies:
            copy.wait_send()
            copy.wait_recv()
        for i in range(len(peers)):
            total = total + got[i]
        if base == 0:
            sent[...] = total
    out_ref[...] = total


def gathered_samples(local_samples):
    nx, ny = lax.axis_size("gx"), lax.axis_size("gy")
    if nx < 2 or ny < 2:
        return lax.psum(local_samples, ("gx", "gy"))
    vmem = pl.BlockSpec(memory_space=pltpu.VMEM)
    return pl.pallas_call(
        functools.partial(samples_kernel, nx, ny),
        out_shape=jax.ShapeDtypeStruct(local_samples.shape, jnp.float32),
        in_specs=[vmem],
        out_specs=vmem,
        scratch_shapes=[
            pltpu.VMEM(local_samples.shape, jnp.float32),
            pltpu.VMEM((nx - 1,) + local_samples.shape, jnp.float32),
            pltpu.VMEM((ny - 1,) + local_samples.shape, jnp.float32),
            pltpu.SemaphoreType.DMA((nx + ny - 2,)),
            pltpu.SemaphoreType.DMA((nx + ny - 2,)),
        ],
        compiler_params=pltpu.CompilerParams(collective_id=1, has_side_effects=True),
    )(local_samples)


def shards(
    sound_speed_sq,
    wind_profile,
    forward_field,
    adjoint_state,
    pair_counts,
    source_cells,
    receiver_cells,
    residuals,
):
    steps_total = forward_field.shape[0]
    width_x, width_y, depth = sound_speed_sq.shape
    slots = residuals.shape[0]
    live = (jnp.arange(slots, dtype=jnp.int32) < pair_counts[0]).astype(jnp.float32)
    gx_first = lax.axis_index("gx") * width_x
    gy_first = lax.axis_index("gy") * width_y
    x_range = jnp.arange(width_x, dtype=jnp.int32)
    y_range = jnp.arange(width_y, dtype=jnp.int32)
    z_range = jnp.arange(depth, dtype=jnp.int32)

    def tile_mask(cells):
        on_x = (cells[:, 0][None, :] - gx_first) == x_range[:, None]
        on_y = (cells[:, 1][None, :] - gy_first) == y_range[:, None]
        return (on_x[:, None, :] & on_y[None, :, :]).astype(jnp.float32)

    source_z = (source_cells[:, 2][None, :] == z_range[:, None]).astype(jnp.bfloat16)
    along_z = jnp.einsum(
        "txyz,zn->txyn", forward_field[:, 0], source_z, preferred_element_type=jnp.float32
    )
    local_samples = jnp.sum(along_z * tile_mask(source_cells)[None], axis=(1, 2))
    samples = gathered_samples(local_samples)
    amplitude = jnp.transpose(residuals) * samples * live[None, :]
    spread = amplitude[:, None, None, :] * tile_mask(receiver_cells)[None]
    receiver_z = (receiver_cells[:, 2][:, None] == z_range[None, :]).astype(jnp.float32)
    injected = jnp.einsum(
        "txyn,nz->txyz", spread, receiver_z, precision=lax.Precision.HIGHEST,
        preferred_element_type=jnp.float32,
    )
    vmem = pl.BlockSpec(memory_space=pltpu.VMEM)
    kernel = functools.partial(
        stencil_kernel, lax.axis_size("gx"), lax.axis_size("gy"), steps_total
    )
    state_new, kernels = pl.pallas_call(
        kernel,
        out_shape=(
            jax.ShapeDtypeStruct((4, width_x, width_y, depth), jnp.float32),
            jax.ShapeDtypeStruct((4, width_x, width_y, depth // 2), jnp.float32),
        ),
        in_specs=[vmem] * 5,
        out_specs=(vmem, vmem),
        scratch_shapes=[
            pltpu.VMEM((2, 4, width_x + 2, width_y, depth), jnp.float32),
            pltpu.VMEM((2, width_x + 2, width_y, depth), jnp.float32),
            pltpu.VMEM((2, 2, 4, width_x, depth), jnp.float32),
            pltpu.VMEM((2, 2, 4, width_x, depth), jnp.float32),
            pltpu.VMEM((2, width_x, depth), jnp.float32),
            pltpu.VMEM((2, 2, width_x, depth), jnp.float32),
            pltpu.VMEM((4, width_x, width_y, depth), jnp.float32),
            pltpu.VMEM((width_x, 4, width_y, depth // 2), jnp.float32),
            pltpu.VMEM((width_x, 4, width_y, depth // 2), jnp.float32),
            pltpu.VMEM((steps_total, 4, width_x + 2, width_y, depth), forward_field.dtype),
            pltpu.VMEM((2, steps_total, 2, 2 * width_x, depth), forward_field.dtype),
            pltpu.VMEM((2, steps_total, 2, 2 * width_x, depth), forward_field.dtype),
            pltpu.SemaphoreType.DMA((2, 2, 4)),
            pltpu.SemaphoreType.DMA((2, 2, 4)),
            pltpu.SemaphoreType.DMA((4,)),
            pltpu.SemaphoreType.DMA((4,)),
            pltpu.SemaphoreType.DMA((width_x,)),
            pltpu.SemaphoreType.DMA((width_x,)),
            pltpu.SemaphoreType.DMA((steps_total, 4)),
            pltpu.SemaphoreType.DMA((steps_total, 4)),
            pltpu.SemaphoreType.DMA((1,)),
        ],
        compiler_params=pltpu.CompilerParams(
            collective_id=0, has_side_effects=True, vmem_limit_bytes=48 * 1024 * 1024
        ),
    )(adjoint_state[0], sound_speed_sq, wind_profile, forward_field, injected)
    return (kernels, state_new[None])


def solution(mesh):
    in_specs = (
        P("gx", "gy", None),
        P(),
        P(None, None, "gx", "gy", None),
        P("pair", None, "gx", "gy", None),
        P("pair"),
        P("pair", None),
        P("pair", None),
        P("pair", None),
    )
    out_specs = (P(None, "gx", "gy", "pair"), P("pair", None, "gx", "gy", None))
    return jax.shard_map(shards, mesh=mesh, in_specs=in_specs, out_specs=out_specs, check_vma=False)
```

```python
import functools

import jax
import jax.numpy as jnp
from jax import lax
from jax.experimental import pallas as pl
from jax.experimental.pallas import tpu as pltpu
from jax.sharding import PartitionSpec as P

step_length = 0.25
Y_SLOT = (0, 2, 1, 3)
MESH = pl.DeviceIdType.MESH


def neighbours(shard, axis, dim):
    size, length = (lax.axis_size(axis), shard.shape[dim])
    up = [(i, i + 1) for i in range(size - 1)]
    down = [(i + 1, i) for i in range(size - 1)]
    last = lax.slice_in_dim(shard, length - 1, length, axis=dim)
    first = lax.slice_in_dim(shard, 0, 1, axis=dim)
    before = lax.ppermute(last, axis, up)
    after = lax.ppermute(first, axis, down)
    return (before, after)


def local_cells(cells, width_x, width_y):
    local_x = cells[:, 0] - lax.axis_index("gx") * width_x
    local_y = cells[:, 1] - lax.axis_index("gy") * width_y
    inside = (local_x >= 0) & (local_x < width_x) & (local_y >= 0) & (local_y < width_y)
    return (
        jnp.clip(local_x, 0, width_x - 1),
        jnp.clip(local_y, 0, width_y - 1),
        cells[:, 2],
        inside.astype(jnp.float32),
    )


def stencil_kernel(
    nx, ny, steps,
    state_in, sound, wind, forward, inj,
    state_out, kernel_out,
    pads, pbuf, ysend, yrecv, ypsend, yprecv, acc_out, ksend, krecv, fpad, fysend, fyr,
    ss, rs, ps, pr, ks, kr, fs, fr, local_sem,
):
    _, width_x, width_y, depth = state_in.shape
    me_p = lax.axis_index("pair")
    gx = lax.axis_index("gx")
    gy = lax.axis_index("gy")
    has_lo_x = gx > 0
    has_hi_x = gx < nx - 1
    has_lo_y = gy > 0
    has_hi_y = gy < ny - 1
    dev_lo_x = (me_p, gx - 1, gy)
    dev_hi_x = (me_p, gx + 1, gy)
    dev_lo_y = (me_p, gx, gy - 1)
    dev_hi_y = (me_p, gx, gy + 1)
    dev_pair = (1 - me_p, gx, gy)
    half = depth // 2

    zero_slab = jnp.zeros((width_y, depth), jnp.float32)
    for par in range(2):
        for c in range(4):
            pads[par, c, 0] = zero_slab
            pads[par, c, width_x + 1] = zero_slab
            for side in range(2):
                yrecv[par, side, c] = jnp.zeros((width_x, depth), jnp.float32)
    for par in range(2):
        pbuf[par, 0] = zero_slab
        pbuf[par, width_x + 1] = zero_slab
    zero_forward = jnp.zeros((width_y, depth), fpad.dtype)
    for t in range(steps):
        for c in range(4):
            fpad[t, c, 0] = zero_forward
            fpad[t, c, width_x + 1] = zero_forward
            for side in range(2):
                fyr[side, t, c // 2, pl.ds((c % 2) * width_x, width_x), :] = jnp.zeros((width_x, depth), fyr.dtype)

    def forward_rows(x, carry):
        for t in range(steps):
            for c in range(4):
                f = forward[t, c, x]
                row = (c % 2) * width_x + x
                fysend[0, t, c // 2, row:row + 1, :] = f[width_y - 1:width_y, :]
                fysend[1, t, c // 2, row:row + 1, :] = f[0:1, :]
        return carry

    interior = pltpu.make_async_copy(forward, fpad.at[:, :, pl.ds(1, width_x)], local_sem.at[0])
    interior.start()
    for par in range(2):
        for side in range(2):
            yprecv[par, side] = jnp.zeros((width_x, depth), jnp.float32)

    barrier = pltpu.get_barrier_semaphore()
    pl.semaphore_signal(barrier, 1, device_id=dev_pair, device_id_type=MESH)
    for cond, dev in ((has_lo_x, dev_lo_x), (has_hi_x, dev_hi_x), (has_lo_y, dev_lo_y), (has_hi_y, dev_hi_y)):
        @pl.when(cond)
        def _():
            pl.semaphore_signal(barrier, 1, device_id=dev, device_id_type=MESH)
    peers = 1 + (
        (gx + nx - 1) // nx + (2 * nx - 2 - gx) // nx
        + (gy + ny - 1) // ny + (2 * ny - 2 - gy) // ny
    )

    iy = lax.broadcasted_iota(jnp.int32, (width_y, depth), 0)
    iz = lax.broadcasted_iota(jnp.int32, (width_y, depth), 1)
    we = wind[0:1, :]
    wn = wind[1:2, :]
    wv = wind[2:3, :]

    def dy(v, lo, hi):
        up = jnp.where(iy == width_y - 1, hi, pltpu.roll(v, width_y - 1, 0))
        down = jnp.where(iy == 0, lo, pltpu.roll(v, 1, 0))
        return (up - down) * 0.5

    def dz(v):
        up = jnp.where(iz == depth - 1, 0.0, pltpu.roll(v, depth - 1, 1))
        down = jnp.where(iz == 0, 0.0, pltpu.roll(v, 1, 1))
        return (up - down) * 0.5

    def exchange(src_lo_x, src_hi_x, dst_lo_x, dst_hi_x, src_y_hi, src_y_lo, dst_y_lo, dst_y_hi, send, recv):
        outs = (
            (has_hi_x, src_hi_x, dst_lo_x, 0, dev_hi_x),
            (has_lo_x, src_lo_x, dst_hi_x, 1, dev_lo_x),
            (has_hi_y, src_y_hi, dst_y_lo, 2, dev_hi_y),
            (has_lo_y, src_y_lo, dst_y_hi, 3, dev_lo_y),
        )
        copies = []
        for cond, src, dst, slot, dev in outs:
            copy = pltpu.make_async_remote_copy(
                src_ref=src, dst_ref=dst, send_sem=send.at[slot], recv_sem=recv.at[slot],
                device_id=dev, device_id_type=MESH,
            )
            copies.append((cond, copy))

            @pl.when(cond)
            def _():
                copy.start()
        return copies

    def settle(copies):
        incoming = (has_lo_x, has_hi_x, has_lo_y, has_hi_y)
        for (cond, copy), arrives in zip(copies, incoming):
            @pl.when(cond)
            def _():
                copy.wait_send()

            @pl.when(arrives)
            def _():
                copy.wait_recv()

    def fill_state(par, x, c, v):
        pads[par, c, x + 1] = v
        ysend[par, 0, Y_SLOT[c], x:x + 1, :] = v[width_y - 1:width_y, :]
        ysend[par, 1, Y_SLOT[c], x:x + 1, :] = v[0:1, :]

    def copy_in(x, carry):
        for c in range(4):
            fill_state(0, x, c, state_in[c, x])
        return carry

    [copy_in(x, 0) for x in range(width_x)]
    pl.semaphore_wait(barrier, peers)
    forward_copies = {}

    def send_forward(t):
        forward_copies[t] = exchange(
            forward.at[t, :, pl.ds(0, 1)], forward.at[t, :, pl.ds(width_x - 1, 1)],
            fpad.at[t, :, pl.ds(0, 1)], fpad.at[t, :, pl.ds(width_x + 1, 1)],
            fysend.at[0, t], fysend.at[1, t], fyr.at[0, t], fyr.at[1, t], fs.at[t], fr.at[t],
        )

    def increment_slab(x, carry, get, snap, first, last):
        xp = x + 1
        p_new = get(0, x)
        a_new = [get(1 + i, x) for i in range(3)]
        fe, fn, fu = [], [], []
        for c in range(4):
            f = fpad[snap, c, xp].astype(jnp.float32)
            fe.append((fpad[snap, c, xp + 1].astype(jnp.float32) - fpad[snap, c, x].astype(jnp.float32)) * 0.5)
            row = (c % 2) * width_x + x
            fn.append(dy(f, fyr[0, snap, c // 2, row:row + 1, :].astype(jnp.float32),
                         fyr[1, snap, c // 2, row:row + 1, :].astype(jnp.float32)))
            fu.append(dz(f))
        pieces = [p_new * (fe[1] + fn[2] + fu[3])]
        for along in (fe, fn, fu):
            pieces.append(p_new * along[0] + a_new[0] * along[1] + a_new[1] * along[2] + a_new[2] * along[3])
        for c in range(4):
            total = pieces[c] if first else acc_out[c, x] + pieces[c]
            if not last:
                acc_out[c, x] = total
                continue
            low, high = total[:, :half], total[:, half:]
            kernel_out[c, x] = jnp.where(me_p == 0, low, high)
            ksend[x, c] = jnp.where(me_p == 0, high, low)
        if last:
            pltpu.make_async_remote_copy(
                src_ref=ksend.at[x], dst_ref=krecv.at[x], send_sem=ks.at[x], recv_sem=kr.at[x],
                device_id=dev_pair, device_id_type=MESH,
            ).start()
        return carry

    def forward_ready(t, first):
        if first:
            interior.wait()
        settle(forward_copies[t])

    for step in range(steps):
        par = step % 2
        nxt = 1 - par
        snap = steps - 1 - step
        last = step == steps - 1
        halves = []
        for part in range(2):
            comps = pl.ds(2 * part, 2) if (part or step == 0) else pl.ds(1, 1)
            halves.append(exchange(
                pads.at[par, comps, pl.ds(1, 1)], pads.at[par, comps, pl.ds(width_x, 1)],
                pads.at[par, comps, pl.ds(0, 1)], pads.at[par, comps, pl.ds(width_x + 1, 1)],
                ysend.at[par, 0, comps], ysend.at[par, 1, comps],
                yrecv.at[par, 0, comps], yrecv.at[par, 1, comps],
                ss.at[par, part], rs.at[par, part],
            ))
        state_copies, velocity_copies = halves
        if step == 0:
            [forward_rows(x, 0) for x in range(width_x)]
        if step > 0:
            forward_ready(snap + 1, step == 1)
            [(functools.partial(
                increment_slab, get=lambda c, x, par=par: pads[par, c, x + 1],
                snap=snap + 1, first=step == 1, last=False))(x, 0) for x in range(width_x)]
        settle(state_copies)

        def pressure_slab(x, carry, par=par, snap=snap, step=step):
            xp = x + 1
            old = pads.at[par]
            if step == 0:
                p = old[0, xp]
                dxp = (old[0, xp + 1] - old[0, x]) * 0.5
                dyp = dy(p, yrecv[par, 0, Y_SLOT[0], x:x + 1, :], yrecv[par, 1, Y_SLOT[0], x:x + 1, :])
            else:
                held = pbuf.at[1 - par]
                p = held[xp]
                dxp = (held[xp + 1] - held[x]) * 0.5
                dyp = dy(p, yprecv[1 - par, 0, x:x + 1, :], yprecv[1 - par, 1, x:x + 1, :])
            dxa = (old[1, xp + 1] - old[1, x]) * 0.5
            dya = dy(old[2, xp], yrecv[par, 0, Y_SLOT[2], x:x + 1, :], yrecv[par, 1, Y_SLOT[2], x:x + 1, :])
            dzp = dz(p)
            dza = dz(old[3, xp])
            divergence = dxa + dya + dza
            p_new = (
                p
                + step_length * (sound[x] * divergence + we * dxp + wn * dyp + wv * dzp)
                + inj[snap, x]
            )
            pbuf[par, xp] = p_new
            ypsend[0, x:x + 1, :] = p_new[width_y - 1:width_y, :]
            ypsend[1, x:x + 1, :] = p_new[0:1, :]
            return carry

        [pressure_slab(x, 0) for x in range(width_x)]
        pressure_copies = exchange(
            pbuf.at[par, pl.ds(1, 1)], pbuf.at[par, pl.ds(width_x, 1)],
            pbuf.at[par, pl.ds(0, 1)], pbuf.at[par, pl.ds(width_x + 1, 1)],
            ypsend.at[0], ypsend.at[1], yprecv.at[par, 0], yprecv.at[par, 1],
            ps, pr,
        )
        send_forward(snap)
        settle(pressure_copies)

        settle(velocity_copies)

        def velocity_slab(x, carry, par=par, nxt=nxt, last=last):
            xp = x + 1
            old = pads.at[par]
            p_new = pbuf[par, xp]
            grad = (
                (pbuf[par, xp + 1] - pbuf[par, x]) * 0.5,
                dy(p_new, yprecv[par, 0, x:x + 1, :], yprecv[par, 1, x:x + 1, :]),
                dz(p_new),
            )
            new_state = [p_new]
            for i in range(3):
                a = old[1 + i, xp]
                dxa = (old[1 + i, xp + 1] - old[1 + i, x]) * 0.5
                dya = dy(a, yrecv[par, 0, Y_SLOT[1 + i], x:x + 1, :], yrecv[par, 1, Y_SLOT[1 + i], x:x + 1, :])
                dza = dz(a)
                new_state.append(a + step_length * (grad[i] + we * dxa + wn * dya + wv * dza))
            for c in range(4):
                if last:
                    state_out[c, x] = new_state[c]
                else:
                    fill_state(nxt, x, c, new_state[c])
            return carry

        [velocity_slab(x, 0) for x in range(width_x)]

    forward_ready(0, steps == 1)
    [(functools.partial(
        increment_slab, get=lambda c, x: state_out[c, x], snap=0, first=steps == 1, last=True))(x, 0) for x in range(width_x)]

    for x in range(width_x):
        copy = pltpu.make_async_remote_copy(
            src_ref=ksend.at[x], dst_ref=krecv.at[x], send_sem=ks.at[x], recv_sem=kr.at[x],
            device_id=dev_pair, device_id_type=MESH,
        )
        copy.wait_send()
        copy.wait_recv()

    def add_partner(x, carry):
        for c in range(4):
            kernel_out[c, x] = kernel_out[c, x] + krecv[x, c]
        return carry

    [add_partner(x, 0) for x in range(width_x)]


def samples_kernel(nx, ny, local_ref, out_ref, got, send_sem, recv_sem):
    me_p = lax.axis_index("pair")
    gx = lax.axis_index("gx")
    gy = lax.axis_index("gy")
    peers = [
        (me_p, (gx + dx) % nx, (gy + dy) % ny)
        for dx in range(nx) for dy in range(ny) if dx or dy
    ]
    barrier = pltpu.get_barrier_semaphore()
    for dev in peers:
        pl.semaphore_signal(barrier, 1, device_id=dev, device_id_type=MESH)
    pl.semaphore_wait(barrier, len(peers))
    copies = []
    for i, dev in enumerate(peers):
        copy = pltpu.make_async_remote_copy(
            src_ref=local_ref, dst_ref=got.at[i], send_sem=send_sem.at[i],
            recv_sem=recv_sem.at[i], device_id=dev, device_id_type=MESH,
        )
        copy.start()
        copies.append(copy)
    total = local_ref[...]
    for i, copy in enumerate(copies):
        copy.wait_send()
        copy.wait_recv()
        total = total + got[i]
    out_ref[...] = total


def gathered_samples(local_samples):
    nx, ny = lax.axis_size("gx"), lax.axis_size("gy")
    if nx < 2 or ny < 2:
        return lax.psum(local_samples, ("gx", "gy"))
    vmem = pl.BlockSpec(memory_space=pltpu.VMEM)
    return pl.pallas_call(
        functools.partial(samples_kernel, nx, ny),
        out_shape=jax.ShapeDtypeStruct(local_samples.shape, jnp.float32),
        in_specs=[vmem],
        out_specs=vmem,
        scratch_shapes=[
            pltpu.VMEM((nx * ny - 1,) + local_samples.shape, jnp.float32),
            pltpu.SemaphoreType.DMA((nx * ny - 1,)),
            pltpu.SemaphoreType.DMA((nx * ny - 1,)),
        ],
        compiler_params=pltpu.CompilerParams(collective_id=1, has_side_effects=True),
    )(local_samples)


def shards(
    sound_speed_sq,
    wind_profile,
    forward_field,
    adjoint_state,
    pair_counts,
    source_cells,
    receiver_cells,
    residuals,
):
    steps_total = forward_field.shape[0]
    width_x, width_y, depth = sound_speed_sq.shape
    slots = residuals.shape[0]
    live = (jnp.arange(slots, dtype=jnp.int32) < pair_counts[0]).astype(jnp.float32)
    gx_first = lax.axis_index("gx") * width_x
    gy_first = lax.axis_index("gy") * width_y
    x_range = jnp.arange(width_x, dtype=jnp.int32)
    y_range = jnp.arange(width_y, dtype=jnp.int32)
    z_range = jnp.arange(depth, dtype=jnp.int32)

    def tile_mask(cells):
        on_x = (cells[:, 0][None, :] - gx_first) == x_range[:, None]
        on_y = (cells[:, 1][None, :] - gy_first) == y_range[:, None]
        return (on_x[:, None, :] & on_y[None, :, :]).astype(jnp.float32)

    source_z = (source_cells[:, 2][None, :] == z_range[:, None]).astype(jnp.bfloat16)
    along_z = jnp.einsum(
        "txyz,zn->txyn", forward_field[:, 0], source_z, preferred_element_type=jnp.float32
    )
    local_samples = jnp.sum(along_z * tile_mask(source_cells)[None], axis=(1, 2))
    samples = gathered_samples(local_samples)
    amplitude = jnp.transpose(residuals) * samples * live[None, :]
    spread = amplitude[:, None, None, :] * tile_mask(receiver_cells)[None]
    receiver_z = (receiver_cells[:, 2][:, None] == z_range[None, :]).astype(jnp.float32)
    injected = jnp.einsum(
        "txyn,nz->txyz", spread, receiver_z, precision=lax.Precision.HIGHEST,
        preferred_element_type=jnp.float32,
    )
    vmem = pl.BlockSpec(memory_space=pltpu.VMEM)
    kernel = functools.partial(
        stencil_kernel, lax.axis_size("gx"), lax.axis_size("gy"), steps_total
    )
    state_new, kernels = pl.pallas_call(
        kernel,
        out_shape=(
            jax.ShapeDtypeStruct((4, width_x, width_y, depth), jnp.float32),
            jax.ShapeDtypeStruct((4, width_x, width_y, depth // 2), jnp.float32),
        ),
        in_specs=[vmem] * 5,
        out_specs=(vmem, vmem),
        scratch_shapes=[
            pltpu.VMEM((2, 4, width_x + 2, width_y, depth), jnp.float32),
            pltpu.VMEM((2, width_x + 2, width_y, depth), jnp.float32),
            pltpu.VMEM((2, 2, 4, width_x, depth), jnp.float32),
            pltpu.VMEM((2, 2, 4, width_x, depth), jnp.float32),
            pltpu.VMEM((2, width_x, depth), jnp.float32),
            pltpu.VMEM((2, 2, width_x, depth), jnp.float32),
            pltpu.VMEM((4, width_x, width_y, depth), jnp.float32),
            pltpu.VMEM((width_x, 4, width_y, depth // 2), jnp.float32),
            pltpu.VMEM((width_x, 4, width_y, depth // 2), jnp.float32),
            pltpu.VMEM((steps_total, 4, width_x + 2, width_y, depth), forward_field.dtype),
            pltpu.VMEM((2, steps_total, 2, 2 * width_x, depth), forward_field.dtype),
            pltpu.VMEM((2, steps_total, 2, 2 * width_x, depth), forward_field.dtype),
            pltpu.SemaphoreType.DMA((2, 2, 4)),
            pltpu.SemaphoreType.DMA((2, 2, 4)),
            pltpu.SemaphoreType.DMA((4,)),
            pltpu.SemaphoreType.DMA((4,)),
            pltpu.SemaphoreType.DMA((width_x,)),
            pltpu.SemaphoreType.DMA((width_x,)),
            pltpu.SemaphoreType.DMA((steps_total, 4)),
            pltpu.SemaphoreType.DMA((steps_total, 4)),
            pltpu.SemaphoreType.DMA((1,)),
        ],
        compiler_params=pltpu.CompilerParams(
            collective_id=0, has_side_effects=True, vmem_limit_bytes=48 * 1024 * 1024
        ),
    )(adjoint_state[0], sound_speed_sq, wind_profile, forward_field, injected)
    return (kernels, state_new[None])


def solution(mesh):
    in_specs = (
        P("gx", "gy", None),
        P(),
        P(None, None, "gx", "gy", None),
        P("pair", None, "gx", "gy", None),
        P("pair"),
        P("pair", None),
        P("pair", None),
        P("pair", None),
    )
    out_specs = (P(None, "gx", "gy", "pair"), P("pair", None, "gx", "gy", None))
    return jax.shard_map(shards, mesh=mesh, in_specs=in_specs, out_specs=out_specs, check_vma=False)
```

```python
import functools

import jax
import jax.numpy as jnp
from jax import lax
from jax.experimental import pallas as pl
from jax.experimental.pallas import tpu as pltpu
from jax.sharding import PartitionSpec as P

step_length = 0.25
Y_SLOT = (0, 2, 1, 3)
MESH = pl.DeviceIdType.MESH


def neighbours(shard, axis, dim):
    size, length = (lax.axis_size(axis), shard.shape[dim])
    up = [(i, i + 1) for i in range(size - 1)]
    down = [(i + 1, i) for i in range(size - 1)]
    last = lax.slice_in_dim(shard, length - 1, length, axis=dim)
    first = lax.slice_in_dim(shard, 0, 1, axis=dim)
    before = lax.ppermute(last, axis, up)
    after = lax.ppermute(first, axis, down)
    return (before, after)


def local_cells(cells, width_x, width_y):
    local_x = cells[:, 0] - lax.axis_index("gx") * width_x
    local_y = cells[:, 1] - lax.axis_index("gy") * width_y
    inside = (local_x >= 0) & (local_x < width_x) & (local_y >= 0) & (local_y < width_y)
    return (
        jnp.clip(local_x, 0, width_x - 1),
        jnp.clip(local_y, 0, width_y - 1),
        cells[:, 2],
        inside.astype(jnp.float32),
    )


def stencil_kernel(
    nx, ny, steps,
    state_in, sound, wind, forward, inj,
    state_out, kernel_out,
    pads, pbuf, ysend, yrecv, ypsend, yprecv, acc_out, ksend, krecv, fpad, fysend, fyr, advect,
    ss, rs, ps, pr, ks, kr, fs, fr, local_sem,
):
    _, width_x, width_y, depth = state_in.shape
    me_p = lax.axis_index("pair")
    gx = lax.axis_index("gx")
    gy = lax.axis_index("gy")
    has_lo_x = gx > 0
    has_hi_x = gx < nx - 1
    has_lo_y = gy > 0
    has_hi_y = gy < ny - 1
    dev_lo_x = (me_p, gx - 1, gy)
    dev_hi_x = (me_p, gx + 1, gy)
    dev_lo_y = (me_p, gx, gy - 1)
    dev_hi_y = (me_p, gx, gy + 1)
    dev_pair = (1 - me_p, gx, gy)
    half = depth // 2

    zero_slab = jnp.zeros((width_y, depth), jnp.float32)
    for par in range(2):
        for c in range(4):
            pads[par, c, 0] = zero_slab
            pads[par, c, width_x + 1] = zero_slab
            for side in range(2):
                yrecv[par, side, c] = jnp.zeros((width_x, depth), jnp.float32)
    for par in range(2):
        pbuf[par, 0] = zero_slab
        pbuf[par, width_x + 1] = zero_slab
    zero_forward = jnp.zeros((width_y, depth), fpad.dtype)
    for t in range(steps):
        for c in range(4):
            fpad[t, c, 0] = zero_forward
            fpad[t, c, width_x + 1] = zero_forward
            for side in range(2):
                fyr[side, t, c // 2, pl.ds((c % 2) * width_x, width_x), :] = jnp.zeros((width_x, depth), fyr.dtype)

    def forward_rows(x, carry):
        for t in range(steps):
            for c in range(4):
                f = forward[t, c, x]
                row = (c % 2) * width_x + x
                fysend[0, t, c // 2, row:row + 1, :] = f[width_y - 1:width_y, :]
                fysend[1, t, c // 2, row:row + 1, :] = f[0:1, :]
        return carry

    [forward_rows(x, 0) for x in range(width_x)]
    interior = pltpu.make_async_copy(forward, fpad.at[:, :, pl.ds(1, width_x)], local_sem.at[0])
    interior.start()
    for par in range(2):
        for side in range(2):
            yprecv[par, side] = jnp.zeros((width_x, depth), jnp.float32)

    barrier = pltpu.get_barrier_semaphore()
    pl.semaphore_signal(barrier, 1, device_id=dev_pair, device_id_type=MESH)
    for cond, dev in ((has_lo_x, dev_lo_x), (has_hi_x, dev_hi_x), (has_lo_y, dev_lo_y), (has_hi_y, dev_hi_y)):
        @pl.when(cond)
        def _():
            pl.semaphore_signal(barrier, 1, device_id=dev, device_id_type=MESH)
    peers = 1 + (
        (gx + nx - 1) // nx + (2 * nx - 2 - gx) // nx
        + (gy + ny - 1) // ny + (2 * ny - 2 - gy) // ny
    )
    pl.semaphore_wait(barrier, peers)

    iy = lax.broadcasted_iota(jnp.int32, (width_y, depth), 0)
    iz = lax.broadcasted_iota(jnp.int32, (width_y, depth), 1)
    we = wind[0:1, :]
    wn = wind[1:2, :]
    wv = wind[2:3, :]

    def dy(v, lo, hi):
        up = jnp.where(iy == width_y - 1, hi, pltpu.roll(v, width_y - 1, 0))
        down = jnp.where(iy == 0, lo, pltpu.roll(v, 1, 0))
        return (up - down) * 0.5

    def dz(v):
        up = jnp.where(iz == depth - 1, 0.0, pltpu.roll(v, depth - 1, 1))
        down = jnp.where(iz == 0, 0.0, pltpu.roll(v, 1, 1))
        return (up - down) * 0.5

    def exchange(src_lo_x, src_hi_x, dst_lo_x, dst_hi_x, src_y_hi, src_y_lo, dst_y_lo, dst_y_hi, send, recv):
        outs = (
            (has_hi_x, src_hi_x, dst_lo_x, 0, dev_hi_x),
            (has_lo_x, src_lo_x, dst_hi_x, 1, dev_lo_x),
            (has_hi_y, src_y_hi, dst_y_lo, 2, dev_hi_y),
            (has_lo_y, src_y_lo, dst_y_hi, 3, dev_lo_y),
        )
        copies = []
        for cond, src, dst, slot, dev in outs:
            copy = pltpu.make_async_remote_copy(
                src_ref=src, dst_ref=dst, send_sem=send.at[slot], recv_sem=recv.at[slot],
                device_id=dev, device_id_type=MESH,
            )
            copies.append((cond, copy))

            @pl.when(cond)
            def _():
                copy.start()
        return copies

    def settle(copies):
        incoming = (has_lo_x, has_hi_x, has_lo_y, has_hi_y)
        for (cond, copy), arrives in zip(copies, incoming):
            @pl.when(cond)
            def _():
                copy.wait_send()

            @pl.when(arrives)
            def _():
                copy.wait_recv()

    def fill_state(par, x, c, v):
        pads[par, c, x + 1] = v
        ysend[par, 0, Y_SLOT[c], x:x + 1, :] = v[width_y - 1:width_y, :]
        ysend[par, 1, Y_SLOT[c], x:x + 1, :] = v[0:1, :]

    def copy_in(x, carry):
        for c in range(4):
            fill_state(0, x, c, state_in[c, x])
        return carry

    [copy_in(x, 0) for x in range(width_x)]
    forward_copies = {}

    def send_forward(t):
        forward_copies[t] = exchange(
            forward.at[t, :, pl.ds(0, 1)], forward.at[t, :, pl.ds(width_x - 1, 1)],
            fpad.at[t, :, pl.ds(0, 1)], fpad.at[t, :, pl.ds(width_x + 1, 1)],
            fysend.at[0, t], fysend.at[1, t], fyr.at[0, t], fyr.at[1, t], fs.at[t], fr.at[t],
        )

    def increment_slab(x, carry, get, snap, first, last):
        xp = x + 1
        p_new = get(0, x)
        a_new = [get(1 + i, x) for i in range(3)]
        fe, fn, fu = [], [], []
        for c in range(4):
            f = fpad[snap, c, xp].astype(jnp.float32)
            fe.append((fpad[snap, c, xp + 1].astype(jnp.float32) - fpad[snap, c, x].astype(jnp.float32)) * 0.5)
            row = (c % 2) * width_x + x
            fn.append(dy(f, fyr[0, snap, c // 2, row:row + 1, :].astype(jnp.float32),
                         fyr[1, snap, c // 2, row:row + 1, :].astype(jnp.float32)))
            fu.append(dz(f))
        pieces = [p_new * (fe[1] + fn[2] + fu[3])]
        for along in (fe, fn, fu):
            pieces.append(p_new * along[0] + a_new[0] * along[1] + a_new[1] * along[2] + a_new[2] * along[3])
        for c in range(4):
            total = pieces[c] if first else acc_out[c, x] + pieces[c]
            if not last:
                acc_out[c, x] = total
                continue
            low, high = total[:, :half], total[:, half:]
            kernel_out[c, x] = jnp.where(me_p == 0, low, high)
            ksend[x, c] = jnp.where(me_p == 0, high, low)
        if last:
            pltpu.make_async_remote_copy(
                src_ref=ksend.at[x], dst_ref=krecv.at[x], send_sem=ks.at[x], recv_sem=kr.at[x],
                device_id=dev_pair, device_id_type=MESH,
            ).start()
        return carry

    def forward_ready(t, first):
        if first:
            interior.wait()
        settle(forward_copies[t])

    for step in range(steps):
        par = step % 2
        nxt = 1 - par
        snap = steps - 1 - step
        last = step == steps - 1
        halves = []
        for part in range(2):
            comps = pl.ds(2 * part, 2) if (part or step == 0) else pl.ds(1, 1)
            halves.append(exchange(
                pads.at[par, comps, pl.ds(1, 1)], pads.at[par, comps, pl.ds(width_x, 1)],
                pads.at[par, comps, pl.ds(0, 1)], pads.at[par, comps, pl.ds(width_x + 1, 1)],
                ysend.at[par, 0, comps], ysend.at[par, 1, comps],
                yrecv.at[par, 0, comps], yrecv.at[par, 1, comps],
                ss.at[par, part], rs.at[par, part],
            ))
        state_copies, velocity_copies = halves
        if step > 0:
            forward_ready(snap + 1, step == 1)
            [(functools.partial(
                increment_slab, get=lambda c, x, par=par: pads[par, c, x + 1],
                snap=snap + 1, first=step == 1, last=False))(x, 0) for x in range(width_x)]
        settle(state_copies)

        def pressure_slab(x, carry, par=par, snap=snap, step=step):
            xp = x + 1
            old = pads.at[par]
            if step == 0:
                p = old[0, xp]
                dxp = (old[0, xp + 1] - old[0, x]) * 0.5
                dyp = dy(p, yrecv[par, 0, Y_SLOT[0], x:x + 1, :], yrecv[par, 1, Y_SLOT[0], x:x + 1, :])
            else:
                held = pbuf.at[1 - par]
                p = held[xp]
                dxp = (held[xp + 1] - held[x]) * 0.5
                dyp = dy(p, yprecv[1 - par, 0, x:x + 1, :], yprecv[1 - par, 1, x:x + 1, :])
            dxa = (old[1, xp + 1] - old[1, x]) * 0.5
            dya = dy(old[2, xp], yrecv[par, 0, Y_SLOT[2], x:x + 1, :], yrecv[par, 1, Y_SLOT[2], x:x + 1, :])
            dzp = dz(p)
            dza = dz(old[3, xp])
            divergence = dxa + dya + dza
            p_new = (
                p
                + step_length * (sound[x] * divergence + we * dxp + wn * dyp + wv * dzp)
                + inj[snap, x]
            )
            pbuf[par, xp] = p_new
            ypsend[0, x:x + 1, :] = p_new[width_y - 1:width_y, :]
            ypsend[1, x:x + 1, :] = p_new[0:1, :]
            return carry

        [pressure_slab(x, 0) for x in range(width_x)]
        pressure_copies = exchange(
            pbuf.at[par, pl.ds(1, 1)], pbuf.at[par, pl.ds(width_x, 1)],
            pbuf.at[par, pl.ds(0, 1)], pbuf.at[par, pl.ds(width_x + 1, 1)],
            ypsend.at[0], ypsend.at[1], yprecv.at[par, 0], yprecv.at[par, 1],
            ps, pr,
        )
        send_forward(snap)
        settle(velocity_copies)

        def advection_slab(x, carry, par=par):
            xp = x + 1
            old = pads.at[par]
            for i in range(3):
                a = old[1 + i, xp]
                dxa = (old[1 + i, xp + 1] - old[1 + i, x]) * 0.5
                dya = dy(a, yrecv[par, 0, Y_SLOT[1 + i], x:x + 1, :], yrecv[par, 1, Y_SLOT[1 + i], x:x + 1, :])
                dza = dz(a)
                advect[i, x] = we * dxa + wn * dya + wv * dza
            return carry

        [advection_slab(x, 0) for x in range(width_x)]
        settle(pressure_copies)

        def velocity_slab(x, carry, par=par, nxt=nxt, last=last):
            xp = x + 1
            old = pads.at[par]
            p_new = pbuf[par, xp]
            grad = (
                (pbuf[par, xp + 1] - pbuf[par, x]) * 0.5,
                dy(p_new, yprecv[par, 0, x:x + 1, :], yprecv[par, 1, x:x + 1, :]),
                dz(p_new),
            )
            new_state = [p_new]
            for i in range(3):
                new_state.append(old[1 + i, xp] + step_length * (grad[i] + advect[i, x]))
            for c in range(4):
                if last:
                    state_out[c, x] = new_state[c]
                else:
                    fill_state(nxt, x, c, new_state[c])
            return carry

        [velocity_slab(x, 0) for x in range(width_x)]

    forward_ready(0, steps == 1)
    [(functools.partial(
        increment_slab, get=lambda c, x: state_out[c, x], snap=0, first=steps == 1, last=True))(x, 0) for x in range(width_x)]

    for x in range(width_x):
        copy = pltpu.make_async_remote_copy(
            src_ref=ksend.at[x], dst_ref=krecv.at[x], send_sem=ks.at[x], recv_sem=kr.at[x],
            device_id=dev_pair, device_id_type=MESH,
        )
        copy.wait_send()
        copy.wait_recv()

    def add_partner(x, carry):
        for c in range(4):
            kernel_out[c, x] = kernel_out[c, x] + krecv[x, c]
        return carry

    [add_partner(x, 0) for x in range(width_x)]


def samples_kernel(nx, ny, local_ref, out_ref, sent, got_x, got_y, send_sem, recv_sem):
    me_p = lax.axis_index("pair")
    gx = lax.axis_index("gx")
    gy = lax.axis_index("gy")
    peers_x = [(me_p, (gx + d) % nx, gy) for d in range(1, nx)]
    peers_y = [(me_p, gx, (gy + d) % ny) for d in range(1, ny)]
    barrier = pltpu.get_barrier_semaphore()
    for dev in peers_x + peers_y:
        pl.semaphore_signal(barrier, 1, device_id=dev, device_id_type=MESH)
    pl.semaphore_wait(barrier, len(peers_x) + len(peers_y))
    rounds = ((local_ref, got_x, peers_x, 0), (sent, got_y, peers_y, nx - 1))
    total = local_ref[...]
    for src, got, peers, base in rounds:
        copies = []
        for i, dev in enumerate(peers):
            copy = pltpu.make_async_remote_copy(
                src_ref=src, dst_ref=got.at[i], send_sem=send_sem.at[base + i],
                recv_sem=recv_sem.at[base + i], device_id=dev, device_id_type=MESH,
            )
            copy.start()
            copies.append(copy)
        for copy in copies:
            copy.wait_send()
            copy.wait_recv()
        for i in range(len(peers)):
            total = total + got[i]
        if base == 0:
            sent[...] = total
    out_ref[...] = total


def gathered_samples(local_samples):
    nx, ny = lax.axis_size("gx"), lax.axis_size("gy")
    if nx < 2 or ny < 2:
        return lax.psum(local_samples, ("gx", "gy"))
    vmem = pl.BlockSpec(memory_space=pltpu.VMEM)
    return pl.pallas_call(
        functools.partial(samples_kernel, nx, ny),
        out_shape=jax.ShapeDtypeStruct(local_samples.shape, jnp.float32),
        in_specs=[vmem],
        out_specs=vmem,
        scratch_shapes=[
            pltpu.VMEM(local_samples.shape, jnp.float32),
            pltpu.VMEM((nx - 1,) + local_samples.shape, jnp.float32),
            pltpu.VMEM((ny - 1,) + local_samples.shape, jnp.float32),
            pltpu.SemaphoreType.DMA((nx + ny - 2,)),
            pltpu.SemaphoreType.DMA((nx + ny - 2,)),
        ],
        compiler_params=pltpu.CompilerParams(collective_id=1, has_side_effects=True),
    )(local_samples)


def shards(
    sound_speed_sq,
    wind_profile,
    forward_field,
    adjoint_state,
    pair_counts,
    source_cells,
    receiver_cells,
    residuals,
):
    steps_total = forward_field.shape[0]
    width_x, width_y, depth = sound_speed_sq.shape
    slots = residuals.shape[0]
    live = (jnp.arange(slots, dtype=jnp.int32) < pair_counts[0]).astype(jnp.float32)
    gx_first = lax.axis_index("gx") * width_x
    gy_first = lax.axis_index("gy") * width_y
    x_range = jnp.arange(width_x, dtype=jnp.int32)
    y_range = jnp.arange(width_y, dtype=jnp.int32)
    z_range = jnp.arange(depth, dtype=jnp.int32)

    def tile_mask(cells):
        on_x = (cells[:, 0][None, :] - gx_first) == x_range[:, None]
        on_y = (cells[:, 1][None, :] - gy_first) == y_range[:, None]
        return (on_x[:, None, :] & on_y[None, :, :]).astype(jnp.float32)

    source_z = (source_cells[:, 2][None, :] == z_range[:, None]).astype(jnp.bfloat16)
    along_z = jnp.einsum(
        "txyz,zn->txyn", forward_field[:, 0], source_z, preferred_element_type=jnp.float32
    )
    local_samples = jnp.sum(along_z * tile_mask(source_cells)[None], axis=(1, 2))
    samples = gathered_samples(local_samples)
    amplitude = jnp.transpose(residuals) * samples * live[None, :]
    spread = amplitude[:, None, None, :] * tile_mask(receiver_cells)[None]
    receiver_z = (receiver_cells[:, 2][:, None] == z_range[None, :]).astype(jnp.float32)
    injected = jnp.einsum(
        "txyn,nz->txyz", spread, receiver_z, precision=lax.Precision.HIGHEST,
        preferred_element_type=jnp.float32,
    )
    vmem = pl.BlockSpec(memory_space=pltpu.VMEM)
    kernel = functools.partial(
        stencil_kernel, lax.axis_size("gx"), lax.axis_size("gy"), steps_total
    )
    state_new, kernels = pl.pallas_call(
        kernel,
        out_shape=(
            jax.ShapeDtypeStruct((4, width_x, width_y, depth), jnp.float32),
            jax.ShapeDtypeStruct((4, width_x, width_y, depth // 2), jnp.float32),
        ),
        in_specs=[vmem] * 5,
        out_specs=(vmem, vmem),
        scratch_shapes=[
            pltpu.VMEM((2, 4, width_x + 2, width_y, depth), jnp.float32),
            pltpu.VMEM((2, width_x + 2, width_y, depth), jnp.float32),
            pltpu.VMEM((2, 2, 4, width_x, depth), jnp.float32),
            pltpu.VMEM((2, 2, 4, width_x, depth), jnp.float32),
            pltpu.VMEM((2, width_x, depth), jnp.float32),
            pltpu.VMEM((2, 2, width_x, depth), jnp.float32),
            pltpu.VMEM((4, width_x, width_y, depth), jnp.float32),
            pltpu.VMEM((width_x, 4, width_y, depth // 2), jnp.float32),
            pltpu.VMEM((width_x, 4, width_y, depth // 2), jnp.float32),
            pltpu.VMEM((steps_total, 4, width_x + 2, width_y, depth), forward_field.dtype),
            pltpu.VMEM((2, steps_total, 2, 2 * width_x, depth), forward_field.dtype),
            pltpu.VMEM((2, steps_total, 2, 2 * width_x, depth), forward_field.dtype),
            pltpu.VMEM((3, width_x, width_y, depth), jnp.float32),
            pltpu.SemaphoreType.DMA((2, 2, 4)),
            pltpu.SemaphoreType.DMA((2, 2, 4)),
            pltpu.SemaphoreType.DMA((4,)),
            pltpu.SemaphoreType.DMA((4,)),
            pltpu.SemaphoreType.DMA((width_x,)),
            pltpu.SemaphoreType.DMA((width_x,)),
            pltpu.SemaphoreType.DMA((steps_total, 4)),
            pltpu.SemaphoreType.DMA((steps_total, 4)),
            pltpu.SemaphoreType.DMA((1,)),
        ],
        compiler_params=pltpu.CompilerParams(
            collective_id=0, has_side_effects=True, vmem_limit_bytes=48 * 1024 * 1024
        ),
    )(adjoint_state[0], sound_speed_sq, wind_profile, forward_field, injected)
    return (kernels, state_new[None])


def solution(mesh):
    in_specs = (
        P("gx", "gy", None),
        P(),
        P(None, None, "gx", "gy", None),
        P("pair", None, "gx", "gy", None),
        P("pair"),
        P("pair", None),
        P("pair", None),
        P("pair", None),
    )
    out_specs = (P(None, "gx", "gy", "pair"), P("pair", None, "gx", "gy", None))
    return jax.shard_map(shards, mesh=mesh, in_specs=in_specs, out_specs=out_specs, check_vma=False)
```

```python
import functools

import jax
import jax.numpy as jnp
from jax import lax
from jax.experimental import pallas as pl
from jax.experimental.pallas import tpu as pltpu
from jax.sharding import PartitionSpec as P

step_length = 0.25
Y_SLOT = (0, 2, 1, 3)
MESH = pl.DeviceIdType.MESH


def neighbours(shard, axis, dim):
    size, length = (lax.axis_size(axis), shard.shape[dim])
    up = [(i, i + 1) for i in range(size - 1)]
    down = [(i + 1, i) for i in range(size - 1)]
    last = lax.slice_in_dim(shard, length - 1, length, axis=dim)
    first = lax.slice_in_dim(shard, 0, 1, axis=dim)
    before = lax.ppermute(last, axis, up)
    after = lax.ppermute(first, axis, down)
    return (before, after)


def local_cells(cells, width_x, width_y):
    local_x = cells[:, 0] - lax.axis_index("gx") * width_x
    local_y = cells[:, 1] - lax.axis_index("gy") * width_y
    inside = (local_x >= 0) & (local_x < width_x) & (local_y >= 0) & (local_y < width_y)
    return (
        jnp.clip(local_x, 0, width_x - 1),
        jnp.clip(local_y, 0, width_y - 1),
        cells[:, 2],
        inside.astype(jnp.float32),
    )


def stencil_kernel(
    nx, ny, steps,
    state_in, sound, wind, forward, inj,
    state_out, kernel_out,
    pads, pbuf, ysend, yrecv, ypsend, yprecv, acc_out, ksend, krecv, fpad, fysend, fyr, advect, early,
    ss, rs, ps, pr, ks, kr, fs, fr, local_sem,
):
    _, width_x, width_y, depth = state_in.shape
    me_p = lax.axis_index("pair")
    gx = lax.axis_index("gx")
    gy = lax.axis_index("gy")
    has_lo_x = gx > 0
    has_hi_x = gx < nx - 1
    has_lo_y = gy > 0
    has_hi_y = gy < ny - 1
    dev_lo_x = (me_p, gx - 1, gy)
    dev_hi_x = (me_p, gx + 1, gy)
    dev_lo_y = (me_p, gx, gy - 1)
    dev_hi_y = (me_p, gx, gy + 1)
    dev_pair = (1 - me_p, gx, gy)
    half = depth // 2

    zero_slab = jnp.zeros((width_y, depth), jnp.float32)
    for par in range(2):
        for c in range(4):
            pads[par, c, 0] = zero_slab
            pads[par, c, width_x + 1] = zero_slab
            for side in range(2):
                yrecv[par, side, c] = jnp.zeros((width_x, depth), jnp.float32)
    for par in range(2):
        pbuf[par, 0] = zero_slab
        pbuf[par, width_x + 1] = zero_slab
    zero_forward = jnp.zeros((width_y, depth), fpad.dtype)
    for t in range(steps):
        for c in range(4):
            fpad[t, c, 0] = zero_forward
            fpad[t, c, width_x + 1] = zero_forward
            for side in range(2):
                fyr[side, t, c // 2, pl.ds((c % 2) * width_x, width_x), :] = jnp.zeros((width_x, depth), fyr.dtype)

    def forward_rows(x, carry):
        for t in range(steps):
            for c in range(4):
                f = forward[t, c, x]
                row = (c % 2) * width_x + x
                fysend[0, t, c // 2, row:row + 1, :] = f[width_y - 1:width_y, :]
                fysend[1, t, c // 2, row:row + 1, :] = f[0:1, :]
        return carry

    [forward_rows(x, 0) for x in range(width_x)]
    interior = pltpu.make_async_copy(forward, fpad.at[:, :, pl.ds(1, width_x)], local_sem.at[0])
    interior.start()
    for par in range(2):
        for side in range(2):
            yprecv[par, side] = jnp.zeros((width_x, depth), jnp.float32)

    barrier = pltpu.get_barrier_semaphore()
    pl.semaphore_signal(barrier, 1, device_id=dev_pair, device_id_type=MESH)
    for cond, dev in ((has_lo_x, dev_lo_x), (has_hi_x, dev_hi_x), (has_lo_y, dev_lo_y), (has_hi_y, dev_hi_y)):
        @pl.when(cond)
        def _():
            pl.semaphore_signal(barrier, 1, device_id=dev, device_id_type=MESH)
    peers = 1 + (
        (gx + nx - 1) // nx + (2 * nx - 2 - gx) // nx
        + (gy + ny - 1) // ny + (2 * ny - 2 - gy) // ny
    )
    pl.semaphore_wait(barrier, peers)

    iy = lax.broadcasted_iota(jnp.int32, (width_y, depth), 0)
    iz = lax.broadcasted_iota(jnp.int32, (width_y, depth), 1)
    we = wind[0:1, :]
    wn = wind[1:2, :]
    wv = wind[2:3, :]

    def dy(v, lo, hi):
        up = jnp.where(iy == width_y - 1, hi, pltpu.roll(v, width_y - 1, 0))
        down = jnp.where(iy == 0, lo, pltpu.roll(v, 1, 0))
        return (up - down) * 0.5

    def dz(v):
        up = jnp.where(iz == depth - 1, 0.0, pltpu.roll(v, depth - 1, 1))
        down = jnp.where(iz == 0, 0.0, pltpu.roll(v, 1, 1))
        return (up - down) * 0.5

    def exchange(src_lo_x, src_hi_x, dst_lo_x, dst_hi_x, src_y_hi, src_y_lo, dst_y_lo, dst_y_hi, send, recv):
        outs = (
            (has_hi_x, src_hi_x, dst_lo_x, 0, dev_hi_x),
            (has_lo_x, src_lo_x, dst_hi_x, 1, dev_lo_x),
            (has_hi_y, src_y_hi, dst_y_lo, 2, dev_hi_y),
            (has_lo_y, src_y_lo, dst_y_hi, 3, dev_lo_y),
        )
        copies = []
        for cond, src, dst, slot, dev in outs:
            copy = pltpu.make_async_remote_copy(
                src_ref=src, dst_ref=dst, send_sem=send.at[slot], recv_sem=recv.at[slot],
                device_id=dev, device_id_type=MESH,
            )
            copies.append((cond, copy))

            @pl.when(cond)
            def _():
                copy.start()
        return copies

    def settle(copies):
        incoming = (has_lo_x, has_hi_x, has_lo_y, has_hi_y)
        for (cond, copy), arrives in zip(copies, incoming):
            @pl.when(cond)
            def _():
                copy.wait_send()

            @pl.when(arrives)
            def _():
                copy.wait_recv()

    def fill_state(par, x, c, v):
        pads[par, c, x + 1] = v
        ysend[par, 0, Y_SLOT[c], x:x + 1, :] = v[width_y - 1:width_y, :]
        ysend[par, 1, Y_SLOT[c], x:x + 1, :] = v[0:1, :]

    def copy_in(x, carry):
        for c in range(4):
            fill_state(0, x, c, state_in[c, x])
        return carry

    [copy_in(x, 0) for x in range(width_x)]
    forward_copies = {}

    def send_forward(t):
        forward_copies[t] = exchange(
            forward.at[t, :, pl.ds(0, 1)], forward.at[t, :, pl.ds(width_x - 1, 1)],
            fpad.at[t, :, pl.ds(0, 1)], fpad.at[t, :, pl.ds(width_x + 1, 1)],
            fysend.at[0, t], fysend.at[1, t], fyr.at[0, t], fyr.at[1, t], fs.at[t], fr.at[t],
        )

    def increment_slab(x, carry, get, snap, first, last):
        xp = x + 1
        p_new = get(0, x)
        a_new = [get(1 + i, x) for i in range(3)]
        fe, fn, fu = [], [], []
        for c in range(4):
            f = fpad[snap, c, xp].astype(jnp.float32)
            fe.append((fpad[snap, c, xp + 1].astype(jnp.float32) - fpad[snap, c, x].astype(jnp.float32)) * 0.5)
            row = (c % 2) * width_x + x
            fn.append(dy(f, fyr[0, snap, c // 2, row:row + 1, :].astype(jnp.float32),
                         fyr[1, snap, c // 2, row:row + 1, :].astype(jnp.float32)))
            fu.append(dz(f))
        pieces = [p_new * (fe[1] + fn[2] + fu[3])]
        for along in (fe, fn, fu):
            pieces.append(p_new * along[0] + a_new[0] * along[1] + a_new[1] * along[2] + a_new[2] * along[3])
        for c in range(4):
            total = pieces[c] if first else acc_out[c, x] + pieces[c]
            if not last:
                acc_out[c, x] = total
                continue
            low, high = total[:, :half], total[:, half:]
            kernel_out[c, x] = jnp.where(me_p == 0, low, high)
            ksend[x, c] = jnp.where(me_p == 0, high, low)
        if last:
            pltpu.make_async_remote_copy(
                src_ref=ksend.at[x], dst_ref=krecv.at[x], send_sem=ks.at[x], recv_sem=kr.at[x],
                device_id=dev_pair, device_id_type=MESH,
            ).start()
        return carry

    def forward_ready(t, first):
        if first:
            interior.wait()
        settle(forward_copies[t])

    for step in range(steps):
        par = step % 2
        nxt = 1 - par
        snap = steps - 1 - step
        last = step == steps - 1
        halves = []
        for part in range(2):
            comps = pl.ds(2 * part, 2) if (part or step == 0) else pl.ds(1, 1)
            halves.append(exchange(
                pads.at[par, comps, pl.ds(1, 1)], pads.at[par, comps, pl.ds(width_x, 1)],
                pads.at[par, comps, pl.ds(0, 1)], pads.at[par, comps, pl.ds(width_x + 1, 1)],
                ysend.at[par, 0, comps], ysend.at[par, 1, comps],
                yrecv.at[par, 0, comps], yrecv.at[par, 1, comps],
                ss.at[par, part], rs.at[par, part],
            ))
        state_copies, velocity_copies = halves
        if step > 0:
            forward_ready(snap + 1, step == 1)
            [(functools.partial(
                increment_slab, get=lambda c, x, par=par: pads[par, c, x + 1],
                snap=snap + 1, first=step == 1, last=False))(x, 0) for x in range(width_x)]
        if step > 0:
            def early_slab(x, carry, par=par):
                xp = x + 1
                held = pbuf.at[1 - par]
                p = held[xp]
                dxp = (held[xp + 1] - held[x]) * 0.5
                dyp = dy(p, yprecv[1 - par, 0, x:x + 1, :], yprecv[1 - par, 1, x:x + 1, :])
                early[0, x] = we * dxp + wn * dyp + wv * dz(p)
                early[1, x] = dz(pads[par, 3, xp])
                return carry

            [early_slab(x, 0) for x in range(width_x)]
        settle(state_copies)

        def pressure_slab(x, carry, par=par, snap=snap, step=step):
            xp = x + 1
            old = pads.at[par]
            dxa = (old[1, xp + 1] - old[1, x]) * 0.5
            dya = dy(old[2, xp], yrecv[par, 0, Y_SLOT[2], x:x + 1, :], yrecv[par, 1, Y_SLOT[2], x:x + 1, :])
            if step == 0:
                p = old[0, xp]
                dxp = (old[0, xp + 1] - old[0, x]) * 0.5
                dyp = dy(p, yrecv[par, 0, Y_SLOT[0], x:x + 1, :], yrecv[par, 1, Y_SLOT[0], x:x + 1, :])
                rest = we * dxp + wn * dyp + wv * dz(p)
                dza = dz(old[3, xp])
            else:
                p = pbuf[1 - par, xp]
                rest = early[0, x]
                dza = early[1, x]
            divergence = dxa + dya + dza
            p_new = p + step_length * (sound[x] * divergence + rest) + inj[snap, x]
            pbuf[par, xp] = p_new
            ypsend[0, x:x + 1, :] = p_new[width_y - 1:width_y, :]
            ypsend[1, x:x + 1, :] = p_new[0:1, :]
            return carry

        [pressure_slab(x, 0) for x in range(width_x)]
        pressure_copies = exchange(
            pbuf.at[par, pl.ds(1, 1)], pbuf.at[par, pl.ds(width_x, 1)],
            pbuf.at[par, pl.ds(0, 1)], pbuf.at[par, pl.ds(width_x + 1, 1)],
            ypsend.at[0], ypsend.at[1], yprecv.at[par, 0], yprecv.at[par, 1],
            ps, pr,
        )
        send_forward(snap)
        settle(velocity_copies)

        def advection_slab(x, carry, par=par):
            xp = x + 1
            old = pads.at[par]
            for i in range(3):
                a = old[1 + i, xp]
                dxa = (old[1 + i, xp + 1] - old[1 + i, x]) * 0.5
                dya = dy(a, yrecv[par, 0, Y_SLOT[1 + i], x:x + 1, :], yrecv[par, 1, Y_SLOT[1 + i], x:x + 1, :])
                dza = dz(a)
                advect[i, x] = we * dxa + wn * dya + wv * dza
            return carry

        [advection_slab(x, 0) for x in range(width_x)]
        settle(pressure_copies)

        def velocity_slab(x, carry, par=par, nxt=nxt, last=last):
            xp = x + 1
            old = pads.at[par]
            p_new = pbuf[par, xp]
            grad = (
                (pbuf[par, xp + 1] - pbuf[par, x]) * 0.5,
                dy(p_new, yprecv[par, 0, x:x + 1, :], yprecv[par, 1, x:x + 1, :]),
                dz(p_new),
            )
            new_state = [p_new]
            for i in range(3):
                new_state.append(old[1 + i, xp] + step_length * (grad[i] + advect[i, x]))
            for c in range(4):
                if last:
                    state_out[c, x] = new_state[c]
                else:
                    fill_state(nxt, x, c, new_state[c])
            return carry

        [velocity_slab(x, 0) for x in range(width_x)]

    forward_ready(0, steps == 1)
    [(functools.partial(
        increment_slab, get=lambda c, x: state_out[c, x], snap=0, first=steps == 1, last=True))(x, 0) for x in range(width_x)]

    for x in range(width_x):
        copy = pltpu.make_async_remote_copy(
            src_ref=ksend.at[x], dst_ref=krecv.at[x], send_sem=ks.at[x], recv_sem=kr.at[x],
            device_id=dev_pair, device_id_type=MESH,
        )
        copy.wait_send()
        copy.wait_recv()

    def add_partner(x, carry):
        for c in range(4):
            kernel_out[c, x] = kernel_out[c, x] + krecv[x, c]
        return carry

    [add_partner(x, 0) for x in range(width_x)]


def samples_kernel(nx, ny, local_ref, out_ref, sent, got_x, got_y, send_sem, recv_sem):
    me_p = lax.axis_index("pair")
    gx = lax.axis_index("gx")
    gy = lax.axis_index("gy")
    peers_x = [(me_p, (gx + d) % nx, gy) for d in range(1, nx)]
    peers_y = [(me_p, gx, (gy + d) % ny) for d in range(1, ny)]
    barrier = pltpu.get_barrier_semaphore()
    for dev in peers_x + peers_y:
        pl.semaphore_signal(barrier, 1, device_id=dev, device_id_type=MESH)
    pl.semaphore_wait(barrier, len(peers_x) + len(peers_y))
    rounds = ((local_ref, got_x, peers_x, 0), (sent, got_y, peers_y, nx - 1))
    total = local_ref[...]
    for src, got, peers, base in rounds:
        copies = []
        for i, dev in enumerate(peers):
            copy = pltpu.make_async_remote_copy(
                src_ref=src, dst_ref=got.at[i], send_sem=send_sem.at[base + i],
                recv_sem=recv_sem.at[base + i], device_id=dev, device_id_type=MESH,
            )
            copy.start()
            copies.append(copy)
        for copy in copies:
            copy.wait_send()
            copy.wait_recv()
        for i in range(len(peers)):
            total = total + got[i]
        if base == 0:
            sent[...] = total
    out_ref[...] = total


def gathered_samples(local_samples):
    nx, ny = lax.axis_size("gx"), lax.axis_size("gy")
    if nx < 2 or ny < 2:
        return lax.psum(local_samples, ("gx", "gy"))
    vmem = pl.BlockSpec(memory_space=pltpu.VMEM)
    return pl.pallas_call(
        functools.partial(samples_kernel, nx, ny),
        out_shape=jax.ShapeDtypeStruct(local_samples.shape, jnp.float32),
        in_specs=[vmem],
        out_specs=vmem,
        scratch_shapes=[
            pltpu.VMEM(local_samples.shape, jnp.float32),
            pltpu.VMEM((nx - 1,) + local_samples.shape, jnp.float32),
            pltpu.VMEM((ny - 1,) + local_samples.shape, jnp.float32),
            pltpu.SemaphoreType.DMA((nx + ny - 2,)),
            pltpu.SemaphoreType.DMA((nx + ny - 2,)),
        ],
        compiler_params=pltpu.CompilerParams(collective_id=1, has_side_effects=True),
    )(local_samples)


def shards(
    sound_speed_sq,
    wind_profile,
    forward_field,
    adjoint_state,
    pair_counts,
    source_cells,
    receiver_cells,
    residuals,
):
    steps_total = forward_field.shape[0]
    width_x, width_y, depth = sound_speed_sq.shape
    slots = residuals.shape[0]
    live = (jnp.arange(slots, dtype=jnp.int32) < pair_counts[0]).astype(jnp.float32)
    gx_first = lax.axis_index("gx") * width_x
    gy_first = lax.axis_index("gy") * width_y
    x_range = jnp.arange(width_x, dtype=jnp.int32)
    y_range = jnp.arange(width_y, dtype=jnp.int32)
    z_range = jnp.arange(depth, dtype=jnp.int32)

    def tile_mask(cells):
        on_x = (cells[:, 0][None, :] - gx_first) == x_range[:, None]
        on_y = (cells[:, 1][None, :] - gy_first) == y_range[:, None]
        return (on_x[:, None, :] & on_y[None, :, :]).astype(jnp.float32)

    source_z = (source_cells[:, 2][None, :] == z_range[:, None]).astype(jnp.bfloat16)
    along_z = jnp.einsum(
        "txyz,zn->txyn", forward_field[:, 0], source_z, preferred_element_type=jnp.float32
    )
    local_samples = jnp.sum(along_z * tile_mask(source_cells)[None], axis=(1, 2))
    samples = gathered_samples(local_samples)
    amplitude = jnp.transpose(residuals) * samples * live[None, :]
    spread = amplitude[:, None, None, :] * tile_mask(receiver_cells)[None]
    receiver_z = (receiver_cells[:, 2][:, None] == z_range[None, :]).astype(jnp.float32)
    injected = jnp.einsum(
        "txyn,nz->txyz", spread, receiver_z, precision=lax.Precision.HIGHEST,
        preferred_element_type=jnp.float32,
    )
    vmem = pl.BlockSpec(memory_space=pltpu.VMEM)
    kernel = functools.partial(
        stencil_kernel, lax.axis_size("gx"), lax.axis_size("gy"), steps_total
    )
    state_new, kernels = pl.pallas_call(
        kernel,
        out_shape=(
            jax.ShapeDtypeStruct((4, width_x, width_y, depth), jnp.float32),
            jax.ShapeDtypeStruct((4, width_x, width_y, depth // 2), jnp.float32),
        ),
        in_specs=[vmem] * 5,
        out_specs=(vmem, vmem),
        scratch_shapes=[
            pltpu.VMEM((2, 4, width_x + 2, width_y, depth), jnp.float32),
            pltpu.VMEM((2, width_x + 2, width_y, depth), jnp.float32),
            pltpu.VMEM((2, 2, 4, width_x, depth), jnp.float32),
            pltpu.VMEM((2, 2, 4, width_x, depth), jnp.float32),
            pltpu.VMEM((2, width_x, depth), jnp.float32),
            pltpu.VMEM((2, 2, width_x, depth), jnp.float32),
            pltpu.VMEM((4, width_x, width_y, depth), jnp.float32),
            pltpu.VMEM((width_x, 4, width_y, depth // 2), jnp.float32),
            pltpu.VMEM((width_x, 4, width_y, depth // 2), jnp.float32),
            pltpu.VMEM((steps_total, 4, width_x + 2, width_y, depth), forward_field.dtype),
            pltpu.VMEM((2, steps_total, 2, 2 * width_x, depth), forward_field.dtype),
            pltpu.VMEM((2, steps_total, 2, 2 * width_x, depth), forward_field.dtype),
            pltpu.VMEM((3, width_x, width_y, depth), jnp.float32),
            pltpu.VMEM((2, width_x, width_y, depth), jnp.float32),
            pltpu.SemaphoreType.DMA((2, 2, 4)),
            pltpu.SemaphoreType.DMA((2, 2, 4)),
            pltpu.SemaphoreType.DMA((4,)),
            pltpu.SemaphoreType.DMA((4,)),
            pltpu.SemaphoreType.DMA((width_x,)),
            pltpu.SemaphoreType.DMA((width_x,)),
            pltpu.SemaphoreType.DMA((steps_total, 4)),
            pltpu.SemaphoreType.DMA((steps_total, 4)),
            pltpu.SemaphoreType.DMA((1,)),
        ],
        compiler_params=pltpu.CompilerParams(
            collective_id=0, has_side_effects=True, vmem_limit_bytes=48 * 1024 * 1024
        ),
    )(adjoint_state[0], sound_speed_sq, wind_profile, forward_field, injected)
    return (kernels, state_new[None])


def solution(mesh):
    in_specs = (
        P("gx", "gy", None),
        P(),
        P(None, None, "gx", "gy", None),
        P("pair", None, "gx", "gy", None),
        P("pair"),
        P("pair", None),
        P("pair", None),
        P("pair", None),
    )
    out_specs = (P(None, "gx", "gy", "pair"), P("pair", None, "gx", "gy", None))
    return jax.shard_map(shards, mesh=mesh, in_specs=in_specs, out_specs=out_specs, check_vma=False)
```

```python
import functools

import jax
import jax.numpy as jnp
from jax import lax
from jax.experimental import pallas as pl
from jax.experimental.pallas import tpu as pltpu
from jax.sharding import PartitionSpec as P

step_length = 0.25
Y_SLOT = (0, 2, 1, 3)
MESH = pl.DeviceIdType.MESH


def neighbours(shard, axis, dim):
    size, length = (lax.axis_size(axis), shard.shape[dim])
    up = [(i, i + 1) for i in range(size - 1)]
    down = [(i + 1, i) for i in range(size - 1)]
    last = lax.slice_in_dim(shard, length - 1, length, axis=dim)
    first = lax.slice_in_dim(shard, 0, 1, axis=dim)
    before = lax.ppermute(last, axis, up)
    after = lax.ppermute(first, axis, down)
    return (before, after)


def local_cells(cells, width_x, width_y):
    local_x = cells[:, 0] - lax.axis_index("gx") * width_x
    local_y = cells[:, 1] - lax.axis_index("gy") * width_y
    inside = (local_x >= 0) & (local_x < width_x) & (local_y >= 0) & (local_y < width_y)
    return (
        jnp.clip(local_x, 0, width_x - 1),
        jnp.clip(local_y, 0, width_y - 1),
        cells[:, 2],
        inside.astype(jnp.float32),
    )


def stencil_kernel(
    nx, ny, steps,
    state_in, sound, wind, forward, inj,
    state_out, kernel_out,
    pads, pbuf, ysend, yrecv, ypsend, yprecv, acc_out, ksend, krecv, fpad, fysend, fyr, advect, early,
    ss, rs, ps, pr, ks, kr, fs, fr, local_sem,
):
    _, width_x, width_y, depth = state_in.shape
    me_p = lax.axis_index("pair")
    gx = lax.axis_index("gx")
    gy = lax.axis_index("gy")
    has_lo_x = gx > 0
    has_hi_x = gx < nx - 1
    has_lo_y = gy > 0
    has_hi_y = gy < ny - 1
    dev_lo_x = (me_p, gx - 1, gy)
    dev_hi_x = (me_p, gx + 1, gy)
    dev_lo_y = (me_p, gx, gy - 1)
    dev_hi_y = (me_p, gx, gy + 1)
    dev_pair = (1 - me_p, gx, gy)
    half = depth // 2

    zero_slab = jnp.zeros((width_y, depth), jnp.float32)
    for par in range(2):
        for c in range(4):
            pads[par, c, 0] = zero_slab
            pads[par, c, width_x + 1] = zero_slab
            for side in range(2):
                yrecv[par, side, c] = jnp.zeros((width_x, depth), jnp.float32)
    for par in range(2):
        pbuf[par, 0] = zero_slab
        pbuf[par, width_x + 1] = zero_slab
    zero_forward = jnp.zeros((width_y, depth), fpad.dtype)
    for t in range(steps):
        for c in range(4):
            fpad[t, c, 0] = zero_forward
            fpad[t, c, width_x + 1] = zero_forward
            for side in range(2):
                fyr[side, t, c // 2, pl.ds((c % 2) * width_x, width_x), :] = jnp.zeros((width_x, depth), fyr.dtype)

    def forward_rows(x, carry):
        for t in range(steps):
            for c in range(4):
                f = forward[t, c, x]
                row = (c % 2) * width_x + x
                fysend[0, t, c // 2, row:row + 1, :] = f[width_y - 1:width_y, :]
                fysend[1, t, c // 2, row:row + 1, :] = f[0:1, :]
        return carry

    [forward_rows(x, 0) for x in range(width_x)]
    interior = pltpu.make_async_copy(forward, fpad.at[:, :, pl.ds(1, width_x)], local_sem.at[0])
    interior.start()
    for par in range(2):
        for side in range(2):
            yprecv[par, side] = jnp.zeros((width_x, depth), jnp.float32)

    barrier = pltpu.get_barrier_semaphore()
    pl.semaphore_signal(barrier, 1, device_id=dev_pair, device_id_type=MESH)
    for cond, dev in ((has_lo_x, dev_lo_x), (has_hi_x, dev_hi_x), (has_lo_y, dev_lo_y), (has_hi_y, dev_hi_y)):
        @pl.when(cond)
        def _():
            pl.semaphore_signal(barrier, 1, device_id=dev, device_id_type=MESH)
    peers = 1 + (
        (gx + nx - 1) // nx + (2 * nx - 2 - gx) // nx
        + (gy + ny - 1) // ny + (2 * ny - 2 - gy) // ny
    )
    pl.semaphore_wait(barrier, peers)

    iy = lax.broadcasted_iota(jnp.int32, (width_y, depth), 0)
    iz = lax.broadcasted_iota(jnp.int32, (width_y, depth), 1)
    we = wind[0:1, :]
    wn = wind[1:2, :]
    wv = wind[2:3, :]

    def dy(v, lo, hi):
        up = jnp.where(iy == width_y - 1, hi, pltpu.roll(v, width_y - 1, 0))
        down = jnp.where(iy == 0, lo, pltpu.roll(v, 1, 0))
        return (up - down) * 0.5

    def dz(v):
        up = jnp.where(iz == depth - 1, 0.0, pltpu.roll(v, depth - 1, 1))
        down = jnp.where(iz == 0, 0.0, pltpu.roll(v, 1, 1))
        return (up - down) * 0.5

    def exchange(src_lo_x, src_hi_x, dst_lo_x, dst_hi_x, src_y_hi, src_y_lo, dst_y_lo, dst_y_hi, send, recv):
        outs = (
            (has_hi_x, src_hi_x, dst_lo_x, 0, dev_hi_x),
            (has_lo_x, src_lo_x, dst_hi_x, 1, dev_lo_x),
            (has_hi_y, src_y_hi, dst_y_lo, 2, dev_hi_y),
            (has_lo_y, src_y_lo, dst_y_hi, 3, dev_lo_y),
        )
        copies = []
        for cond, src, dst, slot, dev in outs:
            copy = pltpu.make_async_remote_copy(
                src_ref=src, dst_ref=dst, send_sem=send.at[slot], recv_sem=recv.at[slot],
                device_id=dev, device_id_type=MESH,
            )
            copies.append((cond, copy))

            @pl.when(cond)
            def _():
                copy.start()
        return copies

    def settle(copies):
        incoming = (has_lo_x, has_hi_x, has_lo_y, has_hi_y)
        for (cond, copy), arrives in zip(copies, incoming):
            @pl.when(cond)
            def _():
                copy.wait_send()

            @pl.when(arrives)
            def _():
                copy.wait_recv()

    def fill_state(par, x, c, v):
        pads[par, c, x + 1] = v
        ysend[par, 0, Y_SLOT[c], x:x + 1, :] = v[width_y - 1:width_y, :]
        ysend[par, 1, Y_SLOT[c], x:x + 1, :] = v[0:1, :]

    def copy_in(x, carry):
        for c in range(4):
            fill_state(0, x, c, state_in[c, x])
        return carry

    [copy_in(x, 0) for x in range(width_x)]
    forward_copies = {}

    def send_forward(t):
        forward_copies[t] = exchange(
            forward.at[t, :, pl.ds(0, 1)], forward.at[t, :, pl.ds(width_x - 1, 1)],
            fpad.at[t, :, pl.ds(0, 1)], fpad.at[t, :, pl.ds(width_x + 1, 1)],
            fysend.at[0, t], fysend.at[1, t], fyr.at[0, t], fyr.at[1, t], fs.at[t], fr.at[t],
        )

    def increment_slab(x, carry, get, snap, first, last):
        xp = x + 1
        p_new = get(0, x)
        a_new = [get(1 + i, x) for i in range(3)]
        fe, fn, fu = [], [], []
        for c in range(4):
            f = fpad[snap, c, xp].astype(jnp.float32)
            fe.append((fpad[snap, c, xp + 1].astype(jnp.float32) - fpad[snap, c, x].astype(jnp.float32)) * 0.5)
            row = (c % 2) * width_x + x
            fn.append(dy(f, fyr[0, snap, c // 2, row:row + 1, :].astype(jnp.float32),
                         fyr[1, snap, c // 2, row:row + 1, :].astype(jnp.float32)))
            fu.append(dz(f))
        pieces = [p_new * (fe[1] + fn[2] + fu[3])]
        for along in (fe, fn, fu):
            pieces.append(p_new * along[0] + a_new[0] * along[1] + a_new[1] * along[2] + a_new[2] * along[3])
        for c in range(4):
            total = pieces[c] if first else acc_out[c, x] + pieces[c]
            if not last:
                acc_out[c, x] = total
                continue
            low, high = total[:, :half], total[:, half:]
            kernel_out[c, x] = jnp.where(me_p == 0, low, high)
            ksend[x, c] = jnp.where(me_p == 0, high, low)
        if last:
            pltpu.make_async_remote_copy(
                src_ref=ksend.at[x], dst_ref=krecv.at[x], send_sem=ks.at[x], recv_sem=kr.at[x],
                device_id=dev_pair, device_id_type=MESH,
            ).start()
        return carry

    def forward_ready(t, first):
        if first:
            interior.wait()
        settle(forward_copies[t])

    for step in range(steps):
        par = step % 2
        nxt = 1 - par
        snap = steps - 1 - step
        last = step == steps - 1
        halves = []
        for part in range(2):
            comps = pl.ds(2 * part, 2) if (part or step == 0) else pl.ds(1, 1)
            halves.append(exchange(
                pads.at[par, comps, pl.ds(1, 1)], pads.at[par, comps, pl.ds(width_x, 1)],
                pads.at[par, comps, pl.ds(0, 1)], pads.at[par, comps, pl.ds(width_x + 1, 1)],
                ysend.at[par, 0, comps], ysend.at[par, 1, comps],
                yrecv.at[par, 0, comps], yrecv.at[par, 1, comps],
                ss.at[par, part], rs.at[par, part],
            ))
        state_copies, velocity_copies = halves
        if step > 0:
            forward_ready(snap + 1, step == 1)
            [(functools.partial(
                increment_slab, get=lambda c, x, par=par: pads[par, c, x + 1],
                snap=snap + 1, first=step == 1, last=False))(x, 0) for x in range(width_x)]
        if step > 0:
            def early_slab(x, carry, par=par):
                xp = x + 1
                held = pbuf.at[1 - par]
                p = held[xp]
                dxp = (held[xp + 1] - held[x]) * 0.5
                dyp = dy(p, yprecv[1 - par, 0, x:x + 1, :], yprecv[1 - par, 1, x:x + 1, :])
                early[0, x] = we * dxp + wn * dyp + wv * dz(p)
                early[1, x] = dz(pads[par, 3, xp])
                return carry

            [early_slab(x, 0) for x in range(width_x)]
        settle(state_copies)

        def pressure_slab(x, carry, par=par, snap=snap, step=step):
            xp = x + 1
            old = pads.at[par]
            dxa = (old[1, xp + 1] - old[1, x]) * 0.5
            dya = dy(old[2, xp], yrecv[par, 0, Y_SLOT[2], x:x + 1, :], yrecv[par, 1, Y_SLOT[2], x:x + 1, :])
            if step == 0:
                p = old[0, xp]
                dxp = (old[0, xp + 1] - old[0, x]) * 0.5
                dyp = dy(p, yrecv[par, 0, Y_SLOT[0], x:x + 1, :], yrecv[par, 1, Y_SLOT[0], x:x + 1, :])
                rest = we * dxp + wn * dyp + wv * dz(p)
                dza = dz(old[3, xp])
            else:
                p = pbuf[1 - par, xp]
                rest = early[0, x]
                dza = early[1, x]
            divergence = dxa + dya + dza
            p_new = p + step_length * (sound[x] * divergence + rest) + inj[snap, x]
            pbuf[par, xp] = p_new
            ypsend[0, x:x + 1, :] = p_new[width_y - 1:width_y, :]
            ypsend[1, x:x + 1, :] = p_new[0:1, :]
            return carry

        [pressure_slab(x, 0) for x in range(width_x)]
        pressure_copies = exchange(
            pbuf.at[par, pl.ds(1, 1)], pbuf.at[par, pl.ds(width_x, 1)],
            pbuf.at[par, pl.ds(0, 1)], pbuf.at[par, pl.ds(width_x + 1, 1)],
            ypsend.at[0], ypsend.at[1], yprecv.at[par, 0], yprecv.at[par, 1],
            ps, pr,
        )
        send_forward(snap)
        settle(velocity_copies)

        def advection_slab(x, carry, par=par):
            xp = x + 1
            old = pads.at[par]
            for i in range(3):
                a = old[1 + i, xp]
                dxa = (old[1 + i, xp + 1] - old[1 + i, x]) * 0.5
                dya = dy(a, yrecv[par, 0, Y_SLOT[1 + i], x:x + 1, :], yrecv[par, 1, Y_SLOT[1 + i], x:x + 1, :])
                dza = dz(a)
                advect[i, x] = we * dxa + wn * dya + wv * dza
            return carry

        [advection_slab(x, 0) for x in range(width_x)]
        settle(pressure_copies)

        def velocity_slab(x, carry, par=par, nxt=nxt, last=last):
            xp = x + 1
            old = pads.at[par]
            p_new = pbuf[par, xp]
            grad = (
                (pbuf[par, xp + 1] - pbuf[par, x]) * 0.5,
                dy(p_new, yprecv[par, 0, x:x + 1, :], yprecv[par, 1, x:x + 1, :]),
                dz(p_new),
            )
            new_state = [p_new]
            for i in range(3):
                new_state.append(old[1 + i, xp] + step_length * (grad[i] + advect[i, x]))
            for c in range(4):
                if last:
                    state_out[c, x] = new_state[c]
                else:
                    fill_state(nxt, x, c, new_state[c])
            return carry

        [velocity_slab(x, 0) for x in range(width_x)]

    forward_ready(0, steps == 1)
    [(functools.partial(
        increment_slab, get=lambda c, x: state_out[c, x], snap=0, first=steps == 1, last=True))(x, 0) for x in range(width_x)]

    for x in range(width_x):
        copy = pltpu.make_async_remote_copy(
            src_ref=ksend.at[x], dst_ref=krecv.at[x], send_sem=ks.at[x], recv_sem=kr.at[x],
            device_id=dev_pair, device_id_type=MESH,
        )
        copy.wait_recv()
        for c in range(4):
            kernel_out[c, x] = kernel_out[c, x] + krecv[x, c]
        copy.wait_send()


def samples_kernel(nx, ny, local_ref, out_ref, sent, got_x, got_y, send_sem, recv_sem):
    me_p = lax.axis_index("pair")
    gx = lax.axis_index("gx")
    gy = lax.axis_index("gy")
    peers_x = [(me_p, (gx + d) % nx, gy) for d in range(1, nx)]
    peers_y = [(me_p, gx, (gy + d) % ny) for d in range(1, ny)]
    barrier = pltpu.get_barrier_semaphore()
    for dev in peers_x + peers_y:
        pl.semaphore_signal(barrier, 1, device_id=dev, device_id_type=MESH)
    pl.semaphore_wait(barrier, len(peers_x) + len(peers_y))
    rounds = ((local_ref, got_x, peers_x, 0), (sent, got_y, peers_y, nx - 1))
    total = local_ref[...]
    for src, got, peers, base in rounds:
        copies = []
        for i, dev in enumerate(peers):
            copy = pltpu.make_async_remote_copy(
                src_ref=src, dst_ref=got.at[i], send_sem=send_sem.at[base + i],
                recv_sem=recv_sem.at[base + i], device_id=dev, device_id_type=MESH,
            )
            copy.start()
            copies.append(copy)
        for copy in copies:
            copy.wait_send()
            copy.wait_recv()
        for i in range(len(peers)):
            total = total + got[i]
        if base == 0:
            sent[...] = total
    out_ref[...] = total


def gathered_samples(local_samples):
    nx, ny = lax.axis_size("gx"), lax.axis_size("gy")
    if nx < 2 or ny < 2:
        return lax.psum(local_samples, ("gx", "gy"))
    vmem = pl.BlockSpec(memory_space=pltpu.VMEM)
    return pl.pallas_call(
        functools.partial(samples_kernel, nx, ny),
        out_shape=jax.ShapeDtypeStruct(local_samples.shape, jnp.float32),
        in_specs=[vmem],
        out_specs=vmem,
        scratch_shapes=[
            pltpu.VMEM(local_samples.shape, jnp.float32),
            pltpu.VMEM((nx - 1,) + local_samples.shape, jnp.float32),
            pltpu.VMEM((ny - 1,) + local_samples.shape, jnp.float32),
            pltpu.SemaphoreType.DMA((nx + ny - 2,)),
            pltpu.SemaphoreType.DMA((nx + ny - 2,)),
        ],
        compiler_params=pltpu.CompilerParams(collective_id=1, has_side_effects=True),
    )(local_samples)


def shards(
    sound_speed_sq,
    wind_profile,
    forward_field,
    adjoint_state,
    pair_counts,
    source_cells,
    receiver_cells,
    residuals,
):
    steps_total = forward_field.shape[0]
    width_x, width_y, depth = sound_speed_sq.shape
    slots = residuals.shape[0]
    live = (jnp.arange(slots, dtype=jnp.int32) < pair_counts[0]).astype(jnp.float32)
    gx_first = lax.axis_index("gx") * width_x
    gy_first = lax.axis_index("gy") * width_y
    x_range = jnp.arange(width_x, dtype=jnp.int32)
    y_range = jnp.arange(width_y, dtype=jnp.int32)
    z_range = jnp.arange(depth, dtype=jnp.int32)

    def tile_mask(cells):
        on_x = (cells[:, 0][None, :] - gx_first) == x_range[:, None]
        on_y = (cells[:, 1][None, :] - gy_first) == y_range[:, None]
        return (on_x[:, None, :] & on_y[None, :, :]).astype(jnp.float32)

    source_z = (source_cells[:, 2][None, :] == z_range[:, None]).astype(jnp.bfloat16)
    along_z = jnp.einsum(
        "txyz,zn->txyn", forward_field[:, 0], source_z, preferred_element_type=jnp.float32
    )
    local_samples = jnp.sum(along_z * tile_mask(source_cells)[None], axis=(1, 2))
    samples = gathered_samples(local_samples)
    amplitude = jnp.transpose(residuals) * samples * live[None, :]
    spread = amplitude[:, None, None, :] * tile_mask(receiver_cells)[None]
    receiver_z = (receiver_cells[:, 2][:, None] == z_range[None, :]).astype(jnp.float32)
    injected = jnp.einsum(
        "txyn,nz->txyz", spread, receiver_z, precision=lax.Precision.HIGHEST,
        preferred_element_type=jnp.float32,
    )
    vmem = pl.BlockSpec(memory_space=pltpu.VMEM)
    kernel = functools.partial(
        stencil_kernel, lax.axis_size("gx"), lax.axis_size("gy"), steps_total
    )
    state_new, kernels = pl.pallas_call(
        kernel,
        out_shape=(
            jax.ShapeDtypeStruct((4, width_x, width_y, depth), jnp.float32),
            jax.ShapeDtypeStruct((4, width_x, width_y, depth // 2), jnp.float32),
        ),
        in_specs=[vmem] * 5,
        out_specs=(vmem, vmem),
        scratch_shapes=[
            pltpu.VMEM((2, 4, width_x + 2, width_y, depth), jnp.float32),
            pltpu.VMEM((2, width_x + 2, width_y, depth), jnp.float32),
            pltpu.VMEM((2, 2, 4, width_x, depth), jnp.float32),
            pltpu.VMEM((2, 2, 4, width_x, depth), jnp.float32),
            pltpu.VMEM((2, width_x, depth), jnp.float32),
            pltpu.VMEM((2, 2, width_x, depth), jnp.float32),
            pltpu.VMEM((4, width_x, width_y, depth), jnp.float32),
            pltpu.VMEM((width_x, 4, width_y, depth // 2), jnp.float32),
            pltpu.VMEM((width_x, 4, width_y, depth // 2), jnp.float32),
            pltpu.VMEM((steps_total, 4, width_x + 2, width_y, depth), forward_field.dtype),
            pltpu.VMEM((2, steps_total, 2, 2 * width_x, depth), forward_field.dtype),
            pltpu.VMEM((2, steps_total, 2, 2 * width_x, depth), forward_field.dtype),
            pltpu.VMEM((3, width_x, width_y, depth), jnp.float32),
            pltpu.VMEM((2, width_x, width_y, depth), jnp.float32),
            pltpu.SemaphoreType.DMA((2, 2, 4)),
            pltpu.SemaphoreType.DMA((2, 2, 4)),
            pltpu.SemaphoreType.DMA((4,)),
            pltpu.SemaphoreType.DMA((4,)),
            pltpu.SemaphoreType.DMA((width_x,)),
            pltpu.SemaphoreType.DMA((width_x,)),
            pltpu.SemaphoreType.DMA((steps_total, 4)),
            pltpu.SemaphoreType.DMA((steps_total, 4)),
            pltpu.SemaphoreType.DMA((1,)),
        ],
        compiler_params=pltpu.CompilerParams(
            collective_id=0, has_side_effects=True, vmem_limit_bytes=48 * 1024 * 1024
        ),
    )(adjoint_state[0], sound_speed_sq, wind_profile, forward_field, injected)
    return (kernels, state_new[None])


def solution(mesh):
    in_specs = (
        P("gx", "gy", None),
        P(),
        P(None, None, "gx", "gy", None),
        P("pair", None, "gx", "gy", None),
        P("pair"),
        P("pair", None),
        P("pair", None),
        P("pair", None),
    )
    out_specs = (P(None, "gx", "gy", "pair"), P("pair", None, "gx", "gy", None))
    return jax.shard_map(shards, mesh=mesh, in_specs=in_specs, out_specs=out_specs, check_vma=False)
```

```python
import functools

import jax
import jax.numpy as jnp
from jax import lax
from jax.experimental import pallas as pl
from jax.experimental.pallas import tpu as pltpu
from jax.sharding import PartitionSpec as P

step_length = 0.25
Y_SLOT = (0, 2, 1, 3)
MESH = pl.DeviceIdType.MESH


def neighbours(shard, axis, dim):
    size, length = (lax.axis_size(axis), shard.shape[dim])
    up = [(i, i + 1) for i in range(size - 1)]
    down = [(i + 1, i) for i in range(size - 1)]
    last = lax.slice_in_dim(shard, length - 1, length, axis=dim)
    first = lax.slice_in_dim(shard, 0, 1, axis=dim)
    before = lax.ppermute(last, axis, up)
    after = lax.ppermute(first, axis, down)
    return (before, after)


def local_cells(cells, width_x, width_y):
    local_x = cells[:, 0] - lax.axis_index("gx") * width_x
    local_y = cells[:, 1] - lax.axis_index("gy") * width_y
    inside = (local_x >= 0) & (local_x < width_x) & (local_y >= 0) & (local_y < width_y)
    return (
        jnp.clip(local_x, 0, width_x - 1),
        jnp.clip(local_y, 0, width_y - 1),
        cells[:, 2],
        inside.astype(jnp.float32),
    )


def stencil_kernel(
    nx, ny, steps,
    state_in, sound, wind, forward, inj,
    state_out, kernel_out,
    pads, pbuf, ysend, yrecv, ypsend, yprecv, acc_out, ksend, krecv, fpad, fysend, fyr, advect, early,
    ss, rs, ps, pr, ks, kr, fs, fr, local_sem,
):
    _, width_x, width_y, depth = state_in.shape
    me_p = lax.axis_index("pair")
    gx = lax.axis_index("gx")
    gy = lax.axis_index("gy")
    has_lo_x = gx > 0
    has_hi_x = gx < nx - 1
    has_lo_y = gy > 0
    has_hi_y = gy < ny - 1
    dev_lo_x = (me_p, gx - 1, gy)
    dev_hi_x = (me_p, gx + 1, gy)
    dev_lo_y = (me_p, gx, gy - 1)
    dev_hi_y = (me_p, gx, gy + 1)
    dev_pair = (1 - me_p, gx, gy)
    half = depth // 2

    zero_slab = jnp.zeros((width_y, depth), jnp.float32)
    for par in range(2):
        for c in range(4):
            pads[par, c, 0] = zero_slab
            pads[par, c, width_x + 1] = zero_slab
            for side in range(2):
                yrecv[par, side, c] = jnp.zeros((width_x, depth), jnp.float32)
    for par in range(2):
        pbuf[par, 0] = zero_slab
        pbuf[par, width_x + 1] = zero_slab
    zero_forward = jnp.zeros((width_y, depth), fpad.dtype)
    for t in range(steps):
        for c in range(4):
            fpad[t, c, 0] = zero_forward
            fpad[t, c, width_x + 1] = zero_forward
            for side in range(2):
                fyr[side, t, c // 2, pl.ds((c % 2) * width_x, width_x), :] = jnp.zeros((width_x, depth), fyr.dtype)

    def forward_rows(x, carry):
        for t in range(steps):
            for c in range(4):
                f = forward[t, c, x]
                row = (c % 2) * width_x + x
                fysend[0, t, c // 2, row:row + 1, :] = f[width_y - 1:width_y, :]
                fysend[1, t, c // 2, row:row + 1, :] = f[0:1, :]
        return carry

    [forward_rows(x, 0) for x in range(width_x)]
    interior = pltpu.make_async_copy(forward, fpad.at[:, :, pl.ds(1, width_x)], local_sem.at[0])
    interior.start()
    for par in range(2):
        for side in range(2):
            yprecv[par, side] = jnp.zeros((width_x, depth), jnp.float32)

    barrier = pltpu.get_barrier_semaphore()
    pl.semaphore_signal(barrier, 1, device_id=dev_pair, device_id_type=MESH)
    for cond, dev in ((has_lo_x, dev_lo_x), (has_hi_x, dev_hi_x), (has_lo_y, dev_lo_y), (has_hi_y, dev_hi_y)):
        @pl.when(cond)
        def _():
            pl.semaphore_signal(barrier, 1, device_id=dev, device_id_type=MESH)
    peers = 1 + (
        (gx + nx - 1) // nx + (2 * nx - 2 - gx) // nx
        + (gy + ny - 1) // ny + (2 * ny - 2 - gy) // ny
    )
    pl.semaphore_wait(barrier, peers)

    iy = lax.broadcasted_iota(jnp.int32, (width_y, depth), 0)
    iz = lax.broadcasted_iota(jnp.int32, (width_y, depth), 1)
    we = wind[0:1, :]
    wn = wind[1:2, :]
    wv = wind[2:3, :]

    def dy(v, lo, hi):
        up = jnp.where(iy == width_y - 1, hi, pltpu.roll(v, width_y - 1, 0))
        down = jnp.where(iy == 0, lo, pltpu.roll(v, 1, 0))
        return (up - down) * 0.5

    def dz(v):
        up = jnp.where(iz == depth - 1, 0.0, pltpu.roll(v, depth - 1, 1))
        down = jnp.where(iz == 0, 0.0, pltpu.roll(v, 1, 1))
        return (up - down) * 0.5

    def exchange(src_lo_x, src_hi_x, dst_lo_x, dst_hi_x, src_y_hi, src_y_lo, dst_y_lo, dst_y_hi, send, recv):
        outs = (
            (has_hi_x, src_hi_x, dst_lo_x, 0, dev_hi_x),
            (has_lo_x, src_lo_x, dst_hi_x, 1, dev_lo_x),
            (has_hi_y, src_y_hi, dst_y_lo, 2, dev_hi_y),
            (has_lo_y, src_y_lo, dst_y_hi, 3, dev_lo_y),
        )
        copies = []
        for cond, src, dst, slot, dev in outs:
            copy = pltpu.make_async_remote_copy(
                src_ref=src, dst_ref=dst, send_sem=send.at[slot], recv_sem=recv.at[slot],
                device_id=dev, device_id_type=MESH,
            )
            copies.append((cond, copy))

            @pl.when(cond)
            def _():
                copy.start()
        return copies

    def settle(copies):
        incoming = (has_lo_x, has_hi_x, has_lo_y, has_hi_y)
        for (cond, copy), arrives in zip(copies, incoming):
            @pl.when(cond)
            def _():
                copy.wait_send()

            @pl.when(arrives)
            def _():
                copy.wait_recv()

    def fill_state(par, x, c, v):
        pads[par, c, x + 1] = v
        ysend[par, 0, Y_SLOT[c], x:x + 1, :] = v[width_y - 1:width_y, :]
        ysend[par, 1, Y_SLOT[c], x:x + 1, :] = v[0:1, :]

    def copy_in(x, carry):
        for c in range(4):
            fill_state(0, x, c, state_in[c, x])
        return carry

    [copy_in(x, 0) for x in range(width_x)]
    forward_copies = {}

    def send_forward(t):
        forward_copies[t] = exchange(
            forward.at[t, :, pl.ds(0, 1)], forward.at[t, :, pl.ds(width_x - 1, 1)],
            fpad.at[t, :, pl.ds(0, 1)], fpad.at[t, :, pl.ds(width_x + 1, 1)],
            fysend.at[0, t], fysend.at[1, t], fyr.at[0, t], fyr.at[1, t], fs.at[t], fr.at[t],
        )

    def increment_slab(x, carry, get, snap, first, last):
        xp = x + 1
        p_new = get(0, x)
        a_new = [get(1 + i, x) for i in range(3)]
        fe, fn, fu = [], [], []
        for c in range(4):
            f = fpad[snap, c, xp].astype(jnp.float32)
            fe.append((fpad[snap, c, xp + 1].astype(jnp.float32) - fpad[snap, c, x].astype(jnp.float32)) * 0.5)
            row = (c % 2) * width_x + x
            fn.append(dy(f, fyr[0, snap, c // 2, row:row + 1, :].astype(jnp.float32),
                         fyr[1, snap, c // 2, row:row + 1, :].astype(jnp.float32)))
            fu.append(dz(f))
        pieces = [p_new * (fe[1] + fn[2] + fu[3])]
        for along in (fe, fn, fu):
            pieces.append(p_new * along[0] + a_new[0] * along[1] + a_new[1] * along[2] + a_new[2] * along[3])
        for c in range(4):
            total = pieces[c] if first else acc_out[c, x] + pieces[c]
            if not last:
                acc_out[c, x] = total
                continue
            low, high = total[:, :half], total[:, half:]
            kernel_out[c, x] = jnp.where(me_p == 0, low, high)
            ksend[x, c] = jnp.where(me_p == 0, high, low)
        if last:
            pltpu.make_async_remote_copy(
                src_ref=ksend.at[x], dst_ref=krecv.at[x], send_sem=ks.at[x], recv_sem=kr.at[x],
                device_id=dev_pair, device_id_type=MESH,
            ).start()
        return carry

    def forward_ready(t, first):
        if first:
            interior.wait()
        settle(forward_copies[t])

    for step in range(steps):
        par = step % 2
        nxt = 1 - par
        snap = steps - 1 - step
        last = step == steps - 1
        halves = []
        for part in range(2):
            comps = pl.ds(2 * part, 2) if (part or step == 0) else pl.ds(1, 1)
            halves.append(exchange(
                pads.at[par, comps, pl.ds(1, 1)], pads.at[par, comps, pl.ds(width_x, 1)],
                pads.at[par, comps, pl.ds(0, 1)], pads.at[par, comps, pl.ds(width_x + 1, 1)],
                ysend.at[par, 0, comps], ysend.at[par, 1, comps],
                yrecv.at[par, 0, comps], yrecv.at[par, 1, comps],
                ss.at[par, part], rs.at[par, part],
            ))
        state_copies, velocity_copies = halves
        if step > 0:
            forward_ready(snap + 1, step == 1)
            [(functools.partial(
                increment_slab, get=lambda c, x, par=par: pads[par, c, x + 1],
                snap=snap + 1, first=step == 1, last=False))(x, 0) for x in range(width_x)]
        if step > 0:
            def early_slab(x, carry, par=par):
                xp = x + 1
                held = pbuf.at[1 - par]
                p = held[xp]
                dxp = (held[xp + 1] - held[x]) * 0.5
                dyp = dy(p, yprecv[1 - par, 0, x:x + 1, :], yprecv[1 - par, 1, x:x + 1, :])
                early[0, x] = we * dxp + wn * dyp + wv * dz(p)
                early[1, x] = dz(pads[par, 3, xp])
                return carry

            [early_slab(x, 0) for x in range(width_x)]
        settle(state_copies)

        def pressure_slab(x, carry, par=par, snap=snap, step=step):
            xp = x + 1
            old = pads.at[par]
            dxa = (old[1, xp + 1] - old[1, x]) * 0.5
            dya = dy(old[2, xp], yrecv[par, 0, Y_SLOT[2], x:x + 1, :], yrecv[par, 1, Y_SLOT[2], x:x + 1, :])
            if step == 0:
                p = old[0, xp]
                dxp = (old[0, xp + 1] - old[0, x]) * 0.5
                dyp = dy(p, yrecv[par, 0, Y_SLOT[0], x:x + 1, :], yrecv[par, 1, Y_SLOT[0], x:x + 1, :])
                rest = we * dxp + wn * dyp + wv * dz(p)
                dza = dz(old[3, xp])
            else:
                p = pbuf[1 - par, xp]
                rest = early[0, x]
                dza = early[1, x]
            divergence = dxa + dya + dza
            p_new = p + step_length * (sound[x] * divergence + rest) + inj[snap, x]
            pbuf[par, xp] = p_new
            ypsend[0, x:x + 1, :] = p_new[width_y - 1:width_y, :]
            ypsend[1, x:x + 1, :] = p_new[0:1, :]
            return carry

        [pressure_slab(x, 0) for x in range(width_x)]
        pressure_copies = exchange(
            pbuf.at[par, pl.ds(1, 1)], pbuf.at[par, pl.ds(width_x, 1)],
            pbuf.at[par, pl.ds(0, 1)], pbuf.at[par, pl.ds(width_x + 1, 1)],
            ypsend.at[0], ypsend.at[1], yprecv.at[par, 0], yprecv.at[par, 1],
            ps, pr,
        )
        if step < steps - 1:
            send_forward(snap)
        if step == steps - 2:
            send_forward(snap - 1)
        settle(velocity_copies)

        def advection_slab(x, carry, par=par):
            xp = x + 1
            old = pads.at[par]
            for i in range(3):
                a = old[1 + i, xp]
                dxa = (old[1 + i, xp + 1] - old[1 + i, x]) * 0.5
                dya = dy(a, yrecv[par, 0, Y_SLOT[1 + i], x:x + 1, :], yrecv[par, 1, Y_SLOT[1 + i], x:x + 1, :])
                dza = dz(a)
                advect[i, x] = we * dxa + wn * dya + wv * dza
            return carry

        [advection_slab(x, 0) for x in range(width_x)]
        settle(pressure_copies)

        def velocity_slab(x, carry, par=par, nxt=nxt, last=last):
            xp = x + 1
            old = pads.at[par]
            p_new = pbuf[par, xp]
            grad = (
                (pbuf[par, xp + 1] - pbuf[par, x]) * 0.5,
                dy(p_new, yprecv[par, 0, x:x + 1, :], yprecv[par, 1, x:x + 1, :]),
                dz(p_new),
            )
            new_state = [p_new]
            for i in range(3):
                new_state.append(old[1 + i, xp] + step_length * (grad[i] + advect[i, x]))
            for c in range(4):
                if last:
                    state_out[c, x] = new_state[c]
                else:
                    fill_state(nxt, x, c, new_state[c])
            return carry

        [velocity_slab(x, 0) for x in range(width_x)]

    forward_ready(0, steps == 1)
    [(functools.partial(
        increment_slab, get=lambda c, x: state_out[c, x], snap=0, first=steps == 1, last=True))(x, 0) for x in range(width_x)]

    for x in range(width_x):
        copy = pltpu.make_async_remote_copy(
            src_ref=ksend.at[x], dst_ref=krecv.at[x], send_sem=ks.at[x], recv_sem=kr.at[x],
            device_id=dev_pair, device_id_type=MESH,
        )
        copy.wait_recv()
        for c in range(4):
            kernel_out[c, x] = kernel_out[c, x] + krecv[x, c]
        copy.wait_send()


def samples_kernel(nx, ny, local_ref, out_ref, sent, got_x, got_y, send_sem, recv_sem):
    me_p = lax.axis_index("pair")
    gx = lax.axis_index("gx")
    gy = lax.axis_index("gy")
    peers_x = [(me_p, (gx + d) % nx, gy) for d in range(1, nx)]
    peers_y = [(me_p, gx, (gy + d) % ny) for d in range(1, ny)]
    barrier = pltpu.get_barrier_semaphore()
    for dev in peers_x + peers_y:
        pl.semaphore_signal(barrier, 1, device_id=dev, device_id_type=MESH)
    pl.semaphore_wait(barrier, len(peers_x) + len(peers_y))
    rounds = ((local_ref, got_x, peers_x, 0), (sent, got_y, peers_y, nx - 1))
    total = local_ref[...]
    for src, got, peers, base in rounds:
        copies = []
        for i, dev in enumerate(peers):
            copy = pltpu.make_async_remote_copy(
                src_ref=src, dst_ref=got.at[i], send_sem=send_sem.at[base + i],
                recv_sem=recv_sem.at[base + i], device_id=dev, device_id_type=MESH,
            )
            copy.start()
            copies.append(copy)
        for copy in copies:
            copy.wait_send()
            copy.wait_recv()
        for i in range(len(peers)):
            total = total + got[i]
        if base == 0:
            sent[...] = total
    out_ref[...] = total


def gathered_samples(local_samples):
    nx, ny = lax.axis_size("gx"), lax.axis_size("gy")
    if nx < 2 or ny < 2:
        return lax.psum(local_samples, ("gx", "gy"))
    vmem = pl.BlockSpec(memory_space=pltpu.VMEM)
    return pl.pallas_call(
        functools.partial(samples_kernel, nx, ny),
        out_shape=jax.ShapeDtypeStruct(local_samples.shape, jnp.float32),
        in_specs=[vmem],
        out_specs=vmem,
        scratch_shapes=[
            pltpu.VMEM(local_samples.shape, jnp.float32),
            pltpu.VMEM((nx - 1,) + local_samples.shape, jnp.float32),
            pltpu.VMEM((ny - 1,) + local_samples.shape, jnp.float32),
            pltpu.SemaphoreType.DMA((nx + ny - 2,)),
            pltpu.SemaphoreType.DMA((nx + ny - 2,)),
        ],
        compiler_params=pltpu.CompilerParams(collective_id=1, has_side_effects=True),
    )(local_samples)


def shards(
    sound_speed_sq,
    wind_profile,
    forward_field,
    adjoint_state,
    pair_counts,
    source_cells,
    receiver_cells,
    residuals,
):
    steps_total = forward_field.shape[0]
    width_x, width_y, depth = sound_speed_sq.shape
    slots = residuals.shape[0]
    live = (jnp.arange(slots, dtype=jnp.int32) < pair_counts[0]).astype(jnp.float32)
    gx_first = lax.axis_index("gx") * width_x
    gy_first = lax.axis_index("gy") * width_y
    x_range = jnp.arange(width_x, dtype=jnp.int32)
    y_range = jnp.arange(width_y, dtype=jnp.int32)
    z_range = jnp.arange(depth, dtype=jnp.int32)

    def tile_mask(cells):
        on_x = (cells[:, 0][None, :] - gx_first) == x_range[:, None]
        on_y = (cells[:, 1][None, :] - gy_first) == y_range[:, None]
        return (on_x[:, None, :] & on_y[None, :, :]).astype(jnp.float32)

    source_z = (source_cells[:, 2][None, :] == z_range[:, None]).astype(jnp.bfloat16)
    along_z = jnp.einsum(
        "txyz,zn->txyn", forward_field[:, 0], source_z, preferred_element_type=jnp.float32
    )
    local_samples = jnp.sum(along_z * tile_mask(source_cells)[None], axis=(1, 2))
    samples = gathered_samples(local_samples)
    amplitude = jnp.transpose(residuals) * samples * live[None, :]
    spread = amplitude[:, None, None, :] * tile_mask(receiver_cells)[None]
    receiver_z = (receiver_cells[:, 2][:, None] == z_range[None, :]).astype(jnp.float32)
    injected = jnp.einsum(
        "txyn,nz->txyz", spread, receiver_z, precision=lax.Precision.HIGHEST,
        preferred_element_type=jnp.float32,
    )
    vmem = pl.BlockSpec(memory_space=pltpu.VMEM)
    kernel = functools.partial(
        stencil_kernel, lax.axis_size("gx"), lax.axis_size("gy"), steps_total
    )
    state_new, kernels = pl.pallas_call(
        kernel,
        out_shape=(
            jax.ShapeDtypeStruct((4, width_x, width_y, depth), jnp.float32),
            jax.ShapeDtypeStruct((4, width_x, width_y, depth // 2), jnp.float32),
        ),
        in_specs=[vmem] * 5,
        out_specs=(vmem, vmem),
        scratch_shapes=[
            pltpu.VMEM((2, 4, width_x + 2, width_y, depth), jnp.float32),
            pltpu.VMEM((2, width_x + 2, width_y, depth), jnp.float32),
            pltpu.VMEM((2, 2, 4, width_x, depth), jnp.float32),
            pltpu.VMEM((2, 2, 4, width_x, depth), jnp.float32),
            pltpu.VMEM((2, width_x, depth), jnp.float32),
            pltpu.VMEM((2, 2, width_x, depth), jnp.float32),
            pltpu.VMEM((4, width_x, width_y, depth), jnp.float32),
            pltpu.VMEM((width_x, 4, width_y, depth // 2), jnp.float32),
            pltpu.VMEM((width_x, 4, width_y, depth // 2), jnp.float32),
            pltpu.VMEM((steps_total, 4, width_x + 2, width_y, depth), forward_field.dtype),
            pltpu.VMEM((2, steps_total, 2, 2 * width_x, depth), forward_field.dtype),
            pltpu.VMEM((2, steps_total, 2, 2 * width_x, depth), forward_field.dtype),
            pltpu.VMEM((3, width_x, width_y, depth), jnp.float32),
            pltpu.VMEM((2, width_x, width_y, depth), jnp.float32),
            pltpu.SemaphoreType.DMA((2, 2, 4)),
            pltpu.SemaphoreType.DMA((2, 2, 4)),
            pltpu.SemaphoreType.DMA((4,)),
            pltpu.SemaphoreType.DMA((4,)),
            pltpu.SemaphoreType.DMA((width_x,)),
            pltpu.SemaphoreType.DMA((width_x,)),
            pltpu.SemaphoreType.DMA((steps_total, 4)),
            pltpu.SemaphoreType.DMA((steps_total, 4)),
            pltpu.SemaphoreType.DMA((1,)),
        ],
        compiler_params=pltpu.CompilerParams(
            collective_id=0, has_side_effects=True, vmem_limit_bytes=48 * 1024 * 1024
        ),
    )(adjoint_state[0], sound_speed_sq, wind_profile, forward_field, injected)
    return (kernels, state_new[None])


def solution(mesh):
    in_specs = (
        P("gx", "gy", None),
        P(),
        P(None, None, "gx", "gy", None),
        P("pair", None, "gx", "gy", None),
        P("pair"),
        P("pair", None),
        P("pair", None),
        P("pair", None),
    )
    out_specs = (P(None, "gx", "gy", "pair"), P("pair", None, "gx", "gy", None))
    return jax.shard_map(shards, mesh=mesh, in_specs=in_specs, out_specs=out_specs, check_vma=False)
```

```python
import functools

import jax
import jax.numpy as jnp
from jax import lax
from jax.experimental import pallas as pl
from jax.experimental.pallas import tpu as pltpu
from jax.sharding import PartitionSpec as P

step_length = 0.25
Y_SLOT = (0, 2, 1, 3)
MESH = pl.DeviceIdType.MESH


def neighbours(shard, axis, dim):
    size, length = (lax.axis_size(axis), shard.shape[dim])
    up = [(i, i + 1) for i in range(size - 1)]
    down = [(i + 1, i) for i in range(size - 1)]
    last = lax.slice_in_dim(shard, length - 1, length, axis=dim)
    first = lax.slice_in_dim(shard, 0, 1, axis=dim)
    before = lax.ppermute(last, axis, up)
    after = lax.ppermute(first, axis, down)
    return (before, after)


def local_cells(cells, width_x, width_y):
    local_x = cells[:, 0] - lax.axis_index("gx") * width_x
    local_y = cells[:, 1] - lax.axis_index("gy") * width_y
    inside = (local_x >= 0) & (local_x < width_x) & (local_y >= 0) & (local_y < width_y)
    return (
        jnp.clip(local_x, 0, width_x - 1),
        jnp.clip(local_y, 0, width_y - 1),
        cells[:, 2],
        inside.astype(jnp.float32),
    )


def stencil_kernel(
    nx, ny, steps,
    state_in, sound, wind, forward, inj,
    state_out, kernel_out,
    pads, pbuf, ysend, yrecv, ypsend, yprecv, acc_out, ksend, krecv, fpad, fysend, fyr, advect, early,
    ss, rs, ps, pr, ks, kr, fs, fr, local_sem,
):
    _, width_x, width_y, depth = state_in.shape
    me_p = lax.axis_index("pair")
    gx = lax.axis_index("gx")
    gy = lax.axis_index("gy")
    has_lo_x = gx > 0
    has_hi_x = gx < nx - 1
    has_lo_y = gy > 0
    has_hi_y = gy < ny - 1
    dev_lo_x = (me_p, gx - 1, gy)
    dev_hi_x = (me_p, gx + 1, gy)
    dev_lo_y = (me_p, gx, gy - 1)
    dev_hi_y = (me_p, gx, gy + 1)
    dev_pair = (1 - me_p, gx, gy)
    half = depth // 2

    zero_slab = jnp.zeros((width_y, depth), jnp.float32)
    for par in range(2):
        for c in range(4):
            pads[par, c, 0] = zero_slab
            pads[par, c, width_x + 1] = zero_slab
            for side in range(2):
                yrecv[par, side, c] = jnp.zeros((width_x, depth), jnp.float32)
    for par in range(2):
        pbuf[par, 0] = zero_slab
        pbuf[par, width_x + 1] = zero_slab
    zero_forward = jnp.zeros((width_y, depth), fpad.dtype)
    for t in range(steps):
        for c in range(4):
            fpad[t, c, 0] = zero_forward
            fpad[t, c, width_x + 1] = zero_forward
            for side in range(2):
                fyr[side, t, c // 2, pl.ds((c % 2) * width_x, width_x), :] = jnp.zeros((width_x, depth), fyr.dtype)

    def forward_rows(x, carry):
        for t in range(steps):
            for c in range(4):
                f = forward[t, c, x]
                row = (c % 2) * width_x + x
                fysend[0, t, c // 2, row:row + 1, :] = f[width_y - 1:width_y, :]
                fysend[1, t, c // 2, row:row + 1, :] = f[0:1, :]
        return carry

    [forward_rows(x, 0) for x in range(width_x)]
    interior = pltpu.make_async_copy(forward, fpad.at[:, :, pl.ds(1, width_x)], local_sem.at[0])
    interior.start()
    for par in range(2):
        for side in range(2):
            yprecv[par, side] = jnp.zeros((width_x, depth), jnp.float32)

    barrier = pltpu.get_barrier_semaphore()
    pl.semaphore_signal(barrier, 1, device_id=dev_pair, device_id_type=MESH)
    for cond, dev in ((has_lo_x, dev_lo_x), (has_hi_x, dev_hi_x), (has_lo_y, dev_lo_y), (has_hi_y, dev_hi_y)):
        @pl.when(cond)
        def _():
            pl.semaphore_signal(barrier, 1, device_id=dev, device_id_type=MESH)
    peers = 1 + (
        (gx + nx - 1) // nx + (2 * nx - 2 - gx) // nx
        + (gy + ny - 1) // ny + (2 * ny - 2 - gy) // ny
    )
    pl.semaphore_wait(barrier, peers)

    iy = lax.broadcasted_iota(jnp.int32, (width_y, depth), 0)
    iz = lax.broadcasted_iota(jnp.int32, (width_y, depth), 1)
    we = wind[0:1, :]
    wn = wind[1:2, :]
    wv = wind[2:3, :]

    def dy(v, lo, hi):
        up = jnp.where(iy == width_y - 1, hi, pltpu.roll(v, width_y - 1, 0))
        down = jnp.where(iy == 0, lo, pltpu.roll(v, 1, 0))
        return (up - down) * 0.5

    def dz(v):
        up = jnp.where(iz == depth - 1, 0.0, pltpu.roll(v, depth - 1, 1))
        down = jnp.where(iz == 0, 0.0, pltpu.roll(v, 1, 1))
        return (up - down) * 0.5

    def exchange(src_lo_x, src_hi_x, dst_lo_x, dst_hi_x, src_y_hi, src_y_lo, dst_y_lo, dst_y_hi, send, recv):
        outs = (
            (has_hi_x, src_hi_x, dst_lo_x, 0, dev_hi_x),
            (has_lo_x, src_lo_x, dst_hi_x, 1, dev_lo_x),
            (has_hi_y, src_y_hi, dst_y_lo, 2, dev_hi_y),
            (has_lo_y, src_y_lo, dst_y_hi, 3, dev_lo_y),
        )
        copies = []
        for cond, src, dst, slot, dev in outs:
            copy = pltpu.make_async_remote_copy(
                src_ref=src, dst_ref=dst, send_sem=send.at[slot], recv_sem=recv.at[slot],
                device_id=dev, device_id_type=MESH,
            )
            copies.append((cond, copy))

            @pl.when(cond)
            def _():
                copy.start()
        return copies

    def settle(copies):
        incoming = (has_lo_x, has_hi_x, has_lo_y, has_hi_y)
        for (cond, copy), arrives in zip(copies, incoming):
            @pl.when(cond)
            def _():
                copy.wait_send()

            @pl.when(arrives)
            def _():
                copy.wait_recv()

    def fill_state(par, x, c, v):
        pads[par, c, x + 1] = v
        ysend[par, 0, Y_SLOT[c], x:x + 1, :] = v[width_y - 1:width_y, :]
        ysend[par, 1, Y_SLOT[c], x:x + 1, :] = v[0:1, :]

    def copy_in(x, carry):
        for c in range(4):
            fill_state(0, x, c, state_in[c, x])
        return carry

    [copy_in(x, 0) for x in range(width_x)]
    forward_copies = {}

    def send_forward(t):
        forward_copies[t] = exchange(
            forward.at[t, :, pl.ds(0, 1)], forward.at[t, :, pl.ds(width_x - 1, 1)],
            fpad.at[t, :, pl.ds(0, 1)], fpad.at[t, :, pl.ds(width_x + 1, 1)],
            fysend.at[0, t], fysend.at[1, t], fyr.at[0, t], fyr.at[1, t], fs.at[t], fr.at[t],
        )

    def increment_slab(x, carry, get, snap, first, last):
        xp = x + 1
        p_new = get(0, x)
        a_new = [get(1 + i, x) for i in range(3)]
        fe, fn, fu = [], [], []
        for c in range(4):
            f = fpad[snap, c, xp].astype(jnp.float32)
            fe.append((fpad[snap, c, xp + 1].astype(jnp.float32) - fpad[snap, c, x].astype(jnp.float32)) * 0.5)
            row = (c % 2) * width_x + x
            fn.append(dy(f, fyr[0, snap, c // 2, row:row + 1, :].astype(jnp.float32),
                         fyr[1, snap, c // 2, row:row + 1, :].astype(jnp.float32)))
            fu.append(dz(f))
        pieces = [p_new * (fe[1] + fn[2] + fu[3])]
        for along in (fe, fn, fu):
            pieces.append(p_new * along[0] + a_new[0] * along[1] + a_new[1] * along[2] + a_new[2] * along[3])
        for c in range(4):
            total = pieces[c] if first else acc_out[c, x] + pieces[c]
            if not last:
                acc_out[c, x] = total
                continue
            low, high = total[:, :half], total[:, half:]
            kernel_out[c, x] = jnp.where(me_p == 0, low, high)
            ksend[x, c] = jnp.where(me_p == 0, high, low)
        if last:
            pltpu.make_async_remote_copy(
                src_ref=ksend.at[x], dst_ref=krecv.at[x], send_sem=ks.at[x], recv_sem=kr.at[x],
                device_id=dev_pair, device_id_type=MESH,
            ).start()
        return carry

    def forward_ready(t, first):
        if first:
            interior.wait()
        settle(forward_copies[t])

    for step in range(steps):
        par = step % 2
        nxt = 1 - par
        snap = steps - 1 - step
        last = step == steps - 1
        halves = []
        for part in range(2):
            comps = pl.ds(2 * part, 2) if (part or step == 0) else pl.ds(1, 1)
            halves.append(exchange(
                pads.at[par, comps, pl.ds(1, 1)], pads.at[par, comps, pl.ds(width_x, 1)],
                pads.at[par, comps, pl.ds(0, 1)], pads.at[par, comps, pl.ds(width_x + 1, 1)],
                ysend.at[par, 0, comps], ysend.at[par, 1, comps],
                yrecv.at[par, 0, comps], yrecv.at[par, 1, comps],
                ss.at[par, part], rs.at[par, part],
            ))
        state_copies, velocity_copies = halves
        if step > 0:
            forward_ready(snap + 1, step == 1)
            [(functools.partial(
                increment_slab, get=lambda c, x, par=par: pads[par, c, x + 1],
                snap=snap + 1, first=step == 1, last=False))(x, 0) for x in range(width_x)]
        if step > 0:
            def early_slab(x, carry, par=par):
                xp = x + 1
                held = pbuf.at[1 - par]
                p = held[xp]
                dxp = (held[xp + 1] - held[x]) * 0.5
                dyp = dy(p, yprecv[1 - par, 0, x:x + 1, :], yprecv[1 - par, 1, x:x + 1, :])
                early[0, x] = we * dxp + wn * dyp + wv * dz(p)
                early[1, x] = dz(pads[par, 3, xp])
                return carry

            [early_slab(x, 0) for x in range(width_x)]
        settle(state_copies)

        def pressure_slab(x, carry, par=par, snap=snap, step=step):
            xp = x + 1
            old = pads.at[par]
            dxa = (old[1, xp + 1] - old[1, x]) * 0.5
            dya = dy(old[2, xp], yrecv[par, 0, Y_SLOT[2], x:x + 1, :], yrecv[par, 1, Y_SLOT[2], x:x + 1, :])
            if step == 0:
                p = old[0, xp]
                dxp = (old[0, xp + 1] - old[0, x]) * 0.5
                dyp = dy(p, yrecv[par, 0, Y_SLOT[0], x:x + 1, :], yrecv[par, 1, Y_SLOT[0], x:x + 1, :])
                rest = we * dxp + wn * dyp + wv * dz(p)
                dza = dz(old[3, xp])
            else:
                p = pbuf[1 - par, xp]
                rest = early[0, x]
                dza = early[1, x]
            divergence = dxa + dya + dza
            p_new = p + step_length * (sound[x] * divergence + rest) + inj[snap, x]
            pbuf[par, xp] = p_new
            ypsend[0, x:x + 1, :] = p_new[width_y - 1:width_y, :]
            ypsend[1, x:x + 1, :] = p_new[0:1, :]
            return carry

        [pressure_slab(x, 0) for x in range(width_x)]
        pressure_copies = exchange(
            pbuf.at[par, pl.ds(1, 1)], pbuf.at[par, pl.ds(width_x, 1)],
            pbuf.at[par, pl.ds(0, 1)], pbuf.at[par, pl.ds(width_x + 1, 1)],
            ypsend.at[0], ypsend.at[1], yprecv.at[par, 0], yprecv.at[par, 1],
            ps, pr,
        )
        if not last:
            send_forward(snap)
        settle(velocity_copies)

        def advection_slab(x, carry, par=par):
            xp = x + 1
            old = pads.at[par]
            for i in range(3):
                a = old[1 + i, xp]
                dxa = (old[1 + i, xp + 1] - old[1 + i, x]) * 0.5
                dya = dy(a, yrecv[par, 0, Y_SLOT[1 + i], x:x + 1, :], yrecv[par, 1, Y_SLOT[1 + i], x:x + 1, :])
                dza = dz(a)
                advect[i, x] = we * dxa + wn * dya + wv * dza
            return carry

        [advection_slab(x, 0) for x in range(width_x)]
        settle(pressure_copies)
        if last:
            send_forward(snap)

        def velocity_slab(x, carry, par=par, nxt=nxt, last=last):
            xp = x + 1
            old = pads.at[par]
            p_new = pbuf[par, xp]
            grad = (
                (pbuf[par, xp + 1] - pbuf[par, x]) * 0.5,
                dy(p_new, yprecv[par, 0, x:x + 1, :], yprecv[par, 1, x:x + 1, :]),
                dz(p_new),
            )
            new_state = [p_new]
            for i in range(3):
                new_state.append(old[1 + i, xp] + step_length * (grad[i] + advect[i, x]))
            for c in range(4):
                if last:
                    state_out[c, x] = new_state[c]
                else:
                    fill_state(nxt, x, c, new_state[c])
            return carry

        [velocity_slab(x, 0) for x in range(width_x)]

    forward_ready(0, steps == 1)
    [(functools.partial(
        increment_slab, get=lambda c, x: state_out[c, x], snap=0, first=steps == 1, last=True))(x, 0) for x in range(width_x)]

    for x in range(width_x):
        copy = pltpu.make_async_remote_copy(
            src_ref=ksend.at[x], dst_ref=krecv.at[x], send_sem=ks.at[x], recv_sem=kr.at[x],
            device_id=dev_pair, device_id_type=MESH,
        )
        copy.wait_recv()
        for c in range(4):
            kernel_out[c, x] = kernel_out[c, x] + krecv[x, c]
        copy.wait_send()


def samples_kernel(nx, ny, local_ref, out_ref, sent, got_x, got_y, send_sem, recv_sem):
    me_p = lax.axis_index("pair")
    gx = lax.axis_index("gx")
    gy = lax.axis_index("gy")
    peers_x = [(me_p, (gx + d) % nx, gy) for d in range(1, nx)]
    peers_y = [(me_p, gx, (gy + d) % ny) for d in range(1, ny)]
    barrier = pltpu.get_barrier_semaphore()
    for dev in peers_x + peers_y:
        pl.semaphore_signal(barrier, 1, device_id=dev, device_id_type=MESH)
    pl.semaphore_wait(barrier, len(peers_x) + len(peers_y))
    rounds = ((local_ref, got_x, peers_x, 0), (sent, got_y, peers_y, nx - 1))
    total = local_ref[...]
    for src, got, peers, base in rounds:
        copies = []
        for i, dev in enumerate(peers):
            copy = pltpu.make_async_remote_copy(
                src_ref=src, dst_ref=got.at[i], send_sem=send_sem.at[base + i],
                recv_sem=recv_sem.at[base + i], device_id=dev, device_id_type=MESH,
            )
            copy.start()
            copies.append(copy)
        for copy in copies:
            copy.wait_send()
            copy.wait_recv()
        for i in range(len(peers)):
            total = total + got[i]
        if base == 0:
            sent[...] = total
    out_ref[...] = total


def gathered_samples(local_samples):
    nx, ny = lax.axis_size("gx"), lax.axis_size("gy")
    if nx < 2 or ny < 2:
        return lax.psum(local_samples, ("gx", "gy"))
    vmem = pl.BlockSpec(memory_space=pltpu.VMEM)
    return pl.pallas_call(
        functools.partial(samples_kernel, nx, ny),
        out_shape=jax.ShapeDtypeStruct(local_samples.shape, jnp.float32),
        in_specs=[vmem],
        out_specs=vmem,
        scratch_shapes=[
            pltpu.VMEM(local_samples.shape, jnp.float32),
            pltpu.VMEM((nx - 1,) + local_samples.shape, jnp.float32),
            pltpu.VMEM((ny - 1,) + local_samples.shape, jnp.float32),
            pltpu.SemaphoreType.DMA((nx + ny - 2,)),
            pltpu.SemaphoreType.DMA((nx + ny - 2,)),
        ],
        compiler_params=pltpu.CompilerParams(collective_id=1, has_side_effects=True),
    )(local_samples)


def shards(
    sound_speed_sq,
    wind_profile,
    forward_field,
    adjoint_state,
    pair_counts,
    source_cells,
    receiver_cells,
    residuals,
):
    steps_total = forward_field.shape[0]
    width_x, width_y, depth = sound_speed_sq.shape
    slots = residuals.shape[0]
    live = (jnp.arange(slots, dtype=jnp.int32) < pair_counts[0]).astype(jnp.float32)
    gx_first = lax.axis_index("gx") * width_x
    gy_first = lax.axis_index("gy") * width_y
    x_range = jnp.arange(width_x, dtype=jnp.int32)
    y_range = jnp.arange(width_y, dtype=jnp.int32)
    z_range = jnp.arange(depth, dtype=jnp.int32)

    def tile_mask(cells):
        on_x = (cells[:, 0][None, :] - gx_first) == x_range[:, None]
        on_y = (cells[:, 1][None, :] - gy_first) == y_range[:, None]
        return (on_x[:, None, :] & on_y[None, :, :]).astype(jnp.float32)

    source_z = (source_cells[:, 2][None, :] == z_range[:, None]).astype(jnp.bfloat16)
    along_z = jnp.einsum(
        "txyz,zn->txyn", forward_field[:, 0], source_z, preferred_element_type=jnp.float32
    )
    local_samples = jnp.sum(along_z * tile_mask(source_cells)[None], axis=(1, 2))
    samples = gathered_samples(local_samples)
    amplitude = jnp.transpose(residuals) * samples * live[None, :]
    spread = amplitude[:, None, None, :] * tile_mask(receiver_cells)[None]
    receiver_z = (receiver_cells[:, 2][:, None] == z_range[None, :]).astype(jnp.float32)
    injected = jnp.einsum(
        "txyn,nz->txyz", spread, receiver_z, precision=lax.Precision.HIGHEST,
        preferred_element_type=jnp.float32,
    )
    vmem = pl.BlockSpec(memory_space=pltpu.VMEM)
    kernel = functools.partial(
        stencil_kernel, lax.axis_size("gx"), lax.axis_size("gy"), steps_total
    )
    state_new, kernels = pl.pallas_call(
        kernel,
        out_shape=(
            jax.ShapeDtypeStruct((4, width_x, width_y, depth), jnp.float32),
            jax.ShapeDtypeStruct((4, width_x, width_y, depth // 2), jnp.float32),
        ),
        in_specs=[vmem] * 5,
        out_specs=(vmem, vmem),
        scratch_shapes=[
            pltpu.VMEM((2, 4, width_x + 2, width_y, depth), jnp.float32),
            pltpu.VMEM((2, width_x + 2, width_y, depth), jnp.float32),
            pltpu.VMEM((2, 2, 4, width_x, depth), jnp.float32),
            pltpu.VMEM((2, 2, 4, width_x, depth), jnp.float32),
            pltpu.VMEM((2, width_x, depth), jnp.float32),
            pltpu.VMEM((2, 2, width_x, depth), jnp.float32),
            pltpu.VMEM((4, width_x, width_y, depth), jnp.float32),
            pltpu.VMEM((width_x, 4, width_y, depth // 2), jnp.float32),
            pltpu.VMEM((width_x, 4, width_y, depth // 2), jnp.float32),
            pltpu.VMEM((steps_total, 4, width_x + 2, width_y, depth), forward_field.dtype),
            pltpu.VMEM((2, steps_total, 2, 2 * width_x, depth), forward_field.dtype),
            pltpu.VMEM((2, steps_total, 2, 2 * width_x, depth), forward_field.dtype),
            pltpu.VMEM((3, width_x, width_y, depth), jnp.float32),
            pltpu.VMEM((2, width_x, width_y, depth), jnp.float32),
            pltpu.SemaphoreType.DMA((2, 2, 4)),
            pltpu.SemaphoreType.DMA((2, 2, 4)),
            pltpu.SemaphoreType.DMA((4,)),
            pltpu.SemaphoreType.DMA((4,)),
            pltpu.SemaphoreType.DMA((width_x,)),
            pltpu.SemaphoreType.DMA((width_x,)),
            pltpu.SemaphoreType.DMA((steps_total, 4)),
            pltpu.SemaphoreType.DMA((steps_total, 4)),
            pltpu.SemaphoreType.DMA((1,)),
        ],
        compiler_params=pltpu.CompilerParams(
            collective_id=0, has_side_effects=True, vmem_limit_bytes=48 * 1024 * 1024
        ),
    )(adjoint_state[0], sound_speed_sq, wind_profile, forward_field, injected)
    return (kernels, state_new[None])


def solution(mesh):
    in_specs = (
        P("gx", "gy", None),
        P(),
        P(None, None, "gx", "gy", None),
        P("pair", None, "gx", "gy", None),
        P("pair"),
        P("pair", None),
        P("pair", None),
        P("pair", None),
    )
    out_specs = (P(None, "gx", "gy", "pair"), P("pair", None, "gx", "gy", None))
    return jax.shard_map(shards, mesh=mesh, in_specs=in_specs, out_specs=out_specs, check_vma=False)
```

```python
import functools

import jax
import jax.numpy as jnp
from jax import lax
from jax.experimental import pallas as pl
from jax.experimental.pallas import tpu as pltpu
from jax.sharding import PartitionSpec as P

step_length = 0.25
Y_SLOT = (0, 2, 1, 3)
MESH = pl.DeviceIdType.MESH


def neighbours(shard, axis, dim):
    size, length = (lax.axis_size(axis), shard.shape[dim])
    up = [(i, i + 1) for i in range(size - 1)]
    down = [(i + 1, i) for i in range(size - 1)]
    last = lax.slice_in_dim(shard, length - 1, length, axis=dim)
    first = lax.slice_in_dim(shard, 0, 1, axis=dim)
    before = lax.ppermute(last, axis, up)
    after = lax.ppermute(first, axis, down)
    return (before, after)


def local_cells(cells, width_x, width_y):
    local_x = cells[:, 0] - lax.axis_index("gx") * width_x
    local_y = cells[:, 1] - lax.axis_index("gy") * width_y
    inside = (local_x >= 0) & (local_x < width_x) & (local_y >= 0) & (local_y < width_y)
    return (
        jnp.clip(local_x, 0, width_x - 1),
        jnp.clip(local_y, 0, width_y - 1),
        cells[:, 2],
        inside.astype(jnp.float32),
    )


def stencil_kernel(
    nx, ny, steps,
    state_in, sound, wind, forward, inj,
    state_out, kernel_out,
    pads, pbuf, ysend, yrecv, ypsend, yprecv, acc_out, ksend, krecv, fpad, fysend, fyr, advect, early,
    ss, rs, ps, pr, ks, kr, fs, fr, local_sem,
):
    _, width_x, width_y, depth = state_in.shape
    me_p = lax.axis_index("pair")
    gx = lax.axis_index("gx")
    gy = lax.axis_index("gy")
    has_lo_x = gx > 0
    has_hi_x = gx < nx - 1
    has_lo_y = gy > 0
    has_hi_y = gy < ny - 1
    dev_lo_x = (me_p, gx - 1, gy)
    dev_hi_x = (me_p, gx + 1, gy)
    dev_lo_y = (me_p, gx, gy - 1)
    dev_hi_y = (me_p, gx, gy + 1)
    dev_pair = (1 - me_p, gx, gy)
    half = depth // 2

    zero_slab = jnp.zeros((width_y, depth), jnp.float32)
    for par in range(2):
        for c in range(4):
            pads[par, c, 0] = zero_slab
            pads[par, c, width_x + 1] = zero_slab
            for side in range(2):
                yrecv[par, side, c] = jnp.zeros((width_x, depth), jnp.float32)
    for par in range(2):
        pbuf[par, 0] = zero_slab
        pbuf[par, width_x + 1] = zero_slab
    zero_forward = jnp.zeros((width_y, depth), fpad.dtype)
    for t in range(steps):
        for c in range(4):
            fpad[t, c, 0] = zero_forward
            fpad[t, c, width_x + 1] = zero_forward
            for side in range(2):
                fyr[side, t, c // 2, pl.ds((c % 2) * width_x, width_x), :] = jnp.zeros((width_x, depth), fyr.dtype)

    def forward_rows(x, carry):
        for t in range(steps):
            for c in range(4):
                f = forward[t, c, x]
                row = (c % 2) * width_x + x
                fysend[0, t, c // 2, row:row + 1, :] = f[width_y - 1:width_y, :]
                fysend[1, t, c // 2, row:row + 1, :] = f[0:1, :]
        return carry

    [forward_rows(x, 0) for x in range(width_x)]
    interior = pltpu.make_async_copy(forward, fpad.at[:, :, pl.ds(1, width_x)], local_sem.at[0])
    interior.start()
    for par in range(2):
        for side in range(2):
            yprecv[par, side] = jnp.zeros((width_x, depth), jnp.float32)

    barrier = pltpu.get_barrier_semaphore()
    pl.semaphore_signal(barrier, 1, device_id=dev_pair, device_id_type=MESH)
    for cond, dev in ((has_lo_x, dev_lo_x), (has_hi_x, dev_hi_x), (has_lo_y, dev_lo_y), (has_hi_y, dev_hi_y)):
        @pl.when(cond)
        def _():
            pl.semaphore_signal(barrier, 1, device_id=dev, device_id_type=MESH)
    peers = 1 + (
        (gx + nx - 1) // nx + (2 * nx - 2 - gx) // nx
        + (gy + ny - 1) // ny + (2 * ny - 2 - gy) // ny
    )
    pl.semaphore_wait(barrier, peers)

    iy = lax.broadcasted_iota(jnp.int32, (width_y, depth), 0)
    iz = lax.broadcasted_iota(jnp.int32, (width_y, depth), 1)
    we = wind[0:1, :]
    wn = wind[1:2, :]
    wv = wind[2:3, :]

    def dy(v, lo, hi):
        up = jnp.where(iy == width_y - 1, hi, pltpu.roll(v, width_y - 1, 0))
        down = jnp.where(iy == 0, lo, pltpu.roll(v, 1, 0))
        return (up - down) * 0.5

    def dz(v):
        up = jnp.where(iz == depth - 1, 0.0, pltpu.roll(v, depth - 1, 1))
        down = jnp.where(iz == 0, 0.0, pltpu.roll(v, 1, 1))
        return (up - down) * 0.5

    def exchange(src_lo_x, src_hi_x, dst_lo_x, dst_hi_x, src_y_hi, src_y_lo, dst_y_lo, dst_y_hi, send, recv):
        outs = (
            (has_hi_x, src_hi_x, dst_lo_x, 0, dev_hi_x),
            (has_lo_x, src_lo_x, dst_hi_x, 1, dev_lo_x),
            (has_hi_y, src_y_hi, dst_y_lo, 2, dev_hi_y),
            (has_lo_y, src_y_lo, dst_y_hi, 3, dev_lo_y),
        )
        copies = []
        for cond, src, dst, slot, dev in outs:
            copy = pltpu.make_async_remote_copy(
                src_ref=src, dst_ref=dst, send_sem=send.at[slot], recv_sem=recv.at[slot],
                device_id=dev, device_id_type=MESH,
            )
            copies.append((cond, copy))

            @pl.when(cond)
            def _():
                copy.start()
        return copies

    def settle(copies):
        incoming = (has_lo_x, has_hi_x, has_lo_y, has_hi_y)
        for (cond, copy), arrives in zip(copies, incoming):
            @pl.when(cond)
            def _():
                copy.wait_send()

            @pl.when(arrives)
            def _():
                copy.wait_recv()

    def fill_state(par, x, c, v):
        pads[par, c, x + 1] = v
        ysend[par, 0, Y_SLOT[c], x:x + 1, :] = v[width_y - 1:width_y, :]
        ysend[par, 1, Y_SLOT[c], x:x + 1, :] = v[0:1, :]

    def copy_in(x, carry):
        for c in range(4):
            fill_state(0, x, c, state_in[c, x])
        return carry

    [copy_in(x, 0) for x in range(width_x)]
    forward_copies = {}

    def send_forward(t):
        forward_copies[t] = exchange(
            forward.at[t, :, pl.ds(0, 1)], forward.at[t, :, pl.ds(width_x - 1, 1)],
            fpad.at[t, :, pl.ds(0, 1)], fpad.at[t, :, pl.ds(width_x + 1, 1)],
            fysend.at[0, t], fysend.at[1, t], fyr.at[0, t], fyr.at[1, t], fs.at[t], fr.at[t],
        )

    def increment_slab(x, carry, get, snap, first, last):
        xp = x + 1
        p_new = get(0, x)
        a_new = [get(1 + i, x) for i in range(3)]
        fe, fn, fu = [], [], []
        for c in range(4):
            f = fpad[snap, c, xp].astype(jnp.float32)
            fe.append((fpad[snap, c, xp + 1].astype(jnp.float32) - fpad[snap, c, x].astype(jnp.float32)) * 0.5)
            row = (c % 2) * width_x + x
            fn.append(dy(f, fyr[0, snap, c // 2, row:row + 1, :].astype(jnp.float32),
                         fyr[1, snap, c // 2, row:row + 1, :].astype(jnp.float32)))
            fu.append(dz(f))
        pieces = [p_new * (fe[1] + fn[2] + fu[3])]
        for along in (fe, fn, fu):
            pieces.append(p_new * along[0] + a_new[0] * along[1] + a_new[1] * along[2] + a_new[2] * along[3])
        for c in range(4):
            total = pieces[c] if first else acc_out[c, x] + pieces[c]
            if not last:
                acc_out[c, x] = total
                continue
            low, high = total[:, :half], total[:, half:]
            kernel_out[c, x] = jnp.where(me_p == 0, low, high)
            ksend[x, c] = jnp.where(me_p == 0, high, low)
        if last:
            pltpu.make_async_remote_copy(
                src_ref=ksend.at[x], dst_ref=krecv.at[x], send_sem=ks.at[x], recv_sem=kr.at[x],
                device_id=dev_pair, device_id_type=MESH,
            ).start()
        return carry

    def forward_ready(t, first):
        if first:
            interior.wait()
        settle(forward_copies[t])

    for step in range(steps):
        par = step % 2
        nxt = 1 - par
        snap = steps - 1 - step
        last = step == steps - 1
        halves = []
        for part in range(2):
            comps = pl.ds(2 * part, 2) if (part or step == 0) else pl.ds(1, 1)
            halves.append(exchange(
                pads.at[par, comps, pl.ds(1, 1)], pads.at[par, comps, pl.ds(width_x, 1)],
                pads.at[par, comps, pl.ds(0, 1)], pads.at[par, comps, pl.ds(width_x + 1, 1)],
                ysend.at[par, 0, comps], ysend.at[par, 1, comps],
                yrecv.at[par, 0, comps], yrecv.at[par, 1, comps],
                ss.at[par, part], rs.at[par, part],
            ))
        state_copies, velocity_copies = halves
        if step > 0:
            forward_ready(snap + 1, step == 1)
            [(functools.partial(
                increment_slab, get=lambda c, x, par=par: pads[par, c, x + 1],
                snap=snap + 1, first=step == 1, last=False))(x, 0) for x in range(width_x)]
        if step > 0:
            def early_slab(x, carry, par=par):
                xp = x + 1
                held = pbuf.at[1 - par]
                p = held[xp]
                dxp = (held[xp + 1] - held[x]) * 0.5
                dyp = dy(p, yprecv[1 - par, 0, x:x + 1, :], yprecv[1 - par, 1, x:x + 1, :])
                early[0, x] = we * dxp + wn * dyp + wv * dz(p)
                early[1, x] = dz(pads[par, 3, xp])
                return carry

            [early_slab(x, 0) for x in range(width_x)]
        settle(state_copies)

        def pressure_slab(x, carry, par=par, snap=snap, step=step):
            xp = x + 1
            old = pads.at[par]
            dxa = (old[1, xp + 1] - old[1, x]) * 0.5
            dya = dy(old[2, xp], yrecv[par, 0, Y_SLOT[2], x:x + 1, :], yrecv[par, 1, Y_SLOT[2], x:x + 1, :])
            if step == 0:
                p = old[0, xp]
                dxp = (old[0, xp + 1] - old[0, x]) * 0.5
                dyp = dy(p, yrecv[par, 0, Y_SLOT[0], x:x + 1, :], yrecv[par, 1, Y_SLOT[0], x:x + 1, :])
                rest = we * dxp + wn * dyp + wv * dz(p)
                dza = dz(old[3, xp])
            else:
                p = pbuf[1 - par, xp]
                rest = early[0, x]
                dza = early[1, x]
            divergence = dxa + dya + dza
            p_new = p + step_length * (sound[x] * divergence + rest) + inj[snap, x]
            pbuf[par, xp] = p_new
            ypsend[0, x:x + 1, :] = p_new[width_y - 1:width_y, :]
            ypsend[1, x:x + 1, :] = p_new[0:1, :]
            return carry

        [pressure_slab(x, 0) for x in range(width_x)]
        pressure_copies = exchange(
            pbuf.at[par, pl.ds(1, 1)], pbuf.at[par, pl.ds(width_x, 1)],
            pbuf.at[par, pl.ds(0, 1)], pbuf.at[par, pl.ds(width_x + 1, 1)],
            ypsend.at[0], ypsend.at[1], yprecv.at[par, 0], yprecv.at[par, 1],
            ps, pr,
        )
        send_forward(snap)
        def vertical_slab(x, carry, par=par):
            for i in range(3):
                advect[i, x] = wv * dz(pads[par, 1 + i, x + 1])
            return carry

        [vertical_slab(x, 0) for x in range(width_x)]
        settle(velocity_copies)

        def advection_slab(x, carry, par=par):
            xp = x + 1
            old = pads.at[par]
            for i in range(3):
                a = old[1 + i, xp]
                dxa = (old[1 + i, xp + 1] - old[1 + i, x]) * 0.5
                dya = dy(a, yrecv[par, 0, Y_SLOT[1 + i], x:x + 1, :], yrecv[par, 1, Y_SLOT[1 + i], x:x + 1, :])
                advect[i, x] = we * dxa + wn * dya + advect[i, x]
            return carry

        [advection_slab(x, 0) for x in range(width_x)]
        settle(pressure_copies)

        def velocity_slab(x, carry, par=par, nxt=nxt, last=last):
            xp = x + 1
            old = pads.at[par]
            p_new = pbuf[par, xp]
            grad = (
                (pbuf[par, xp + 1] - pbuf[par, x]) * 0.5,
                dy(p_new, yprecv[par, 0, x:x + 1, :], yprecv[par, 1, x:x + 1, :]),
                dz(p_new),
            )
            new_state = [p_new]
            for i in range(3):
                new_state.append(old[1 + i, xp] + step_length * (grad[i] + advect[i, x]))
            for c in range(4):
                if last:
                    state_out[c, x] = new_state[c]
                else:
                    fill_state(nxt, x, c, new_state[c])
            return carry

        [velocity_slab(x, 0) for x in range(width_x)]

    forward_ready(0, steps == 1)
    [(functools.partial(
        increment_slab, get=lambda c, x: state_out[c, x], snap=0, first=steps == 1, last=True))(x, 0) for x in range(width_x)]

    for x in range(width_x):
        copy = pltpu.make_async_remote_copy(
            src_ref=ksend.at[x], dst_ref=krecv.at[x], send_sem=ks.at[x], recv_sem=kr.at[x],
            device_id=dev_pair, device_id_type=MESH,
        )
        copy.wait_recv()
        for c in range(4):
            kernel_out[c, x] = kernel_out[c, x] + krecv[x, c]
        copy.wait_send()


def samples_kernel(nx, ny, local_ref, out_ref, sent, got_x, got_y, send_sem, recv_sem):
    me_p = lax.axis_index("pair")
    gx = lax.axis_index("gx")
    gy = lax.axis_index("gy")
    peers_x = [(me_p, (gx + d) % nx, gy) for d in range(1, nx)]
    peers_y = [(me_p, gx, (gy + d) % ny) for d in range(1, ny)]
    barrier = pltpu.get_barrier_semaphore()
    for dev in peers_x + peers_y:
        pl.semaphore_signal(barrier, 1, device_id=dev, device_id_type=MESH)
    pl.semaphore_wait(barrier, len(peers_x) + len(peers_y))
    rounds = ((local_ref, got_x, peers_x, 0), (sent, got_y, peers_y, nx - 1))
    total = local_ref[...]
    for src, got, peers, base in rounds:
        copies = []
        for i, dev in enumerate(peers):
            copy = pltpu.make_async_remote_copy(
                src_ref=src, dst_ref=got.at[i], send_sem=send_sem.at[base + i],
                recv_sem=recv_sem.at[base + i], device_id=dev, device_id_type=MESH,
            )
            copy.start()
            copies.append(copy)
        for copy in copies:
            copy.wait_send()
            copy.wait_recv()
        for i in range(len(peers)):
            total = total + got[i]
        if base == 0:
            sent[...] = total
    out_ref[...] = total


def gathered_samples(local_samples):
    nx, ny = lax.axis_size("gx"), lax.axis_size("gy")
    if nx < 2 or ny < 2:
        return lax.psum(local_samples, ("gx", "gy"))
    vmem = pl.BlockSpec(memory_space=pltpu.VMEM)
    return pl.pallas_call(
        functools.partial(samples_kernel, nx, ny),
        out_shape=jax.ShapeDtypeStruct(local_samples.shape, jnp.float32),
        in_specs=[vmem],
        out_specs=vmem,
        scratch_shapes=[
            pltpu.VMEM(local_samples.shape, jnp.float32),
            pltpu.VMEM((nx - 1,) + local_samples.shape, jnp.float32),
            pltpu.VMEM((ny - 1,) + local_samples.shape, jnp.float32),
            pltpu.SemaphoreType.DMA((nx + ny - 2,)),
            pltpu.SemaphoreType.DMA((nx + ny - 2,)),
        ],
        compiler_params=pltpu.CompilerParams(collective_id=1, has_side_effects=True),
    )(local_samples)


def shards(
    sound_speed_sq,
    wind_profile,
    forward_field,
    adjoint_state,
    pair_counts,
    source_cells,
    receiver_cells,
    residuals,
):
    steps_total = forward_field.shape[0]
    width_x, width_y, depth = sound_speed_sq.shape
    slots = residuals.shape[0]
    live = (jnp.arange(slots, dtype=jnp.int32) < pair_counts[0]).astype(jnp.float32)
    gx_first = lax.axis_index("gx") * width_x
    gy_first = lax.axis_index("gy") * width_y
    x_range = jnp.arange(width_x, dtype=jnp.int32)
    y_range = jnp.arange(width_y, dtype=jnp.int32)
    z_range = jnp.arange(depth, dtype=jnp.int32)

    def tile_mask(cells):
        on_x = (cells[:, 0][None, :] - gx_first) == x_range[:, None]
        on_y = (cells[:, 1][None, :] - gy_first) == y_range[:, None]
        return (on_x[:, None, :] & on_y[None, :, :]).astype(jnp.float32)

    source_z = (source_cells[:, 2][None, :] == z_range[:, None]).astype(jnp.bfloat16)
    along_z = jnp.einsum(
        "txyz,zn->txyn", forward_field[:, 0], source_z, preferred_element_type=jnp.float32
    )
    local_samples = jnp.sum(along_z * tile_mask(source_cells)[None], axis=(1, 2))
    samples = gathered_samples(local_samples)
    amplitude = jnp.transpose(residuals) * samples * live[None, :]
    spread = amplitude[:, None, None, :] * tile_mask(receiver_cells)[None]
    receiver_z = (receiver_cells[:, 2][:, None] == z_range[None, :]).astype(jnp.float32)
    injected = jnp.einsum(
        "txyn,nz->txyz", spread, receiver_z, precision=lax.Precision.HIGHEST,
        preferred_element_type=jnp.float32,
    )
    vmem = pl.BlockSpec(memory_space=pltpu.VMEM)
    kernel = functools.partial(
        stencil_kernel, lax.axis_size("gx"), lax.axis_size("gy"), steps_total
    )
    state_new, kernels = pl.pallas_call(
        kernel,
        out_shape=(
            jax.ShapeDtypeStruct((4, width_x, width_y, depth), jnp.float32),
            jax.ShapeDtypeStruct((4, width_x, width_y, depth // 2), jnp.float32),
        ),
        in_specs=[vmem] * 5,
        out_specs=(vmem, vmem),
        scratch_shapes=[
            pltpu.VMEM((2, 4, width_x + 2, width_y, depth), jnp.float32),
            pltpu.VMEM((2, width_x + 2, width_y, depth), jnp.float32),
            pltpu.VMEM((2, 2, 4, width_x, depth), jnp.float32),
            pltpu.VMEM((2, 2, 4, width_x, depth), jnp.float32),
            pltpu.VMEM((2, width_x, depth), jnp.float32),
            pltpu.VMEM((2, 2, width_x, depth), jnp.float32),
            pltpu.VMEM((4, width_x, width_y, depth), jnp.float32),
            pltpu.VMEM((width_x, 4, width_y, depth // 2), jnp.float32),
            pltpu.VMEM((width_x, 4, width_y, depth // 2), jnp.float32),
            pltpu.VMEM((steps_total, 4, width_x + 2, width_y, depth), forward_field.dtype),
            pltpu.VMEM((2, steps_total, 2, 2 * width_x, depth), forward_field.dtype),
            pltpu.VMEM((2, steps_total, 2, 2 * width_x, depth), forward_field.dtype),
            pltpu.VMEM((3, width_x, width_y, depth), jnp.float32),
            pltpu.VMEM((2, width_x, width_y, depth), jnp.float32),
            pltpu.SemaphoreType.DMA((2, 2, 4)),
            pltpu.SemaphoreType.DMA((2, 2, 4)),
            pltpu.SemaphoreType.DMA((4,)),
            pltpu.SemaphoreType.DMA((4,)),
            pltpu.SemaphoreType.DMA((width_x,)),
            pltpu.SemaphoreType.DMA((width_x,)),
            pltpu.SemaphoreType.DMA((steps_total, 4)),
            pltpu.SemaphoreType.DMA((steps_total, 4)),
            pltpu.SemaphoreType.DMA((1,)),
        ],
        compiler_params=pltpu.CompilerParams(
            collective_id=0, has_side_effects=True, vmem_limit_bytes=48 * 1024 * 1024
        ),
    )(adjoint_state[0], sound_speed_sq, wind_profile, forward_field, injected)
    return (kernels, state_new[None])


def solution(mesh):
    in_specs = (
        P("gx", "gy", None),
        P(),
        P(None, None, "gx", "gy", None),
        P("pair", None, "gx", "gy", None),
        P("pair"),
        P("pair", None),
        P("pair", None),
        P("pair", None),
    )
    out_specs = (P(None, "gx", "gy", "pair"), P("pair", None, "gx", "gy", None))
    return jax.shard_map(shards, mesh=mesh, in_specs=in_specs, out_specs=out_specs, check_vma=False)
```
